128 devices in a mesh: lift: 8 (over z, x_lo), tile: 16 (over x_hi, y, core).
Axes of the slice: x: 4 (x_hi: 2, x_lo: 2; x = x_hi * 2 + x_lo), y: 4, z: 4, core: 2. Of those that a mesh axis runs over, the one named last changes fastest.
Arguments:
- oxygen: float32 [8, 16, 16, 256, 256], P('lift', None, 'tile'), may hold values from 0 to 1
- velocity: float32 [8, 16, 16, 256, 256], P('lift', None, 'tile'), may hold values from 0.2 to 1
- spacing: float32 [8], P('lift'), may hold values from 1 to 2
- inlets: int32 [8, 16, 256, 256], P('lift', 'tile'), may hold values 0 or 1
- proj_x: float32 [8, 16, 4, 256, 256], P('lift', 'tile'), may hold values from -1 to 1
- proj_y: float32 [8, 16, 4, 256, 256], P('lift', 'tile'), may hold values from -1 to 1
- sources: int32 [8, 16, 4], P('lift', 'tile'), may hold values from 0 to 15, as said below
Outputs:
- oxygen_next: float32 [8, 16, 16, 256, 256], P('lift', None, 'tile')
The draws below stay inside these ranges and needn't reach their ends.
Inputs may be any that keep to these rules, and one draw needn't show every extreme that they name: sources[l, t, 0] is the tile (t + 8) % 16; the other entries may be any tile of the lift below; entries of lift 0 are not used.
All inputs are finite; a program needn't handle non-finite values. No bound on the sum of `inlets` on one device may be relied on, other than what follows from the above.
Results may differ from the reference program's by a relative error of at most 0.0001.
Values sent between devices are 32-bit elements; how exact they have to be, the bound alone decides.
No kernel may reach another device: no remote copies, remote signals or barrier semaphores. Data moves between devices by JAX's collectives and lax.ppermute only.
A program may use at most 128 MiB of HBM per device.

```python
import math
import jax
import jax.numpy as jnp
from jax import lax

NZ = 16
CX = 256
CY = 256
TCOL = 4
K = 4
STEPS = 2
LIFTS = 8
TILES = 16


def projection_block(key, width):
    key_diag, key_off = jax.random.split(key)
    shape = (LIFTS, TILES, K, width, width)
    diagonal = jax.random.uniform(key_diag, shape, jnp.float32, 0.5, 1.0)
    off_part = jax.random.uniform(key_off, shape, jnp.float32, -1.0, 1.0) * (0.6 / math.sqrt(width))
    row_index = lax.broadcasted_iota(jnp.int32, shape, 3)
    col_index = lax.broadcasted_iota(jnp.int32, shape, 4)
    identity = (row_index == col_index).astype(jnp.float32)
    return (identity * diagonal + (1.0 - identity) * off_part) * K ** (-0.5)


def draw_proj_x(key, part):
    return projection_block(jax.random.fold_in(key, 11), CX)


def draw_proj_y(key, part):
    return projection_block(jax.random.fold_in(key, 23), CY)


def draw_sources(key, part):
    shape = (LIFTS, TILES, K)
    drawn = jax.random.randint(jax.random.fold_in(key, 37), shape, 0, TILES)
    tile_ids = lax.broadcasted_iota(jnp.int32, shape, 1)
    slot_ids = lax.broadcasted_iota(jnp.int32, shape, 2)
    partner = (tile_ids + TILES // 2) % TILES
    return jnp.where(slot_ids == 0, partner, drawn).astype(jnp.int32)


def with_ends(array, stream_key, smallest, largest):
    longest = array.shape.index(max(array.shape))
    spots = []
    for shift in (0, 1):
        where = [jax.random.randint(jax.random.fold_in(stream_key, axis), (), 0, length) for axis, length in enumerate(array.shape)]
        where[longest] = (where[longest] + shift) % array.shape[longest]
        spots.append(tuple(where))
    return array.at[spots[0]].set(smallest).at[spots[1]].set(largest)


def block_scale(own_key, shape, cuts, low, high):
    def one(axis_at, blocks):
        steps = jax.random.uniform(jax.random.fold_in(jax.random.fold_in(own_key, 6), axis_at), (blocks,), jnp.float32, low / len(cuts), high / len(cuts))
        return jnp.repeat(jnp.exp(steps), shape[axis_at] // blocks).reshape((-1,) + (1,) * (len(shape) - axis_at - 1))

    level = one(*cuts[0])
    for cut in cuts[1:]:
        level = level * one(*cut)
    return level


def setup_inputs(seed: int = 0) -> dict:
    splits = jax.random.split(jax.random.key(seed), 8)
    return {
        "oxygen": jnp.clip(1.0 * jax.random.uniform(splits[0], (LIFTS, NZ, TILES, CX, CY), jnp.float32) ** block_scale(splits[0], (LIFTS, NZ, TILES, CX, CY), ((0, 8), (2, 16)), -0.2, 0.2), 0.0, 1.0),
        "velocity": jnp.clip(0.2 + 0.8 * jax.random.uniform(splits[1], (LIFTS, NZ, TILES, CX, CY), jnp.float32) ** block_scale(splits[1], (LIFTS, NZ, TILES, CX, CY), ((0, 8), (2, 16)), -0.2, 0.2), 0.2, 1.0),
        "spacing": jnp.clip(jnp.exp(math.log(2.0) - 0.6931472 * jax.random.uniform(splits[2], (LIFTS,), jnp.float32) ** block_scale(splits[2], (LIFTS,), ((0, 8),), -0.2, 0.2)), 1.0, 2.0),
        "inlets": with_ends((jax.random.randint(splits[3], (LIFTS, TILES, CX, CY), 0, 8) < 1).astype(jnp.int32), jax.random.fold_in(splits[3], 1), 0, 1),
        "proj_x": draw_proj_x(jax.random.fold_in(splits[7], 71), 0),
        "proj_y": draw_proj_y(jax.random.fold_in(splits[7], 71), 0),
        "sources": draw_sources(jax.random.fold_in(splits[7], 71), 0),
    }


TIME_STEP = 0.1
INJECT_RATE = 2.0
AMBIENT = 1.0
HIGHEST = lax.Precision.HIGHEST


def horizontal(field):
    lifts, depth, tiles, width_x, width_y = field.shape
    tile_rows = tiles // TCOL
    grid = field.reshape(lifts, depth, tile_rows, TCOL, width_x, width_y)
    grid = grid.transpose(0, 1, 2, 4, 3, 5).reshape(lifts, depth, tile_rows * width_x, TCOL * width_y)
    padded = jnp.pad(grid, ((0, 0), (0, 0), (1, 1), (1, 1)))
    beside_all = padded[:, :, 2:, 1:-1] + padded[:, :, :-2, 1:-1] + padded[:, :, 1:-1, 2:] + padded[:, :, 1:-1, :-2]
    lapl = beside_all - 4.0 * grid
    lapl = lapl.reshape(lifts, depth, tile_rows, width_x, TCOL, width_y).transpose(0, 1, 2, 4, 3, 5)
    return lapl.reshape(field.shape)


def pick_planes(planes, index):
    return planes[index]


def reference(oxygen, velocity, spacing, inlets, proj_x, proj_y, sources):
    field = oxygen
    inverse = (1.0 / (spacing * spacing))[:, None, None, None, None]
    inject = INJECT_RATE * inlets.astype(jnp.float32)
    onehot = (sources[1:, :, :, None] == jnp.arange(TILES, dtype=jnp.int32)).astype(jnp.float32)
    for step_index in range(STEPS):
        top_plane = field[:, NZ - 1]
        bottom_plane = field[:, 0]
        picked = jax.vmap(pick_planes)(top_plane[:-1], sources[1:])
        from_below = jnp.einsum('ltkab,ltkbc,ltkdc->ltad', proj_x[1:], picked, proj_y[1:], precision=HIGHEST)
        ghost_below = jnp.concatenate([jnp.zeros((1, TILES, CX, CY), jnp.float32), from_below], axis=0)
        pieces = jnp.einsum('ltkba,ltbc,ltkcd->ltkad', proj_x[1:], bottom_plane[1:], proj_y[1:], precision=HIGHEST)
        from_above = jnp.einsum('ltks,ltkad->lsad', onehot, pieces, precision=HIGHEST)
        ghost_above = jnp.concatenate([from_above, jnp.full((1, TILES, CX, CY), AMBIENT, jnp.float32)], axis=0)
        stacked = jnp.concatenate([ghost_below[:, None], field, ghost_above[:, None]], axis=1)
        under = stacked[:, :-2]
        over = stacked[:, 2:]
        change = inverse * horizontal(field) + over + under - 2.0 * field - velocity * (field - under)
        change = change.at[:, 0].add(inject * (1.0 - field[:, 0]))
        field = field + TIME_STEP * change
    return field
```

```python
import functools

import jax
import jax.numpy as jnp
from jax import lax
from jax.experimental import pallas as pl
from jax.experimental.pallas import tpu as pltpu
from jax.sharding import PartitionSpec as P

TCOL = 4
STEPS = 2
LIFTS = 8
TILES = 16
NZ = 16
W = 256
TIME_STEP = 0.1
INJECT_RATE = 2.0
AMBIENT = 1.0
F32 = jnp.float32
BF16 = jnp.bfloat16
MIB = 1 << 20


def tile_of(x_half, y, core):
    return x_half * 8 + (y % 4) * 2 + core


def coords(tile):
    return tile // 8, (tile // 2) % 4, tile % 2


def along_y(steps):
    return [(t, tile_of(coords(t)[0], coords(t)[1] + steps, coords(t)[2])) for t in range(TILES)]


OTHER_CORE = [(t, t ^ 1) for t in range(TILES)]


def to_lift(steps, flip):
    pairs = []
    for lift in range(LIFTS):
        if 0 <= lift + steps < LIFTS:
            for t in range(TILES):
                pairs.append((lift * TILES + t, (lift + steps) * TILES + (t ^ (8 if flip else 0))))
    return pairs


def split(value):
    high = value.astype(BF16)
    return high, (value - high.astype(F32)).astype(BF16)


def product(a, b, dims):
    def one(u, v):
        return lax.dot_general(u, v, (dims, ((), ())), preferred_element_type=F32)

    return one(a[0], b[0]) + (one(a[0], b[1]) + one(a[1], b[0]))


def relative(table, k):
    source, tile = table[k], table[4]
    x_step = ((source >> 3) ^ (tile >> 3)) & 1
    y_step = ((source >> 1) - (tile >> 1)) & 3
    core_step = (source ^ tile) & 1
    return core_step, y_step, x_step


def pieces_kernel(table, px, py, bottom, first, rest, keep):
    first[...] = jnp.zeros_like(first)
    rest[...] = jnp.zeros_like(rest)
    keep[...] = jnp.zeros_like(keep)
    plane = split(bottom[...])
    for k in range(4):
        left = product(split(px[k]), plane, ((0,), (0,)))
        piece = product(split(left), split(py[k]), ((1,), (0,)))
        core_step, y_step, x_step = relative(table, k)

        @pl.when(core_step == 0)
        def _():
            slot = y_step * 2 + x_step
            keep[slot] = keep[slot] + piece

        @pl.when((core_step == 1) & (y_step == 2))
        def _():
            first[x_step] = first[x_step] + piece

        @pl.when((core_step == 1) & (y_step != 2))
        def _():
            slot = jnp.minimum(y_step, 2) * 2 + x_step
            rest[slot] = rest[slot] + piece


def full(shape):
    return pl.BlockSpec(shape, lambda *_: (0,) * len(shape))


SMEM_SPEC = pl.BlockSpec(memory_space=pltpu.SMEM)


def plane_shape(count=None):
    return jax.ShapeDtypeStruct((W, W) if count is None else (count, W, W), F32)


def pieces_of(table, px, py, bottom):
    return pl.pallas_call(
        pieces_kernel,
        out_shape=(plane_shape(2), plane_shape(6), plane_shape(8)),
        in_specs=[SMEM_SPEC] + [pl.BlockSpec(memory_space=pltpu.VMEM)] * 3,
        out_specs=[pl.BlockSpec(memory_space=pltpu.VMEM)] * 3,
        compiler_params=pltpu.CompilerParams(vmem_limit_bytes=24 * MIB),
        cost_estimate=pl.CostEstimate(flops=8 * 6 * W**3, bytes_accessed=7 * MIB, transcendentals=0),
        name="pieces",
    )(table, px, py, bottom)


def below_kernel(table, px, py, speed, field, *refs):
    tops, (out, bottom, picked, sems) = refs[:16], refs[16:]
    for k in range(4):
        core_step, y_step, x_step = relative(table, k)
        slot = core_step * 8 + y_step * 2 + x_step
        for j in range(16):

            @pl.when(slot == j)
            def _():
                pltpu.make_async_copy(tops[j], picked.at[k], sems.at[k]).start()

    total = jnp.zeros((W, W), F32)
    for k in range(4):
        pltpu.make_async_copy(tops[0], picked.at[k], sems.at[k]).wait()
        left = product(split(px[k]), split(picked[k]), ((1,), (0,)))
        total = total + product(split(left), split(py[k]), ((1,), (1,)))
    new = field[0] + TIME_STEP * (total + speed[0] * total)
    out[0] = new
    bottom[...] = new


def below_update(table, px, py, speed, field, tops):
    plane0 = pl.BlockSpec((1, W, W), lambda i: (0, 0, 0))
    return pl.pallas_call(
        below_kernel,
        grid=(1,),
        out_shape=(plane_shape(NZ), plane_shape()),
        in_specs=[SMEM_SPEC, full((4, W, W)), full((4, W, W)), plane0, plane0]
        + [pl.BlockSpec(memory_space=pl.ANY)] * 16,
        out_specs=[plane0, full((W, W))],
        scratch_shapes=[pltpu.VMEM((4, W, W), F32), pltpu.SemaphoreType.DMA((4,))],
        input_output_aliases={4: 0},
        compiler_params=pltpu.CompilerParams(vmem_limit_bytes=24 * MIB),
        cost_estimate=pl.CostEstimate(flops=8 * 6 * W**3, bytes_accessed=5 * MIB, transcendentals=0),
        name="below",
    )(table, px, py, speed, field, *tops)


def above_kernel(table, straight, flipped, field, out, top):
    ghost = straight[...] + flipped[...]
    ghost = jnp.where(table[5] == 1, AMBIENT, ghost)
    new = field[0] + TIME_STEP * ghost
    out[0] = new
    top[...] = new


def above_update(table, straight, flipped, field):
    last = pl.BlockSpec((1, W, W), lambda i: (NZ - 1, 0, 0))
    return pl.pallas_call(
        above_kernel,
        grid=(1,),
        out_shape=(plane_shape(NZ), plane_shape()),
        in_specs=[SMEM_SPEC, full((W, W)), full((W, W)), last],
        out_specs=[last, full((W, W))],
        input_output_aliases={3: 0},
        compiler_params=pltpu.CompilerParams(vmem_limit_bytes=8 * MIB),
        cost_estimate=pl.CostEstimate(flops=3 * W * W, bytes_accessed=MIB, transcendentals=0),
        name="above",
    )(table, straight, flipped, field)


def rims_kernel(field, row_low, row_high, col_low, col_high, low, high):
    z = pl.program_id(0)
    plane = field[0]
    row_low[pl.ds(z, 1), :] = plane[0:1, :]
    row_high[pl.ds(z, 1), :] = plane[W - 1 : W, :]
    lane = lax.broadcasted_iota(jnp.int32, (W, 128), 1)

    @pl.when(z == 0)
    def _():
        low[...] = jnp.zeros_like(low)
        high[...] = jnp.zeros_like(high)

    low[...] = jnp.where(lane == z, plane[:, 0:1], low[...])
    high[...] = jnp.where(lane == z, plane[:, W - 1 : W], high[...])

    @pl.when(z == NZ - 1)
    def _():
        col_low[...] = low[...].T[:NZ]
        col_high[...] = high[...].T[:NZ]


def rims_of(field):
    rim = jax.ShapeDtypeStruct((NZ, W), F32)
    return pl.pallas_call(
        rims_kernel,
        grid=(NZ,),
        out_shape=(rim,) * 4,
        in_specs=[pl.BlockSpec((1, W, W), lambda z: (z, 0, 0))],
        out_specs=[full((NZ, W))] * 4,
        scratch_shapes=[pltpu.VMEM((W, 128), F32)] * 2,
        compiler_params=pltpu.CompilerParams(vmem_limit_bytes=8 * MIB),
        cost_estimate=pl.CostEstimate(flops=NZ * W * W, bytes_accessed=4 * MIB, transcendentals=0),
        name="rims",
    )(field)


def stencil_kernel(inverse, here, below, above, speed, inlets, x_low, x_high, y_low, y_high, out, low, high):
    z = pl.program_id(0)

    @pl.when(z == 0)
    def _():
        pad = jnp.zeros((128 - NZ, W), F32)
        low[...] = jnp.concatenate([y_low[...], pad], axis=0).T
        high[...] = jnp.concatenate([y_high[...], pad], axis=0).T

    field = here[0]
    pick = lax.broadcasted_iota(jnp.int32, (W, 128), 1) == z
    col_low = jnp.sum(jnp.where(pick, low[...], 0.0), axis=1, keepdims=True)
    col_high = jnp.sum(jnp.where(pick, high[...], 0.0), axis=1, keepdims=True)
    row = lax.broadcasted_iota(jnp.int32, (W, W), 0)
    lane = lax.broadcasted_iota(jnp.int32, (W, W), 1)
    beside = jnp.where(row == 0, x_low[pl.ds(z, 1), :], pltpu.roll(field, 1, 0))
    beside = beside + jnp.where(row == W - 1, x_high[pl.ds(z, 1), :], pltpu.roll(field, W - 1, 0))
    beside = beside + jnp.where(lane == 0, col_low, pltpu.roll(field, 1, 1))
    beside = beside + jnp.where(lane == W - 1, col_high, pltpu.roll(field, W - 1, 1))
    lapl = (beside - 4.0 * field) * inverse[0]
    under = jnp.where(z == 0, 0.0, below[0])
    over = jnp.where(z == NZ - 1, 0.0, above[0])
    change = lapl + over + under - 2.0 * field - speed[0] * (field - under)
    out[0] = field + TIME_STEP * change

    @pl.when(z == 0)
    def _():
        inject = INJECT_RATE * inlets[...].astype(F32)
        out[0] = out[0] + TIME_STEP * (inject * (1.0 - here[0]))


def stencil(inverse, field, speed, inlets, halos):
    rim = full((NZ, W))
    return pl.pallas_call(
        stencil_kernel,
        grid=(NZ,),
        out_shape=plane_shape(NZ),
        in_specs=[
            SMEM_SPEC,
            pl.BlockSpec((1, W, W), lambda z: (z, 0, 0)),
            pl.BlockSpec((1, W, W), lambda z: (jnp.maximum(z - 1, 0), 0, 0)),
            pl.BlockSpec((1, W, W), lambda z: (jnp.minimum(z + 1, NZ - 1), 0, 0)),
            pl.BlockSpec((1, W, W), lambda z: (z, 0, 0)),
            full((W, W)),
            rim,
            rim,
            rim,
            rim,
        ],
        out_specs=pl.BlockSpec((1, W, W), lambda z: (z, 0, 0)),
        scratch_shapes=[pltpu.VMEM((W, 128), F32)] * 2,
        compiler_params=pltpu.CompilerParams(vmem_limit_bytes=16 * MIB),
        cost_estimate=pl.CostEstimate(flops=16 * NZ * W * W, bytes_accessed=12 * MIB, transcendentals=0),
        name="stencil",
    )(inverse, field, field, field, speed, inlets, *halos)


def exchange_rims(field):
    row_low, row_high, col_low, col_high = rims_of(field)
    x_low = lax.ppermute(row_high, "tile", [(t, t + TCOL) for t in range(TILES - TCOL)])
    x_high = lax.ppermute(row_low, "tile", [(t + TCOL, t) for t in range(TILES - TCOL)])
    inside = [t for t in range(TILES) if t % TCOL < TCOL - 1]
    y_low = lax.ppermute(col_high, "tile", [(t, t + 1) for t in inside])
    y_high = lax.ppermute(col_low, "tile", [(t + 1, t) for t in inside])
    return x_low, x_high, y_low, y_high


def send_y(value, steps):
    return lax.ppermute(value, "tile", along_y(steps))


def send_lift(value, steps, flip):
    return lax.ppermute(value, ("lift", "tile"), to_lift(steps, flip))


def other_core(value):
    return lax.ppermute(value, "tile", OTHER_CORE)


def gather_tops(top):
    mine = send_lift(top, 1, False)
    flip = send_lift(top, 1, True)
    left_mine = send_y(mine, 1)
    right_flip = send_y(flip, -1)
    left_flip = send_y(flip, 1)
    right_mine = send_y(mine, -1)
    far_mine = send_y(left_mine, 1)
    far_flip = send_y(right_flip, -1)
    near = [mine, flip, right_mine, right_flip, far_mine, far_flip, left_mine, left_flip]
    return near + [other_core(value) for value in near]


def reduce_pieces(first, rest, keep):
    first = other_core(first)
    rest = other_core(rest)
    far_mine = send_y(keep[4] + first[0], 1)
    far_flip = send_y(keep[5] + first[1], -1)
    right_flip = send_y(keep[3] + rest[3], 1)
    left_mine = send_y(keep[6] + rest[4], -1)
    right_mine = send_y(keep[2] + rest[2] + far_mine, 1)
    left_flip = send_y(keep[7] + rest[5] + far_flip, -1)
    mine = keep[0] + rest[0] + left_mine + right_mine
    flip = keep[1] + rest[1] + left_flip + right_flip
    return send_lift(mine, -1, False), send_lift(flip, -1, True)


def on_device(oxygen, velocity, spacing, inlets, proj_x, proj_y, sources):
    field = oxygen.reshape(NZ, W, W)
    speed = velocity.reshape(NZ, W, W)
    inlets = inlets.reshape(W, W)
    px = proj_x.reshape(4, W, W)
    py = proj_y.reshape(4, W, W)
    inverse = 1.0 / (spacing * spacing)
    tile = lax.axis_index("tile").astype(jnp.int32)
    is_top = (lax.axis_index("lift") == LIFTS - 1).astype(jnp.int32)
    table = jnp.concatenate([sources.reshape(4) & (TILES - 1), tile[None], is_top[None]])
    top, bottom = field[NZ - 1], field[0]
    for _ in range(STEPS):
        tops = gather_tops(top)
        parts = reduce_pieces(*pieces_of(table, px, py, bottom))
        halos = exchange_rims(field)
        field = stencil(inverse, field, speed, inlets, halos)
        field, bottom = below_update(table, px, py, speed, field, tops)
        field, top = above_update(table, *parts, field)
    return field.reshape(1, NZ, 1, W, W)


def solution(mesh):
    return jax.shard_map(
        on_device,
        mesh=mesh,
        in_specs=(
            P("lift", None, "tile", None, None),
            P("lift", None, "tile", None, None),
            P("lift"),
            P("lift", "tile", None, None),
            P("lift", "tile", None, None, None),
            P("lift", "tile", None, None, None),
            P("lift", "tile", None),
        ),
        out_specs=P("lift", None, "tile", None, None),
        check_vma=False,
    )
```

```python
import functools

import jax
import jax.numpy as jnp
from jax import lax
from jax.experimental import pallas as pl
from jax.experimental.pallas import tpu as pltpu
from jax.sharding import PartitionSpec as P

TCOL = 4
STEPS = 2
LIFTS = 8
TILES = 16
NZ = 16
W = 256
TIME_STEP = 0.1
INJECT_RATE = 2.0
AMBIENT = 1.0
F32 = jnp.float32
BF16 = jnp.bfloat16
MIB = 1 << 20


def tile_of(x_half, y, core):
    return x_half * 8 + (y % 4) * 2 + core


def coords(tile):
    return tile // 8, (tile // 2) % 4, tile % 2


def along_y(steps):
    return [(t, tile_of(coords(t)[0], coords(t)[1] + steps, coords(t)[2])) for t in range(TILES)]


OTHER_CORE = [(t, t ^ 1) for t in range(TILES)]


def to_lift(steps, flip):
    pairs = []
    for lift in range(LIFTS):
        if 0 <= lift + steps < LIFTS:
            for t in range(TILES):
                pairs.append((lift * TILES + t, (lift + steps) * TILES + (t ^ (8 if flip else 0))))
    return pairs


def split(value):
    high = value.astype(BF16)
    return high, (value - high.astype(F32)).astype(BF16)


def product(a, b, dims):
    def one(u, v):
        return lax.dot_general(u, v, (dims, ((), ())), preferred_element_type=F32)

    return one(a[0], b[0]) + (one(a[0], b[1]) + one(a[1], b[0]))


def relative(table, k):
    source, tile = table[k], table[4]
    x_step = ((source >> 3) ^ (tile >> 3)) & 1
    y_step = ((source >> 1) - (tile >> 1)) & 3
    core_step = (source ^ tile) & 1
    return core_step, y_step, x_step


def pieces_kernel(table, px, py, bottom, give, keep):
    give[...] = jnp.zeros_like(give)
    keep[...] = jnp.zeros_like(keep)
    plane = split(bottom[...])
    for k in range(4):
        left = product(split(px[k]), plane, ((0,), (0,)))
        piece = product(split(left), split(py[k]), ((1,), (0,)))
        core_step, y_step, x_step = relative(table, k)
        slot = y_step * 2 + x_step

        @pl.when(core_step == 0)
        def _():
            keep[slot] = keep[slot] + piece

        @pl.when(core_step == 1)
        def _():
            give[slot] = give[slot] + piece


def full(shape):
    return pl.BlockSpec(shape, lambda *_: (0,) * len(shape))


SMEM_SPEC = pl.BlockSpec(memory_space=pltpu.SMEM)


def plane_shape(count=None):
    return jax.ShapeDtypeStruct((W, W) if count is None else (count, W, W), F32)


def pieces_of(table, px, py, bottom):
    return pl.pallas_call(
        pieces_kernel,
        out_shape=(plane_shape(8), plane_shape(8)),
        in_specs=[SMEM_SPEC] + [pl.BlockSpec(memory_space=pltpu.VMEM)] * 3,
        out_specs=[pl.BlockSpec(memory_space=pltpu.VMEM)] * 2,
        compiler_params=pltpu.CompilerParams(vmem_limit_bytes=24 * MIB),
        cost_estimate=pl.CostEstimate(flops=8 * 6 * W**3, bytes_accessed=7 * MIB, transcendentals=0),
        name="pieces",
    )(table, px, py, bottom)


def below_kernel(table, px, py, speed, field, tops, out, bottom, picked, sems):
    def fetch(k):
        source, tile = table[k], table[4]
        x_step = ((source >> 3) ^ (tile >> 3)) & 1
        return pltpu.make_async_copy(tops.at[(source & 7) * 2 + x_step], picked.at[k], sems.at[k])

    for k in range(4):
        fetch(k).start()
    total = jnp.zeros((W, W), F32)
    for k in range(4):
        fetch(k).wait()
        left = product(split(px[k]), split(picked[k]), ((1,), (0,)))
        total = total + product(split(left), split(py[k]), ((1,), (1,)))
    new = field[0] + TIME_STEP * (total + speed[...] * total)
    out[0] = new
    bottom[...] = new


def below_update(table, px, py, speed, field, tops):
    plane0 = pl.BlockSpec((1, W, W), lambda i: (0, 0, 0))
    return pl.pallas_call(
        below_kernel,
        grid=(1,),
        out_shape=(plane_shape(NZ), plane_shape()),
        in_specs=[SMEM_SPEC, full((4, W, W)), full((4, W, W)), full((W, W)), plane0]
        + [pl.BlockSpec(memory_space=pltpu.HBM)],
        out_specs=[plane0, full((W, W))],
        scratch_shapes=[pltpu.VMEM((4, W, W), F32), pltpu.SemaphoreType.DMA((4,))],
        input_output_aliases={4: 0},
        compiler_params=pltpu.CompilerParams(vmem_limit_bytes=53 * MIB),
        cost_estimate=pl.CostEstimate(flops=8 * 6 * W**3, bytes_accessed=5 * MIB, transcendentals=0),
        name="below",
    )(table, px, py, speed, field, tops)


def above_kernel(table, straight, flipped, field, out, top):
    ghost = straight[...] + flipped[...]
    ghost = jnp.where(table[5] == 1, AMBIENT, ghost)
    new = field[0] + TIME_STEP * ghost
    out[0] = new
    top[...] = new


def above_update(table, straight, flipped, field):
    last = pl.BlockSpec((1, W, W), lambda i: (NZ - 1, 0, 0))
    return pl.pallas_call(
        above_kernel,
        grid=(1,),
        out_shape=(plane_shape(NZ), plane_shape()),
        in_specs=[SMEM_SPEC, full((W, W)), full((W, W)), last],
        out_specs=[last, full((W, W))],
        input_output_aliases={3: 0},
        compiler_params=pltpu.CompilerParams(vmem_limit_bytes=53 * MIB),
        cost_estimate=pl.CostEstimate(flops=3 * W * W, bytes_accessed=MIB, transcendentals=0),
        name="above",
    )(table, straight, flipped, field)


def rims_kernel(field, row_low, row_high, col_low, col_high, low, high):
    z = pl.program_id(0)
    plane = field[0]
    row_low[pl.ds(z, 1), :] = plane[0:1, :]
    row_high[pl.ds(z, 1), :] = plane[W - 1 : W, :]
    lane = lax.broadcasted_iota(jnp.int32, (W, 128), 1)

    @pl.when(z == 0)
    def _():
        low[...] = jnp.zeros_like(low)
        high[...] = jnp.zeros_like(high)

    low[...] = jnp.where(lane == z, plane[:, 0:1], low[...])
    high[...] = jnp.where(lane == z, plane[:, W - 1 : W], high[...])

    @pl.when(z == NZ - 1)
    def _():
        col_low[...] = low[...].T[:NZ]
        col_high[...] = high[...].T[:NZ]


def rims_of(field):
    rim = jax.ShapeDtypeStruct((NZ, W), F32)
    return pl.pallas_call(
        rims_kernel,
        grid=(NZ,),
        out_shape=(rim,) * 4,
        in_specs=[pl.BlockSpec((1, W, W), lambda z: (z, 0, 0))],
        out_specs=[full((NZ, W))] * 4,
        scratch_shapes=[pltpu.VMEM((W, 128), F32)] * 2,
        compiler_params=pltpu.CompilerParams(vmem_limit_bytes=53 * MIB),
        cost_estimate=pl.CostEstimate(flops=NZ * W * W, bytes_accessed=4 * MIB, transcendentals=0),
        name="rims",
    )(field)


def stencil_kernel(inverse, here, below, above, speed, inlets, x_low, x_high, y_low, y_high, out, low, high):
    z = pl.program_id(0)

    @pl.when(z == 0)
    def _():
        pad = jnp.zeros((128 - NZ, W), F32)
        low[...] = jnp.concatenate([y_low[...], pad], axis=0).T
        high[...] = jnp.concatenate([y_high[...], pad], axis=0).T

    field = here[0]
    pick = lax.broadcasted_iota(jnp.int32, (W, 128), 1) == z
    col_low = jnp.sum(jnp.where(pick, low[...], 0.0), axis=1, keepdims=True)
    col_high = jnp.sum(jnp.where(pick, high[...], 0.0), axis=1, keepdims=True)
    row = lax.broadcasted_iota(jnp.int32, (W, W), 0)
    lane = lax.broadcasted_iota(jnp.int32, (W, W), 1)
    beside = jnp.where(row == 0, x_low[pl.ds(z, 1), :], pltpu.roll(field, 1, 0))
    beside = beside + jnp.where(row == W - 1, x_high[pl.ds(z, 1), :], pltpu.roll(field, W - 1, 0))
    beside = beside + jnp.where(lane == 0, col_low, pltpu.roll(field, 1, 1))
    beside = beside + jnp.where(lane == W - 1, col_high, pltpu.roll(field, W - 1, 1))
    lapl = (beside - 4.0 * field) * inverse[0]
    under = jnp.where(z == 0, 0.0, below[0])
    over = jnp.where(z == NZ - 1, 0.0, above[0])
    change = lapl + over + under - 2.0 * field - speed[0] * (field - under)
    out[0] = field + TIME_STEP * change

    @pl.when(z == 0)
    def _():
        inject = INJECT_RATE * inlets[...].astype(F32)
        out[0] = out[0] + TIME_STEP * (inject * (1.0 - here[0]))


def stencil(inverse, field, speed, inlets, halos):
    rim = full((NZ, W))
    return pl.pallas_call(
        stencil_kernel,
        grid=(NZ,),
        out_shape=plane_shape(NZ),
        in_specs=[
            SMEM_SPEC,
            pl.BlockSpec((1, W, W), lambda z: (z, 0, 0)),
            pl.BlockSpec((1, W, W), lambda z: (jnp.maximum(z - 1, 0), 0, 0)),
            pl.BlockSpec((1, W, W), lambda z: (jnp.minimum(z + 1, NZ - 1), 0, 0)),
            pl.BlockSpec((1, W, W), lambda z: (z, 0, 0)),
            full((W, W)),
            rim,
            rim,
            rim,
            rim,
        ],
        out_specs=pl.BlockSpec((1, W, W), lambda z: (z, 0, 0)),
        scratch_shapes=[pltpu.VMEM((W, 128), F32)] * 2,
        compiler_params=pltpu.CompilerParams(vmem_limit_bytes=53 * MIB),
        cost_estimate=pl.CostEstimate(flops=16 * NZ * W * W, bytes_accessed=12 * MIB, transcendentals=0),
        name="stencil",
    )(inverse, field, field, field, speed, inlets, *halos)


def exchange_rims(field):
    row_low, row_high, col_low, col_high = rims_of(field)
    x_low = lax.ppermute(row_high, "tile", [(t, t + TCOL) for t in range(TILES - TCOL)])
    x_high = lax.ppermute(row_low, "tile", [(t + TCOL, t) for t in range(TILES - TCOL)])
    inside = [t for t in range(TILES) if t % TCOL < TCOL - 1]
    y_low = lax.ppermute(col_high, "tile", [(t, t + 1) for t in inside])
    y_high = lax.ppermute(col_low, "tile", [(t + 1, t) for t in inside])
    return x_low, x_high, y_low, y_high


def send_y(value, steps):
    return lax.ppermute(value, "tile", along_y(steps))


def send_lift(value, steps, flip):
    return lax.ppermute(value, ("lift", "tile"), to_lift(steps, flip))


def other_core(value):
    return lax.ppermute(value, "tile", OTHER_CORE)


BY_HALF = [list(range(8)), list(range(8, 16))]


def gather_tops(top):
    pair = jnp.stack([send_lift(top, 1, False), send_lift(top, 1, True)])
    return lax.all_gather(pair, "tile", axis_index_groups=BY_HALF, axis=0, tiled=True)


def reduce_pieces(give, keep):
    slots = keep + other_core(give)
    far_mine = send_y(slots[4], 1)
    far_flip = send_y(slots[5], -1)
    right = jnp.stack([slots[2] + far_mine, slots[3]])
    left = jnp.stack([slots[6], slots[7] + far_flip])
    total = slots[0:2] + send_y(right, 1) + send_y(left, -1)
    return send_lift(total[0], -1, False), send_lift(total[1], -1, True)


def on_device(oxygen, velocity, spacing, inlets, proj_x, proj_y, sources):
    field = oxygen.reshape(NZ, W, W)
    speed = velocity.reshape(NZ, W, W)
    inlets = inlets.reshape(W, W)
    px = proj_x.reshape(4, W, W)
    py = proj_y.reshape(4, W, W)
    inverse = 1.0 / (spacing * spacing)
    tile = lax.axis_index("tile").astype(jnp.int32)
    is_top = (lax.axis_index("lift") == LIFTS - 1).astype(jnp.int32)
    table = jnp.concatenate([sources.reshape(4) & (TILES - 1), tile[None], is_top[None]])
    top, bottom = field[NZ - 1], field[0]
    for _ in range(STEPS):
        tops = gather_tops(top)
        parts = reduce_pieces(*pieces_of(table, px, py, bottom))
        halos = exchange_rims(field)
        field = stencil(inverse, field, speed, inlets, halos)
        field, bottom = below_update(table, px, py, speed[0], field, tops)
        field, top = above_update(table, *parts, field)
    return field.reshape(1, NZ, 1, W, W)


def solution(mesh):
    return jax.shard_map(
        on_device,
        mesh=mesh,
        in_specs=(
            P("lift", None, "tile", None, None),
            P("lift", None, "tile", None, None),
            P("lift"),
            P("lift", "tile", None, None),
            P("lift", "tile", None, None, None),
            P("lift", "tile", None, None, None),
            P("lift", "tile", None),
        ),
        out_specs=P("lift", None, "tile", None, None),
        check_vma=False,
    )
```

```python
import jax
import jax.numpy as jnp
from jax import lax
from jax.experimental import pallas as pl
from jax.experimental.pallas import tpu as pltpu
from jax.sharding import PartitionSpec as P

TCOL = 4
LIFTS = 8
TILES = 16
NZ = 16
W = 256
H = W // 2
TIME_STEP = 0.1
INJECT_RATE = 2.0
AMBIENT = 1.0
F32 = jnp.float32
BF16 = jnp.bfloat16
MIB = 1 << 20


def tile_of(x_half, y, core):
    return x_half * 8 + (y % 4) * 2 + core


def coords(tile):
    return tile // 8, (tile // 2) % 4, tile % 2


def along_y(steps):
    return [(t, tile_of(coords(t)[0], coords(t)[1] + steps, coords(t)[2])) for t in range(TILES)]


OTHER_CORE = [(t, t ^ 1) for t in range(TILES)]
OTHER_HALF = [(t, t ^ 8) for t in range(TILES)]
BY_HALF = [list(range(8)), list(range(8, 16))]


def to_lift(steps, flip):
    pairs = []
    for lift in range(LIFTS):
        if 0 <= lift + steps < LIFTS:
            for t in range(TILES):
                pairs.append((lift * TILES + t, (lift + steps) * TILES + (t ^ (8 if flip else 0))))
    return pairs


def send_y(value, steps):
    return lax.ppermute(value, "tile", along_y(steps))


def send_lift(value, steps, flip):
    return lax.ppermute(value, ("lift", "tile"), to_lift(steps, flip))


def split(value):
    high = value.astype(BF16)
    return high, (value - high.astype(F32)).astype(BF16)


def product(a, b, dims):
    def one(u, v):
        return lax.dot_general(u, v, (dims, ((), ())), preferred_element_type=F32)

    return one(a[0], b[0]) + (one(a[0], b[1]) + one(a[1], b[0]))


SMEM_SPEC = pl.BlockSpec(memory_space=pltpu.SMEM)
VMEM_SPEC = pl.BlockSpec(memory_space=pltpu.VMEM)


def planes(*count):
    return jax.ShapeDtypeStruct((*count, W, W), F32)


def cost(flops, mib):
    return pl.CostEstimate(flops=flops, bytes_accessed=mib * MIB, transcendentals=0)


def pieces_kernel(table, px, py, bottom, give, keep):
    give[...] = jnp.zeros_like(give)
    keep[...] = jnp.zeros_like(keep)
    plane = split(bottom[...])
    for k in range(4):
        left = product(split(px[k]), plane, ((0,), (0,)))
        piece = product(split(left), split(py[k]), ((1,), (0,)))
        source, tile = table[k], table[4]
        x_step = ((source >> 3) ^ (tile >> 3)) & 1
        y_step = ((source >> 1) - (tile >> 1)) & 3
        core_step = (source ^ tile) & 1
        place = jnp.where(y_step == 2, 0, jnp.where(y_step == 3, 3, y_step + 1))
        slot = x_step * 4 + place

        @pl.when(core_step == 0)
        def _():
            keep[slot] = keep[slot] + piece

        @pl.when(core_step == 1)
        def _():
            give[slot] = give[slot] + piece


def pieces_of(table, px, py, bottom):
    return pl.pallas_call(
        pieces_kernel,
        out_shape=(planes(8), planes(8)),
        in_specs=[SMEM_SPEC] + [VMEM_SPEC] * 3,
        out_specs=[VMEM_SPEC] * 2,
        compiler_params=pltpu.CompilerParams(vmem_limit_bytes=24 * MIB),
        cost_estimate=cost(8 * 6 * W**3, 7),
        name="pieces",
    )(table, px, py, bottom)


def below_kernel(table, px, py, speed, field, tops, out, picked, sems):
    def fetch(k):
        source, tile = table[k], table[4]
        x_step = ((source >> 3) ^ (tile >> 3)) & 1
        return pltpu.make_async_copy(tops.at[(source & 7) * 2 + x_step], picked.at[k], sems.at[k])

    for k in range(4):
        fetch(k).start()
    total = jnp.zeros((W, W), F32)
    for k in range(4):
        fetch(k).wait()
        left = product(split(px[k]), split(picked[k]), ((1,), (0,)))
        total = total + product(split(left), split(py[k]), ((1,), (1,)))
    total = jnp.where(table[5] == 1, total, 0.0)
    out[...] = field[...] + TIME_STEP * (total + speed[...] * total)


def below_update(table, px, py, speed, plane, tops):
    return pl.pallas_call(
        below_kernel,
        out_shape=planes(),
        in_specs=[SMEM_SPEC] + [VMEM_SPEC] * 4 + [pl.BlockSpec(memory_space=pltpu.HBM)],
        out_specs=VMEM_SPEC,
        scratch_shapes=[pltpu.VMEM((4, W, W), F32), pltpu.SemaphoreType.DMA((4,))],
        compiler_params=pltpu.CompilerParams(vmem_limit_bytes=16 * MIB),
        cost_estimate=cost(8 * 6 * W**3, 5),
        name="below",
    )(table, px, py, speed, plane, tops)


def rims_kernel(field, bottom, top, row_low, row_high, col_low, col_high):
    lane = lax.broadcasted_iota(jnp.int32, (W, 128), 1)
    low = jnp.zeros((W, 128), F32)
    high = jnp.zeros((W, 128), F32)
    for z in range(NZ):
        ref = bottom if z == 0 else top if z == NZ - 1 else field.at[z]
        row_low[z : z + 1, :] = ref[0:1, :]
        row_high[z : z + 1, :] = ref[W - 1 : W, :]
        low = jnp.where(lane == z, ref[:, 0:1], low)
        high = jnp.where(lane == z, ref[:, W - 1 : W], high)
    col_low[...] = low.T[:NZ]
    col_high[...] = high.T[:NZ]


def rims_of(field, bottom, top):
    rim = jax.ShapeDtypeStruct((NZ, W), F32)
    return pl.pallas_call(
        rims_kernel,
        out_shape=(rim,) * 4,
        in_specs=[VMEM_SPEC] * 3,
        out_specs=[VMEM_SPEC] * 4,
        compiler_params=pltpu.CompilerParams(vmem_limit_bytes=16 * MIB),
        cost_estimate=cost(NZ * W * W, 4),
        name="rims",
    )(field, bottom, top)


def stencil_kernel(inverse, field, bottom, top, speed, inlets, x_low, x_high, y_low, y_high, out, low, high):
    pad = jnp.zeros((128 - NZ, W), F32)
    low[...] = jnp.concatenate([y_low[...], pad], axis=0).T
    high[...] = jnp.concatenate([y_high[...], pad], axis=0).T
    scale = inverse[0]

    def update(z, here, under, over):
        pick = lax.broadcasted_iota(jnp.int32, (W, 128), 1) == z
        col_low = jnp.sum(jnp.where(pick, low[...], 0.0), axis=1, keepdims=True)
        col_high = jnp.sum(jnp.where(pick, high[...], 0.0), axis=1, keepdims=True)
        row = lax.broadcasted_iota(jnp.int32, (W, W), 0)
        lane = lax.broadcasted_iota(jnp.int32, (W, W), 1)
        beside = jnp.where(row == 0, x_low[pl.ds(z, 1), :], pltpu.roll(here, 1, 0))
        beside = beside + jnp.where(row == W - 1, x_high[pl.ds(z, 1), :], pltpu.roll(here, W - 1, 0))
        beside = beside + jnp.where(lane == 0, col_low, pltpu.roll(here, 1, 1))
        beside = beside + jnp.where(lane == W - 1, col_high, pltpu.roll(here, W - 1, 1))
        lapl = (beside - 4.0 * here) * scale
        change = lapl + over + under - 2.0 * here - speed[z] * (here - under)
        return here + TIME_STEP * change

    zero = jnp.zeros((W, W), F32)
    first = bottom[...]
    inject = INJECT_RATE * inlets[...].astype(F32)
    out[0] = update(0, first, zero, field[1]) + TIME_STEP * (inject * (1.0 - first))
    out[1] = update(1, field[1], first, field[2])

    def middle(z, carry):
        out[z] = update(z, field[z], field[z - 1], field[z + 1])
        return carry

    lax.fori_loop(2, NZ - 2, middle, 0)
    out[NZ - 2] = update(NZ - 2, field[NZ - 2], field[NZ - 3], top[...])
    out[NZ - 1] = update(NZ - 1, top[...], field[NZ - 2], zero)


def stencil(inverse, field, bottom, top, speed, inlets, halos):
    return pl.pallas_call(
        stencil_kernel,
        out_shape=planes(NZ),
        in_specs=[SMEM_SPEC] + [VMEM_SPEC] * 9,
        out_specs=VMEM_SPEC,
        scratch_shapes=[pltpu.VMEM((W, 128), F32)] * 2,
        compiler_params=pltpu.CompilerParams(vmem_limit_bytes=24 * MIB),
        cost_estimate=cost(16 * NZ * W * W, 12),
        name="stencil",
    )(inverse, field, bottom, top, speed, inlets, *halos)


def place_kernel(bottom, top, field, out, sems):
    copies = [
        pltpu.make_async_copy(bottom, out.at[0], sems.at[0]),
        pltpu.make_async_copy(top, out.at[NZ - 1], sems.at[1]),
    ]
    for copy in copies:
        copy.start()
    for copy in copies:
        copy.wait()


def place_ends(bottom, top, field):
    return pl.pallas_call(
        place_kernel,
        out_shape=planes(NZ),
        in_specs=[VMEM_SPEC] * 2 + [pl.BlockSpec(memory_space=pl.ANY)],
        out_specs=pl.BlockSpec(memory_space=pl.ANY),
        scratch_shapes=[pltpu.SemaphoreType.DMA((2,))],
        input_output_aliases={2: 0},
        cost_estimate=cost(1, 1),
        name="place_ends",
    )(bottom, top, field)


def exchange_rims(rims):
    row_low, row_high, col_low, col_high = rims
    x_low = lax.ppermute(row_high, "tile", [(t, t + TCOL) for t in range(TILES - TCOL)])
    x_high = lax.ppermute(row_low, "tile", [(t + TCOL, t) for t in range(TILES - TCOL)])
    inside = [t for t in range(TILES) if t % TCOL < TCOL - 1]
    y_low = lax.ppermute(col_high, "tile", [(t, t + 1) for t in inside])
    y_high = lax.ppermute(col_low, "tile", [(t + 1, t) for t in inside])
    return x_low, x_high, y_low, y_high


def climb(plane):
    return send_lift(plane, 1, False), send_lift(plane, 1, True)


def gather_pair(mine, flip):
    return lax.all_gather(jnp.stack([mine, flip]), "tile", axis_index_groups=BY_HALF, axis=0, tiled=True)


def reduce_pieces(give, keep):
    taken = lax.ppermute(give, "tile", OTHER_CORE)
    far = lax.ppermute(keep[4] + taken[4], "tile", OTHER_HALF)
    rest = lax.ppermute(keep[5:8] + taken[5:8], "tile", OTHER_HALF)
    far = far + (keep[0] + taken[0])
    from_left = send_y(far[:H], 1)
    from_right = send_y(far[H:], -1)
    mine = rest + (keep[1:4] + taken[1:4])
    right = jnp.concatenate([mine[1, :H] + from_left, mine[1, H:]])
    left = jnp.concatenate([mine[2, :H], mine[2, H:] + from_right])
    return mine[0] + (send_y(right, 1) + send_y(left, -1))


def on_device(oxygen, velocity, spacing, inlets, proj_x, proj_y, sources):
    field = oxygen.reshape(NZ, W, W)
    speed = velocity.reshape(NZ, W, W)
    inlets = inlets.reshape(W, W)
    px = proj_x.reshape(4, W, W)
    py = proj_y.reshape(4, W, W)
    inverse = 1.0 / (spacing * spacing)
    tile = lax.axis_index("tile").astype(jnp.int32)
    lift = lax.axis_index("lift")
    has_below = (lift > 0).astype(jnp.int32)
    is_top = lift == LIFTS - 1
    table = jnp.concatenate([sources.reshape(4) & (TILES - 1), tile[None], has_below[None]])
    speed_low = speed[0]
    bottom, top = field[0], field[NZ - 1]

    def with_above(plane, ghost):
        return plane + TIME_STEP * jnp.where(is_top, AMBIENT, send_lift(ghost, -1, False))

    mine, flip = climb(top)
    tops = gather_pair(mine, flip)
    ghost = reduce_pieces(*pieces_of(table, px, py, bottom))
    halos = exchange_rims(rims_of(field, bottom, top))
    field = stencil(inverse, field, bottom, top, speed, inlets, halos)
    mine, flip = climb(field[NZ - 1])
    bottom = below_update(table, px, py, speed_low, field[0], tops)
    tops = gather_pair(
        mine + TIME_STEP * ghost, flip + TIME_STEP * lax.ppermute(ghost, "tile", OTHER_HALF)
    )
    top = with_above(field[NZ - 1], ghost)
    ghost = reduce_pieces(*pieces_of(table, px, py, bottom))
    halos = exchange_rims(rims_of(field, bottom, top))
    field = stencil(inverse, field, bottom, top, speed, inlets, halos)
    bottom = below_update(table, px, py, speed_low, field[0], tops)
    top = with_above(field[NZ - 1], ghost)
    return place_ends(bottom, top, field).reshape(1, NZ, 1, W, W)


def solution(mesh):
    return jax.shard_map(
        on_device,
        mesh=mesh,
        in_specs=(
            P("lift", None, "tile", None, None),
            P("lift", None, "tile", None, None),
            P("lift"),
            P("lift", "tile", None, None),
            P("lift", "tile", None, None, None),
            P("lift", "tile", None, None, None),
            P("lift", "tile", None),
        ),
        out_specs=P("lift", None, "tile", None, None),
        check_vma=False,
    )
```

```python
import jax
import jax.numpy as jnp
from jax import lax
from jax.experimental import pallas as pl
from jax.experimental.pallas import tpu as pltpu
from jax.sharding import PartitionSpec as P

TCOL = 4
LIFTS = 8
TILES = 16
NZ = 16
W = 256
H = W // 2
TIME_STEP = 0.1
INJECT_RATE = 2.0
AMBIENT = 1.0
F32 = jnp.float32
BF16 = jnp.bfloat16
MIB = 1 << 20


def tile_of(x_half, y, core):
    return x_half * 8 + (y % 4) * 2 + core


def coords(tile):
    return tile // 8, (tile // 2) % 4, tile % 2


def along_y(steps):
    return [(t, tile_of(coords(t)[0], coords(t)[1] + steps, coords(t)[2])) for t in range(TILES)]


OTHER_CORE = [(t, t ^ 1) for t in range(TILES)]
OTHER_HALF = [(t, t ^ 8) for t in range(TILES)]
BY_HALF = [list(range(8)), list(range(8, 16))]


def to_lift(steps, flip):
    pairs = []
    for lift in range(LIFTS):
        if 0 <= lift + steps < LIFTS:
            for t in range(TILES):
                pairs.append((lift * TILES + t, (lift + steps) * TILES + (t ^ (8 if flip else 0))))
    return pairs


def send_y(value, steps):
    return lax.ppermute(value, "tile", along_y(steps))


def send_lift(value, steps, flip):
    return lax.ppermute(value, ("lift", "tile"), to_lift(steps, flip))


def split(value):
    high = value.astype(BF16)
    return high, (value - high.astype(F32)).astype(BF16)


def product(a, b, dims):
    def one(u, v):
        return lax.dot_general(u, v, (dims, ((), ())), preferred_element_type=F32)

    return one(a[0], b[0]) + (one(a[0], b[1]) + one(a[1], b[0]))


SMEM_SPEC = pl.BlockSpec(memory_space=pltpu.SMEM)
VMEM_SPEC = pl.BlockSpec(memory_space=pltpu.VMEM)


def planes(*count):
    return jax.ShapeDtypeStruct((*count, W, W), F32)


MARK = jax.ShapeDtypeStruct((8, 128), F32)


SMALL = pl.CostEstimate(flops=1024, bytes_accessed=1024, transcendentals=0)


def pieces_kernel(table, px, py, bottom, give, keep):
    give[...] = jnp.zeros_like(give)
    keep[...] = jnp.zeros_like(keep)
    plane = split(bottom[...])
    for k in range(4):
        left = product(split(px[k]), plane, ((0,), (0,)))
        piece = product(split(left), split(py[k]), ((1,), (0,)))
        source, tile = table[k], table[4]
        x_step = ((source >> 3) ^ (tile >> 3)) & 1
        y_step = ((source >> 1) - (tile >> 1)) & 3
        core_step = (source ^ tile) & 1
        slot = x_step * 4 + y_step

        @pl.when(core_step == 0)
        def _():
            keep[slot] = keep[slot] + piece

        @pl.when(core_step == 1)
        def _():
            give[slot] = give[slot] + piece


def pieces_of(table, px, py, bottom):
    return pl.pallas_call(
        pieces_kernel,
        out_shape=(planes(8), planes(8)),
        in_specs=[SMEM_SPEC] + [VMEM_SPEC] * 3,
        out_specs=[VMEM_SPEC] * 2,
        compiler_params=pltpu.CompilerParams(vmem_limit_bytes=24 * MIB),
        cost_estimate=SMALL,
        name="pieces",
    )(table, px, py, bottom)


def from_below(table, px, py, tops, picked, sems):
    def fetch(k):
        source, tile = table[k], table[4]
        x_step = ((source >> 3) ^ (tile >> 3)) & 1
        return pltpu.make_async_copy(tops.at[(source & 7) * 2 + x_step], picked.at[k], sems.at[k])

    for k in range(4):
        fetch(k).start()
    total = jnp.zeros((W, W), F32)
    for k in range(4):
        fetch(k).wait()
        left = product(split(px[k]), split(picked[k]), ((1,), (0,)))
        total = total + product(split(left), split(py[k]), ((1,), (1,)))
    return jnp.where(table[5] == 1, total, 0.0)


def below_kernel(mark, table, px, py, speed, field, tops, out, picked, sems):
    total = from_below(table, px, py, tops, picked, sems)
    out[...] = field[...] + TIME_STEP * (total + speed[...] * total)


def below_update(mark, table, px, py, speed, plane, tops):
    return pl.pallas_call(
        below_kernel,
        out_shape=planes(),
        in_specs=[SMEM_SPEC] * 2 + [VMEM_SPEC] * 4 + [pl.BlockSpec(memory_space=pltpu.HBM)],
        out_specs=VMEM_SPEC,
        scratch_shapes=[pltpu.VMEM((4, W, W), F32), pltpu.SemaphoreType.DMA((4,))],
        compiler_params=pltpu.CompilerParams(vmem_limit_bytes=50 * MIB),
        cost_estimate=SMALL,
        name="below",
    )(mark, table, px, py, speed, plane, tops)


def ends_kernel(table, px, py, speed, ghost, tops, field, out, picked, ends, sems):
    def end(i, back):
        plane = (0, NZ - 1)[i]
        if back:
            return pltpu.make_async_copy(ends.at[i], out.at[plane], sems.at[4 + i])
        return pltpu.make_async_copy(field.at[plane], ends.at[i], sems.at[4 + i])

    end(0, False).start()
    end(1, False).start()
    end(1, False).wait()
    ends[1] = ends[1] + TIME_STEP * jnp.where(table[6] == 1, AMBIENT, ghost[...])
    end(1, True).start()
    total = from_below(table, px, py, tops, picked, sems)
    end(0, False).wait()
    ends[0] = ends[0] + TIME_STEP * (total + speed[...] * total)
    end(0, True).start()
    end(1, True).wait()
    end(0, True).wait()


def fix_ends(table, px, py, speed, ghost, tops, field):
    return pl.pallas_call(
        ends_kernel,
        out_shape=planes(NZ),
        in_specs=[SMEM_SPEC] + [VMEM_SPEC] * 4 + [pl.BlockSpec(memory_space=pltpu.HBM)] * 2,
        out_specs=pl.BlockSpec(memory_space=pltpu.HBM),
        scratch_shapes=[
            pltpu.VMEM((4, W, W), F32),
            pltpu.VMEM((2, W, W), F32),
            pltpu.SemaphoreType.DMA((6,)),
        ],
        input_output_aliases={6: 0},
        compiler_params=pltpu.CompilerParams(vmem_limit_bytes=50 * MIB),
        cost_estimate=SMALL,
        name="fix_ends",
    )(table, px, py, speed, ghost, tops, field)


def rims_kernel(mark, field, bottom, top, row_low, row_high, col_low, col_high):
    lane = lax.broadcasted_iota(jnp.int32, (W, 128), 1)
    low = jnp.zeros((W, 128), F32)
    high = jnp.zeros((W, 128), F32)
    for z in range(NZ):
        ref = bottom if z == 0 else top if z == NZ - 1 else field.at[z]
        row_low[z : z + 1, :] = ref[0:1, :]
        row_high[z : z + 1, :] = ref[W - 1 : W, :]
        low = jnp.where(lane == z, ref[:, 0:1], low)
        high = jnp.where(lane == z, ref[:, W - 1 : W], high)
    col_low[...] = low.T[:NZ]
    col_high[...] = high.T[:NZ]


def rims_of(mark, field, bottom, top):
    rim = jax.ShapeDtypeStruct((NZ, W), F32)
    return pl.pallas_call(
        rims_kernel,
        out_shape=(rim,) * 4,
        in_specs=[SMEM_SPEC] + [VMEM_SPEC] * 3,
        out_specs=[VMEM_SPEC] * 4,
        compiler_params=pltpu.CompilerParams(vmem_limit_bytes=16 * MIB),
        cost_estimate=SMALL,
        name="rims",
    )(mark, field, bottom, top)


def stencil_kernel(inverse, field, bottom, top, speed, inlets, x_low, x_high, y_low, y_high, out, mark, low, high):
    mark[...] = jnp.zeros_like(mark)
    pad = jnp.zeros((128 - NZ, W), F32)
    low[...] = jnp.concatenate([y_low[...], pad], axis=0).T
    high[...] = jnp.concatenate([y_high[...], pad], axis=0).T
    scale = inverse[0]

    def update(z, here, under, over):
        pick = lax.broadcasted_iota(jnp.int32, (W, 128), 1) == z
        col_low = jnp.sum(jnp.where(pick, low[...], 0.0), axis=1, keepdims=True)
        col_high = jnp.sum(jnp.where(pick, high[...], 0.0), axis=1, keepdims=True)
        row = lax.broadcasted_iota(jnp.int32, (W, W), 0)
        lane = lax.broadcasted_iota(jnp.int32, (W, W), 1)
        beside = jnp.where(row == 0, x_low[pl.ds(z, 1), :], pltpu.roll(here, 1, 0))
        beside = beside + jnp.where(row == W - 1, x_high[pl.ds(z, 1), :], pltpu.roll(here, W - 1, 0))
        beside = beside + jnp.where(lane == 0, col_low, pltpu.roll(here, 1, 1))
        beside = beside + jnp.where(lane == W - 1, col_high, pltpu.roll(here, W - 1, 1))
        lapl = (beside - 4.0 * here) * scale
        change = lapl + over + under - 2.0 * here - speed[z] * (here - under)
        return here + TIME_STEP * change

    zero = jnp.zeros((W, W), F32)
    first = bottom[...]
    inject = INJECT_RATE * inlets[...].astype(F32)
    out[0] = update(0, first, zero, field[1]) + TIME_STEP * (inject * (1.0 - first))
    out[1] = update(1, field[1], first, field[2])

    def middle(z, carry):
        out[z] = update(z, field[z], field[z - 1], field[z + 1])
        return carry

    lax.fori_loop(2, NZ - 2, middle, 0)
    out[NZ - 2] = update(NZ - 2, field[NZ - 2], field[NZ - 3], top[...])
    out[NZ - 1] = update(NZ - 1, top[...], field[NZ - 2], zero)


def stencil(inverse, field, bottom, top, speed, inlets, halos):
    return pl.pallas_call(
        stencil_kernel,
        out_shape=(planes(NZ), MARK),
        in_specs=[SMEM_SPEC] + [VMEM_SPEC] * 9,
        out_specs=[VMEM_SPEC] * 2,
        scratch_shapes=[pltpu.VMEM((W, 128), F32)] * 2,
        compiler_params=pltpu.CompilerParams(vmem_limit_bytes=24 * MIB),
        cost_estimate=SMALL,
        name="stencil",
    )(inverse, field, bottom, top, speed, inlets, *halos)


def exchange_rims(rims):
    row_low, row_high, col_low, col_high = rims
    x_low = lax.ppermute(row_high, "tile", [(t, t + TCOL) for t in range(TILES - TCOL)])
    x_high = lax.ppermute(row_low, "tile", [(t + TCOL, t) for t in range(TILES - TCOL)])
    inside = [t for t in range(TILES) if t % TCOL < TCOL - 1]
    y_low = lax.ppermute(col_high, "tile", [(t, t + 1) for t in inside])
    y_high = lax.ppermute(col_low, "tile", [(t + 1, t) for t in inside])
    return x_low, x_high, y_low, y_high


def climb(plane):
    return send_lift(plane, 1, False), send_lift(plane, 1, True)


def gather_pair(mine, flip):
    return lax.all_gather(jnp.stack([mine, flip]), "tile", axis_index_groups=BY_HALF, axis=0, tiled=True)


def zero_of(value):
    return 0.0 * value[(0,) * value.ndim]


def reduce_cores(give, keep):
    taken = lax.ppermute(give, "tile", OTHER_CORE)
    slots = keep + taken
    return slots[4:8], slots[0:4], zero_of(slots)


def reduce_halves(give):
    return lax.ppermute(give, "tile", OTHER_HALF)


def reduce_ring(slots):
    return slots[0], send_y(slots[1], 1), send_y(slots[2], 2), send_y(slots[3], -1)


def on_device(oxygen, velocity, spacing, inlets, proj_x, proj_y, sources):
    field = oxygen.reshape(NZ, W, W)
    speed = velocity.reshape(NZ, W, W)
    inlets = inlets.reshape(W, W)
    px = proj_x.reshape(4, W, W)
    py = proj_y.reshape(4, W, W)
    inverse = 1.0 / (spacing * spacing)
    tile = lax.axis_index("tile").astype(jnp.int32)
    lift = lax.axis_index("lift")
    has_below = (lift > 0).astype(jnp.int32)
    is_top = lift == LIFTS - 1
    table = jnp.concatenate([sources.reshape(4) & (TILES - 1), tile[None], has_below[None], is_top[None].astype(jnp.int32)])
    speed_low = speed[0]
    bottom, top = field[0], field[NZ - 1]

    mine, flip = climb(top)
    give, keep = pieces_of(table, px, py, bottom)
    give, keep, mark = reduce_cores(give, keep)
    tops = gather_pair(mine + mark, flip + mark)
    got = reduce_halves(give)
    rims = rims_of(mark[None], field, bottom, top)
    field, mark = stencil(inverse, field, bottom, top, speed, inlets, exchange_rims(rims))
    low, high = field[0], field[NZ - 1]
    mine, flip = climb(high)
    slots = keep + got + zero_of(mark)
    own, *parts = reduce_ring(slots)
    bottom = below_update(zero_of(slots)[None], table, px, py, speed_low, low, tops)
    give, keep = pieces_of(table, px, py, bottom)
    give, keep, mark = reduce_cores(give, keep)
    got_near = reduce_halves(give[0:2])
    ghost = own + (parts[0] + parts[1] + parts[2]) + (mark + zero_of(got_near))
    other_ghost = lax.ppermute(ghost, "tile", OTHER_HALF)
    tops = gather_pair(mine + TIME_STEP * ghost, flip + TIME_STEP * other_ghost)
    ghost_above = jnp.where(is_top, AMBIENT, send_lift(ghost, -1, False))
    top = high + TIME_STEP * ghost_above
    got_far = reduce_halves(give[2:4])
    rims = rims_of(mark[None], field, bottom, top)
    field, mark = stencil(inverse, field, bottom, top, speed, inlets, exchange_rims(rims))
    near, far = keep[0:2] + got_near, keep[2:4] + got_far + zero_of(mark)
    own, *parts = reduce_ring([near[0], near[1], far[0], far[1]])
    ghost = send_lift(own + (parts[0] + parts[1] + parts[2]), -1, False)
    field = fix_ends(table, px, py, speed_low, ghost, tops, field)
    return field.reshape(1, NZ, 1, W, W)


def solution(mesh):
    return jax.shard_map(
        on_device,
        mesh=mesh,
        in_specs=(
            P("lift", None, "tile", None, None),
            P("lift", None, "tile", None, None),
            P("lift"),
            P("lift", "tile", None, None),
            P("lift", "tile", None, None, None),
            P("lift", "tile", None, None, None),
            P("lift", "tile", None),
        ),
        out_specs=P("lift", None, "tile", None, None),
        check_vma=False,
    )
```

```python
import jax
import jax.numpy as jnp
from jax import lax
from jax.experimental import pallas as pl
from jax.experimental.pallas import tpu as pltpu
from jax.sharding import PartitionSpec as P

TCOL = 4
LIFTS = 8
TILES = 16
NZ = 16
W = 256
H = W // 2
TIME_STEP = 0.1
INJECT_RATE = 2.0
AMBIENT = 1.0
F32 = jnp.float32
BF16 = jnp.bfloat16
MIB = 1 << 20


def tile_of(x_half, y, core):
    return x_half * 8 + (y % 4) * 2 + core


def coords(tile):
    return tile // 8, (tile // 2) % 4, tile % 2


def along_y(steps):
    return [(t, tile_of(coords(t)[0], coords(t)[1] + steps, coords(t)[2])) for t in range(TILES)]


OTHER_CORE = [(t, t ^ 1) for t in range(TILES)]
OTHER_HALF = [(t, t ^ 8) for t in range(TILES)]
BY_HALF = [list(range(8)), list(range(8, 16))]


def to_lift(steps, flip):
    pairs = []
    for lift in range(LIFTS):
        if 0 <= lift + steps < LIFTS:
            for t in range(TILES):
                pairs.append((lift * TILES + t, (lift + steps) * TILES + (t ^ (8 if flip else 0))))
    return pairs


def send_y(value, steps):
    return lax.ppermute(value, "tile", along_y(steps))


def send_lift(value, steps, flip):
    return lax.ppermute(value, ("lift", "tile"), to_lift(steps, flip))


def split(value):
    high = value.astype(BF16)
    return high, (value - high.astype(F32)).astype(BF16)


def product(a, b, dims):
    def one(u, v):
        return lax.dot_general(u, v, (dims, ((), ())), preferred_element_type=F32)

    return one(a[0], b[0]) + (one(a[0], b[1]) + one(a[1], b[0]))


SMEM_SPEC = pl.BlockSpec(memory_space=pltpu.SMEM)
VMEM_SPEC = pl.BlockSpec(memory_space=pltpu.VMEM)


def planes(*count):
    return jax.ShapeDtypeStruct((*count, W, W), F32)


MARK = jax.ShapeDtypeStruct((8, 128), F32)


SMALL = pl.CostEstimate(flops=1024, bytes_accessed=1024, transcendentals=0)


def pieces_kernel(table, px, py, bottom, give, keep):
    give[...] = jnp.zeros_like(give)
    keep[...] = jnp.zeros_like(keep)
    plane = split(bottom[...])
    for k in range(4):
        left = product(split(px[k]), plane, ((0,), (0,)))
        piece = product(split(left), split(py[k]), ((1,), (0,)))
        source, tile = table[k], table[4]
        x_step = ((source >> 3) ^ (tile >> 3)) & 1
        y_step = ((source >> 1) - (tile >> 1)) & 3
        core_step = (source ^ tile) & 1
        slot = x_step * 4 + y_step

        @pl.when(core_step == 0)
        def _():
            keep[slot] = keep[slot] + piece

        @pl.when(core_step == 1)
        def _():
            give[slot] = give[slot] + piece


def pieces_of(table, px, py, bottom):
    return pl.pallas_call(
        pieces_kernel,
        out_shape=(planes(8), planes(8)),
        in_specs=[SMEM_SPEC] + [VMEM_SPEC] * 3,
        out_specs=[VMEM_SPEC] * 2,
        compiler_params=pltpu.CompilerParams(vmem_limit_bytes=24 * MIB),
        cost_estimate=SMALL,
        name="pieces",
    )(table, px, py, bottom)


def from_below(table, px, py, tops, picked, sems):
    def fetch(k):
        source, tile = table[k], table[4]
        x_step = ((source >> 3) ^ (tile >> 3)) & 1
        return pltpu.make_async_copy(tops.at[(source & 7) * 2 + x_step], picked.at[k], sems.at[k])

    for k in range(4):
        fetch(k).start()
    total = jnp.zeros((W, W), F32)
    for k in range(4):
        fetch(k).wait()
        left = product(split(px[k]), split(picked[k]), ((1,), (0,)))
        total = total + product(split(left), split(py[k]), ((1,), (1,)))
    return jnp.where(table[5] == 1, total, 0.0)


def below_kernel(mark, table, px, py, speed, field, tops, out, picked, sems):
    total = from_below(table, px, py, tops, picked, sems)
    out[...] = field[...] + TIME_STEP * (total + speed[...] * total)


def below_update(mark, table, px, py, speed, plane, tops):
    return pl.pallas_call(
        below_kernel,
        out_shape=planes(),
        in_specs=[SMEM_SPEC] * 2 + [VMEM_SPEC] * 4 + [pl.BlockSpec(memory_space=pltpu.HBM)],
        out_specs=VMEM_SPEC,
        scratch_shapes=[pltpu.VMEM((4, W, W), F32), pltpu.SemaphoreType.DMA((4,))],
        compiler_params=pltpu.CompilerParams(vmem_limit_bytes=50 * MIB),
        cost_estimate=SMALL,
        name="below",
    )(mark, table, px, py, speed, plane, tops)


def ends_kernel(table, px, py, speed, ghost, tops, field, out, picked, ends, sems):
    def end(i, back):
        plane = (0, NZ - 1)[i]
        if back:
            return pltpu.make_async_copy(ends.at[i], out.at[plane], sems.at[4 + i])
        return pltpu.make_async_copy(field.at[plane], ends.at[i], sems.at[4 + i])

    end(0, False).start()
    end(1, False).start()
    end(1, False).wait()
    ends[1] = ends[1] + TIME_STEP * jnp.where(table[6] == 1, AMBIENT, ghost[...])
    end(1, True).start()
    total = from_below(table, px, py, tops, picked, sems)
    end(0, False).wait()
    ends[0] = ends[0] + TIME_STEP * (total + speed[...] * total)
    end(0, True).start()
    end(1, True).wait()
    end(0, True).wait()


def fix_ends(table, px, py, speed, ghost, tops, field):
    return pl.pallas_call(
        ends_kernel,
        out_shape=planes(NZ),
        in_specs=[SMEM_SPEC] + [VMEM_SPEC] * 4 + [pl.BlockSpec(memory_space=pltpu.HBM)] * 2,
        out_specs=pl.BlockSpec(memory_space=pltpu.HBM),
        scratch_shapes=[
            pltpu.VMEM((4, W, W), F32),
            pltpu.VMEM((2, W, W), F32),
            pltpu.SemaphoreType.DMA((6,)),
        ],
        input_output_aliases={6: 0},
        compiler_params=pltpu.CompilerParams(vmem_limit_bytes=50 * MIB),
        cost_estimate=SMALL,
        name="fix_ends",
    )(table, px, py, speed, ghost, tops, field)


def rims_kernel(mark, field, bottom, top, row_low, row_high, col_low, col_high):
    lane = lax.broadcasted_iota(jnp.int32, (W, 128), 1)
    low = jnp.zeros((W, 128), F32)
    high = jnp.zeros((W, 128), F32)
    for z in range(NZ):
        ref = bottom if z == 0 else top if z == NZ - 1 else field.at[z]
        row_low[z : z + 1, :] = ref[0:1, :]
        row_high[z : z + 1, :] = ref[W - 1 : W, :]
        low = jnp.where(lane == z, ref[:, 0:1], low)
        high = jnp.where(lane == z, ref[:, W - 1 : W], high)
    col_low[...] = low.T[:NZ]
    col_high[...] = high.T[:NZ]


def rims_of(mark, field, bottom, top):
    rim = jax.ShapeDtypeStruct((NZ, W), F32)
    return pl.pallas_call(
        rims_kernel,
        out_shape=(rim,) * 4,
        in_specs=[SMEM_SPEC] + [VMEM_SPEC] * 3,
        out_specs=[VMEM_SPEC] * 4,
        compiler_params=pltpu.CompilerParams(vmem_limit_bytes=16 * MIB),
        cost_estimate=SMALL,
        name="rims",
    )(mark, field, bottom, top)


def stencil_kernel(inverse, field, bottom, top, speed, inlets, x_low, x_high, y_low, y_high, out, mark, low, high):
    mark[...] = jnp.zeros_like(mark)
    pad = jnp.zeros((128 - NZ, W), F32)
    low[...] = jnp.concatenate([y_low[...], pad], axis=0).T
    high[...] = jnp.concatenate([y_high[...], pad], axis=0).T
    scale = inverse[0]

    def update(z, here, under, over):
        pick = lax.broadcasted_iota(jnp.int32, (W, 128), 1) == z
        col_low = jnp.sum(jnp.where(pick, low[...], 0.0), axis=1, keepdims=True)
        col_high = jnp.sum(jnp.where(pick, high[...], 0.0), axis=1, keepdims=True)
        row = lax.broadcasted_iota(jnp.int32, (W, W), 0)
        lane = lax.broadcasted_iota(jnp.int32, (W, W), 1)
        beside = jnp.where(row == 0, x_low[pl.ds(z, 1), :], pltpu.roll(here, 1, 0))
        beside = beside + jnp.where(row == W - 1, x_high[pl.ds(z, 1), :], pltpu.roll(here, W - 1, 0))
        beside = beside + jnp.where(lane == 0, col_low, pltpu.roll(here, 1, 1))
        beside = beside + jnp.where(lane == W - 1, col_high, pltpu.roll(here, W - 1, 1))
        lapl = (beside - 4.0 * here) * scale
        change = lapl + over + under - 2.0 * here - speed[z] * (here - under)
        return here + TIME_STEP * change

    zero = jnp.zeros((W, W), F32)
    first = bottom[...]
    inject = INJECT_RATE * inlets[...].astype(F32)
    out[0] = update(0, first, zero, field[1]) + TIME_STEP * (inject * (1.0 - first))
    out[1] = update(1, field[1], first, field[2])

    def middle(z, carry):
        out[z] = update(z, field[z], field[z - 1], field[z + 1])
        return carry

    lax.fori_loop(2, NZ - 2, middle, 0)
    out[NZ - 2] = update(NZ - 2, field[NZ - 2], field[NZ - 3], top[...])
    out[NZ - 1] = update(NZ - 1, top[...], field[NZ - 2], zero)


def stencil(inverse, field, bottom, top, speed, inlets, halos):
    return pl.pallas_call(
        stencil_kernel,
        out_shape=(planes(NZ), MARK),
        in_specs=[SMEM_SPEC] + [VMEM_SPEC] * 9,
        out_specs=[VMEM_SPEC] * 2,
        scratch_shapes=[pltpu.VMEM((W, 128), F32)] * 2,
        compiler_params=pltpu.CompilerParams(vmem_limit_bytes=24 * MIB),
        cost_estimate=SMALL,
        name="stencil",
    )(inverse, field, bottom, top, speed, inlets, *halos)


def exchange_rims(rims):
    row_low, row_high, col_low, col_high = rims
    x_low = lax.ppermute(row_high, "tile", [(t, t + TCOL) for t in range(TILES - TCOL)])
    x_high = lax.ppermute(row_low, "tile", [(t + TCOL, t) for t in range(TILES - TCOL)])
    inside = [t for t in range(TILES) if t % TCOL < TCOL - 1]
    y_low = lax.ppermute(col_high, "tile", [(t, t + 1) for t in inside])
    y_high = lax.ppermute(col_low, "tile", [(t + 1, t) for t in inside])
    return x_low, x_high, y_low, y_high


def climb(plane):
    return send_lift(plane, 1, False), send_lift(plane, 1, True)


def gather_pair(mine, flip):
    return lax.all_gather(jnp.stack([mine, flip]), "tile", axis_index_groups=BY_HALF, axis=0, tiled=True)


def zero_of(value):
    return 0.0 * value[(0,) * value.ndim]


def reduce_cores(give, keep):
    taken = lax.ppermute(give, "tile", OTHER_CORE)
    slots = keep + taken
    return slots[4:8], slots[0:4], zero_of(slots)


def reduce_halves(give):
    return lax.ppermute(give, "tile", OTHER_HALF)


def reduce_ring(slots):
    return slots[0], send_y(slots[1], 1), send_y(slots[2], 2), send_y(slots[3], -1)


def on_device(oxygen, velocity, spacing, inlets, proj_x, proj_y, sources):
    field = oxygen.reshape(NZ, W, W)
    speed = velocity.reshape(NZ, W, W)
    inlets = inlets.reshape(W, W)
    px = proj_x.reshape(4, W, W)
    py = proj_y.reshape(4, W, W)
    inverse = 1.0 / (spacing * spacing)
    tile = lax.axis_index("tile").astype(jnp.int32)
    lift = lax.axis_index("lift")
    has_below = (lift > 0).astype(jnp.int32)
    is_top = lift == LIFTS - 1
    table = jnp.concatenate([sources.reshape(4) & (TILES - 1), tile[None], has_below[None], is_top[None].astype(jnp.int32)])
    speed_low = speed[0]
    bottom, top = field[0], field[NZ - 1]

    mine, flip = climb(top)
    give, keep = pieces_of(table, px, py, bottom)
    mark = zero_of(keep)
    tops = gather_pair(mine + mark, flip + mark)
    give, keep, mark = reduce_cores(give, keep)
    got = reduce_halves(give)
    rims = rims_of(mark[None], field, bottom, top)
    field, mark = stencil(inverse, field, bottom, top, speed, inlets, exchange_rims(rims))
    low, high = field[0], field[NZ - 1]
    mine, flip = climb(high)
    slots = keep + got + zero_of(mark)
    own, *parts = reduce_ring(slots)
    mark = zero_of(slots) + zero_of(mine) + zero_of(flip)
    bottom = below_update(mark[None], table, px, py, speed_low, low, tops)
    ghost = own + (parts[0] + parts[1] + parts[2])
    other_ghost = lax.ppermute(ghost, "tile", OTHER_HALF)
    ghost_above = jnp.where(is_top, AMBIENT, send_lift(ghost, -1, False))
    give, keep = pieces_of(table, px, py, bottom + zero_of(ghost))
    mark = zero_of(keep)
    tops = gather_pair(mine + TIME_STEP * ghost + mark, flip + TIME_STEP * other_ghost)
    top = high + TIME_STEP * ghost_above
    give, keep, mark = reduce_cores(give, keep)
    got = reduce_halves(give + zero_of(ghost_above))
    halos = exchange_rims(rims_of(mark[None], field, bottom, top))
    field, mark = stencil(inverse, field, bottom, top, speed, inlets, halos)
    own, *parts = reduce_ring(keep + got + sum(zero_of(halo) for halo in halos))
    ghost = own + (parts[0] + parts[1] + parts[2]) + zero_of(mark)
    ghost = send_lift(ghost, -1, False)
    field = fix_ends(table, px, py, speed_low, ghost, tops, field)
    return field.reshape(1, NZ, 1, W, W)


def solution(mesh):
    return jax.shard_map(
        on_device,
        mesh=mesh,
        in_specs=(
            P("lift", None, "tile", None, None),
            P("lift", None, "tile", None, None),
            P("lift"),
            P("lift", "tile", None, None),
            P("lift", "tile", None, None, None),
            P("lift", "tile", None, None, None),
            P("lift", "tile", None),
        ),
        out_specs=P("lift", None, "tile", None, None),
        check_vma=False,
    )
```

```python
import jax
import jax.numpy as jnp
from jax import lax
from jax.experimental import pallas as pl
from jax.experimental.pallas import tpu as pltpu
from jax.sharding import PartitionSpec as P

TCOL = 4
LIFTS = 8
TILES = 16
NZ = 16
W = 256
H = W // 2
TIME_STEP = 0.1
INJECT_RATE = 2.0
AMBIENT = 1.0
F32 = jnp.float32
BF16 = jnp.bfloat16
MIB = 1 << 20


def tile_of(x_half, y, core):
    return x_half * 8 + (y % 4) * 2 + core


def coords(tile):
    return tile // 8, (tile // 2) % 4, tile % 2


def along_y(steps):
    return [(t, tile_of(coords(t)[0], coords(t)[1] + steps, coords(t)[2])) for t in range(TILES)]


OTHER_CORE = [(t, t ^ 1) for t in range(TILES)]
OTHER_HALF = [(t, t ^ 8) for t in range(TILES)]
BY_HALF = [list(range(8)), list(range(8, 16))]


def to_lift(steps, flip):
    return [
        (lift * TILES + t, (lift + steps) % LIFTS * TILES + (t ^ (8 if flip else 0)))
        for lift in range(LIFTS)
        for t in range(TILES)
    ]


def send_y(value, steps):
    return lax.ppermute(value, "tile", along_y(steps))


def send_lift(value, steps, flip):
    return lax.ppermute(value, ("lift", "tile"), to_lift(steps, flip))


def split(value):
    high = value.astype(BF16)
    return high, (value - high.astype(F32)).astype(BF16)


def product(a, b, dims):
    def one(u, v):
        return lax.dot_general(u, v, (dims, ((), ())), preferred_element_type=F32)

    return one(a[0], b[0]) + (one(a[0], b[1]) + one(a[1], b[0]))


SMEM_SPEC = pl.BlockSpec(memory_space=pltpu.SMEM)
VMEM_SPEC = pl.BlockSpec(memory_space=pltpu.VMEM)


def planes(*count):
    return jax.ShapeDtypeStruct((*count, W, W), F32)


MARK = jax.ShapeDtypeStruct((8, 128), F32)


SMALL = pl.CostEstimate(flops=1024, bytes_accessed=1024, transcendentals=0)


def pieces_kernel(table, px, py, bottom, *refs):
    give, keep, mark = refs[-3:]
    mark[...] = jnp.zeros_like(mark)
    give[...] = jnp.zeros_like(give)
    keep[...] = jnp.zeros_like(keep)
    plane = split(bottom[...])
    for k in range(4):
        left = product(split(px[k]), plane, ((0,), (0,)))
        piece = product(split(left), split(py[k]), ((1,), (0,)))
        source, tile = table[k], table[4]
        x_step = ((source >> 3) ^ (tile >> 3)) & 1
        y_step = ((source >> 1) - (tile >> 1)) & 3
        core_step = (source ^ tile) & 1
        slot = x_step * 4 + y_step

        @pl.when(core_step == 0)
        def _():
            keep[slot] = keep[slot] + piece

        @pl.when(core_step == 1)
        def _():
            give[slot] = give[slot] + piece


ANY_SPEC = pl.BlockSpec(memory_space=pl.ANY)


def pieces_of(table, px, py, bottom, *earlier):
    return pl.pallas_call(
        pieces_kernel,
        out_shape=(planes(8), planes(8), MARK),
        in_specs=[SMEM_SPEC] + [VMEM_SPEC] * 3 + [ANY_SPEC] * len(earlier),
        out_specs=[VMEM_SPEC] * 3,
        compiler_params=pltpu.CompilerParams(vmem_limit_bytes=24 * MIB),
        cost_estimate=SMALL,
        name="pieces",
    )(table, px, py, bottom, *earlier)


def small_kernel(body, name, out_shape, inputs, earlier=()):
    count = len(inputs)

    def kernel(*refs):
        body(*refs[:count], *refs[count + len(earlier) :])

    return pl.pallas_call(
        kernel,
        out_shape=out_shape,
        in_specs=[VMEM_SPEC] * count + [ANY_SPEC] * len(earlier),
        out_specs=jax.tree.map(lambda _: VMEM_SPEC, out_shape),
        compiler_params=pltpu.CompilerParams(vmem_limit_bytes=16 * MIB),
        cost_estimate=SMALL,
        name=name,
    )(*inputs, *earlier)


def pair_body(mine, flip, out):
    out[0] = mine[...]
    out[1] = flip[...]


def new_pair_body(mine, flip, ghost, other, out):
    out[0] = mine[...] + TIME_STEP * ghost[...]
    out[1] = flip[...] + TIME_STEP * other[...]


def cores_body(keep, taken, give_half, keep_half):
    keep_half[...] = keep[0:4] + taken[0:4]
    give_half[...] = keep[4:8] + taken[4:8]


def halves_body(keep, got, *outs):
    for i in range(4):
        outs[i][...] = keep[i] + got[i]


def ghost_body(own, a, b, c, out):
    out[...] = own[...] + (a[...] + b[...] + c[...])


def from_below(table, px, py, tops, picked, sems):
    def fetch(k):
        source, tile = table[k], table[4]
        x_step = ((source >> 3) ^ (tile >> 3)) & 1
        return pltpu.make_async_copy(tops.at[(source & 7) * 2 + x_step], picked.at[k], sems.at[k])

    for k in range(4):
        fetch(k).start()
    total = jnp.zeros((W, W), F32)
    for k in range(4):
        fetch(k).wait()
        left = product(split(px[k]), split(picked[k]), ((1,), (0,)))
        total = total + product(split(left), split(py[k]), ((1,), (1,)))
    return jnp.where(table[5] == 1, total, 0.0)


def below_kernel(table, px, py, speed, field, tops, *refs):
    out, picked, sems = refs[-3:]
    total = from_below(table, px, py, tops, picked, sems)
    out[...] = field[...] + TIME_STEP * (total + speed[...] * total)


def below_update(table, px, py, speed, plane, tops, *earlier):
    return pl.pallas_call(
        below_kernel,
        out_shape=planes(),
        in_specs=[SMEM_SPEC] + [VMEM_SPEC] * 4 + [pl.BlockSpec(memory_space=pltpu.HBM)] + [ANY_SPEC] * len(earlier),
        out_specs=VMEM_SPEC,
        scratch_shapes=[pltpu.VMEM((4, W, W), F32), pltpu.SemaphoreType.DMA((4,))],
        compiler_params=pltpu.CompilerParams(vmem_limit_bytes=50 * MIB),
        cost_estimate=SMALL,
        name="below",
    )(table, px, py, speed, plane, tops, *earlier)


def ends_kernel(table, px, py, speed, ghost, tops, field, out, picked, ends, sems):
    def end(i, back):
        plane = (0, NZ - 1)[i]
        if back:
            return pltpu.make_async_copy(ends.at[i], out.at[plane], sems.at[4 + i])
        return pltpu.make_async_copy(field.at[plane], ends.at[i], sems.at[4 + i])

    end(0, False).start()
    end(1, False).start()
    end(1, False).wait()
    ends[1] = ends[1] + TIME_STEP * jnp.where(table[6] == 1, AMBIENT, ghost[...])
    end(1, True).start()
    total = from_below(table, px, py, tops, picked, sems)
    end(0, False).wait()
    ends[0] = ends[0] + TIME_STEP * (total + speed[...] * total)
    end(0, True).start()
    end(1, True).wait()
    end(0, True).wait()


def fix_ends(table, px, py, speed, ghost, tops, field):
    return pl.pallas_call(
        ends_kernel,
        out_shape=planes(NZ),
        in_specs=[SMEM_SPEC] + [VMEM_SPEC] * 4 + [pl.BlockSpec(memory_space=pltpu.HBM)] * 2,
        out_specs=pl.BlockSpec(memory_space=pltpu.HBM),
        scratch_shapes=[
            pltpu.VMEM((4, W, W), F32),
            pltpu.VMEM((2, W, W), F32),
            pltpu.SemaphoreType.DMA((6,)),
        ],
        input_output_aliases={6: 0},
        compiler_params=pltpu.CompilerParams(vmem_limit_bytes=50 * MIB),
        cost_estimate=SMALL,
        name="fix_ends",
    )(table, px, py, speed, ghost, tops, field)


def rims_kernel(field, bottom, top, *refs):
    row_low, row_high, col_low, col_high = refs[-4:]
    lane = lax.broadcasted_iota(jnp.int32, (W, 128), 1)
    low = jnp.zeros((W, 128), F32)
    high = jnp.zeros((W, 128), F32)
    for z in range(NZ):
        ref = bottom if z == 0 else top if z == NZ - 1 else field.at[z]
        row_low[z : z + 1, :] = ref[0:1, :]
        row_high[z : z + 1, :] = ref[W - 1 : W, :]
        low = jnp.where(lane == z, ref[:, 0:1], low)
        high = jnp.where(lane == z, ref[:, W - 1 : W], high)
    col_low[...] = low.T[:NZ]
    col_high[...] = high.T[:NZ]


def rims_of(field, bottom, top, *earlier):
    rim = jax.ShapeDtypeStruct((NZ, W), F32)
    return pl.pallas_call(
        rims_kernel,
        out_shape=(rim,) * 4,
        in_specs=[VMEM_SPEC] * 3 + [ANY_SPEC] * len(earlier),
        out_specs=[VMEM_SPEC] * 4,
        compiler_params=pltpu.CompilerParams(vmem_limit_bytes=16 * MIB),
        cost_estimate=SMALL,
        name="rims",
    )(field, bottom, top, *earlier)


def stencil_kernel(inverse, inside, field, bottom, top, speed, inlets, x_low, x_high, y_low, y_high, out, mark, low, high):
    mark[...] = jnp.zeros_like(mark)
    pad = jnp.zeros((128 - NZ, W), F32)
    low[...] = jnp.concatenate([jnp.where(inside[2] == 1, y_low[...], 0.0), pad], axis=0).T
    high[...] = jnp.concatenate([jnp.where(inside[3] == 1, y_high[...], 0.0), pad], axis=0).T
    scale = inverse[0]

    def update(z, here, under, over):
        pick = lax.broadcasted_iota(jnp.int32, (W, 128), 1) == z
        col_low = jnp.sum(jnp.where(pick, low[...], 0.0), axis=1, keepdims=True)
        col_high = jnp.sum(jnp.where(pick, high[...], 0.0), axis=1, keepdims=True)
        row = lax.broadcasted_iota(jnp.int32, (W, W), 0)
        lane = lax.broadcasted_iota(jnp.int32, (W, W), 1)
        row_low = jnp.where(inside[0] == 1, x_low[pl.ds(z, 1), :], 0.0)
        row_high = jnp.where(inside[1] == 1, x_high[pl.ds(z, 1), :], 0.0)
        beside = jnp.where(row == 0, row_low, pltpu.roll(here, 1, 0))
        beside = beside + jnp.where(row == W - 1, row_high, pltpu.roll(here, W - 1, 0))
        beside = beside + jnp.where(lane == 0, col_low, pltpu.roll(here, 1, 1))
        beside = beside + jnp.where(lane == W - 1, col_high, pltpu.roll(here, W - 1, 1))
        lapl = (beside - 4.0 * here) * scale
        change = lapl + over + under - 2.0 * here - speed[z] * (here - under)
        return here + TIME_STEP * change

    zero = jnp.zeros((W, W), F32)
    first = bottom[...]
    inject = INJECT_RATE * inlets[...].astype(F32)
    out[0] = update(0, first, zero, field[1]) + TIME_STEP * (inject * (1.0 - first))
    out[1] = update(1, field[1], first, field[2])

    def middle(z, carry):
        out[z] = update(z, field[z], field[z - 1], field[z + 1])
        return carry

    lax.fori_loop(2, NZ - 2, middle, 0)
    out[NZ - 2] = update(NZ - 2, field[NZ - 2], field[NZ - 3], top[...])
    out[NZ - 1] = update(NZ - 1, top[...], field[NZ - 2], zero)


def stencil(inverse, inside, field, bottom, top, speed, inlets, halos):
    return pl.pallas_call(
        stencil_kernel,
        out_shape=(planes(NZ), MARK),
        in_specs=[SMEM_SPEC] * 2 + [VMEM_SPEC] * 9,
        out_specs=[VMEM_SPEC] * 2,
        scratch_shapes=[pltpu.VMEM((W, 128), F32)] * 2,
        compiler_params=pltpu.CompilerParams(vmem_limit_bytes=24 * MIB),
        cost_estimate=SMALL,
        name="stencil",
    )(inverse, inside, field, bottom, top, speed, inlets, *halos)


def exchange_rims(rims):
    row_low, row_high, col_low, col_high = rims
    up = [(t, (t + TCOL) % TILES) for t in range(TILES)]
    right = [(t, t - t % TCOL + (t + 1) % TCOL) for t in range(TILES)]
    x_low = lax.ppermute(row_high, "tile", up)
    x_high = lax.ppermute(row_low, "tile", [(d, s) for s, d in up])
    y_low = lax.ppermute(col_high, "tile", right)
    y_high = lax.ppermute(col_low, "tile", [(d, s) for s, d in right])
    return x_low, x_high, y_low, y_high


def climb(plane):
    return send_lift(plane, 1, False), send_lift(plane, 1, True)


def gather_pair(pair):
    return lax.all_gather(pair, "tile", axis_index_groups=BY_HALF, axis=0, tiled=True)


def reduce_cores(give, keep, *earlier):
    taken = lax.ppermute(give, "tile", OTHER_CORE)
    return small_kernel(cores_body, "cores_sum", (planes(4), planes(4)), (keep, taken), earlier)


def reduce_halves(give):
    return lax.ppermute(give, "tile", OTHER_HALF)


def reduce_ring(keep, got, *earlier):
    own, *others = small_kernel(halves_body, "halves_sum", (planes(),) * 4, (keep, got), earlier)
    return own, *(send_y(part, step) for part, step in zip(others, (1, 2, -1)))


def ghost_sum(parts, *earlier):
    return small_kernel(ghost_body, "ghost_sum", planes(), parts, earlier)


def on_device(oxygen, velocity, spacing, inlets, proj_x, proj_y, sources):
    field = oxygen.reshape(NZ, W, W)
    speed = velocity.reshape(NZ, W, W)
    inlets = inlets.reshape(W, W)
    px = proj_x.reshape(4, W, W)
    py = proj_y.reshape(4, W, W)
    inverse = 1.0 / (spacing * spacing)
    tile = lax.axis_index("tile").astype(jnp.int32)
    lift = lax.axis_index("lift")
    has_below = (lift > 0).astype(jnp.int32)
    is_top = lift == LIFTS - 1
    table = jnp.concatenate([sources.reshape(4) & (TILES - 1), tile[None], has_below[None], is_top[None].astype(jnp.int32)])
    inside = jnp.stack([tile >= TCOL, tile < TILES - TCOL, tile % TCOL > 0, tile % TCOL < TCOL - 1]).astype(jnp.int32)
    speed_low = speed[0]
    bottom, top = field[0], field[NZ - 1]

    mine, flip = climb(top)
    give, keep, mark = pieces_of(table, px, py, bottom)
    tops = gather_pair(small_kernel(pair_body, "pair", planes(2), (mine, flip), (mark,)))
    give, keep = reduce_cores(give, keep)
    got = reduce_halves(give)
    halos = exchange_rims(rims_of(field, bottom, top, give))
    field, mark = stencil(inverse, inside, field, bottom, top, speed, inlets, halos)
    low, high = field[0], field[NZ - 1]
    mine, flip = climb(high)
    parts = reduce_ring(keep, got, mark)
    bottom = below_update(table, px, py, speed_low, low, tops, parts[0], mine, flip)
    ghost = ghost_sum(parts)
    other_ghost = lax.ppermute(ghost, "tile", OTHER_HALF)
    ghost_above = jnp.where(is_top, AMBIENT, send_lift(ghost, -1, False))
    give, keep, mark = pieces_of(table, px, py, bottom, ghost)
    pair = small_kernel(new_pair_body, "new_pair", planes(2), (mine, flip, ghost, other_ghost), (mark,))
    tops = gather_pair(pair)
    top = high + TIME_STEP * ghost_above
    give, keep = reduce_cores(give, keep, top)
    got = reduce_halves(give)
    halos = exchange_rims(rims_of(field, bottom, top, give))
    field, mark = stencil(inverse, inside, field, bottom, top, speed, inlets, halos)
    parts = reduce_ring(keep, got, *halos)
    ghost = send_lift(ghost_sum(parts, mark), -1, False)
    field = fix_ends(table, px, py, speed_low, ghost, tops, field)
    return field.reshape(1, NZ, 1, W, W)


def solution(mesh):
    return jax.shard_map(
        on_device,
        mesh=mesh,
        in_specs=(
            P("lift", None, "tile", None, None),
            P("lift", None, "tile", None, None),
            P("lift"),
            P("lift", "tile", None, None),
            P("lift", "tile", None, None, None),
            P("lift", "tile", None, None, None),
            P("lift", "tile", None),
        ),
        out_specs=P("lift", None, "tile", None, None),
        check_vma=False,
    )
```

```python
import jax
import jax.numpy as jnp
from jax import lax
from jax.experimental import pallas as pl
from jax.experimental.pallas import tpu as pltpu
from jax.sharding import PartitionSpec as P

TCOL = 4
LIFTS = 8
TILES = 16
NZ = 16
W = 256
H = W // 2
TIME_STEP = 0.1
INJECT_RATE = 2.0
AMBIENT = 1.0
F32 = jnp.float32
BF16 = jnp.bfloat16
MIB = 1 << 20


def tile_of(x_half, y, core):
    return x_half * 8 + (y % 4) * 2 + core


def coords(tile):
    return tile // 8, (tile // 2) % 4, tile % 2


def along_y(steps):
    return [(t, tile_of(coords(t)[0], coords(t)[1] + steps, coords(t)[2])) for t in range(TILES)]


OTHER_CORE = [(t, t ^ 1) for t in range(TILES)]
OTHER_HALF = [(t, t ^ 8) for t in range(TILES)]
BY_HALF = [list(range(8)), list(range(8, 16))]


def to_lift(steps, flip):
    return [
        (lift * TILES + t, (lift + steps) % LIFTS * TILES + (t ^ (8 if flip else 0)))
        for lift in range(LIFTS)
        for t in range(TILES)
    ]


def send_y(value, steps):
    return lax.ppermute(value, "tile", along_y(steps))


def send_lift(value, steps, flip):
    return lax.ppermute(value, ("lift", "tile"), to_lift(steps, flip))


def split(value):
    high = value.astype(BF16)
    return high, (value - high.astype(F32)).astype(BF16)


def product(a, b, dims):
    def one(u, v):
        return lax.dot_general(u, v, (dims, ((), ())), preferred_element_type=F32)

    return one(a[0], b[0]) + (one(a[0], b[1]) + one(a[1], b[0]))


SMEM_SPEC = pl.BlockSpec(memory_space=pltpu.SMEM)
VMEM_SPEC = pl.BlockSpec(memory_space=pltpu.VMEM)


def planes(*count):
    return jax.ShapeDtypeStruct((*count, W, W), F32)


MARK = jax.ShapeDtypeStruct((8, 128), F32)


SMALL = pl.CostEstimate(flops=1024, bytes_accessed=1024, transcendentals=0)


def pieces_kernel(table, px, py, bottom, *refs):
    give, keep, mark = refs[-3:]
    mark[...] = jnp.zeros_like(mark)
    give[...] = jnp.zeros_like(give)
    keep[...] = jnp.zeros_like(keep)
    plane = split(bottom[...])
    for k in range(4):
        left = product(split(px[k]), plane, ((0,), (0,)))
        piece = product(split(left), split(py[k]), ((1,), (0,)))
        source, tile = table[k], table[4]
        x_step = ((source >> 3) ^ (tile >> 3)) & 1
        y_step = ((source >> 1) - (tile >> 1)) & 3
        core_step = (source ^ tile) & 1
        slot = x_step * 4 + y_step

        @pl.when(core_step == 0)
        def _():
            keep[slot] = keep[slot] + piece

        @pl.when(core_step == 1)
        def _():
            give[slot] = give[slot] + piece


ANY_SPEC = pl.BlockSpec(memory_space=pl.ANY)


def pieces_of(table, px, py, bottom, *earlier):
    return pl.pallas_call(
        pieces_kernel,
        out_shape=(planes(8), planes(8), MARK),
        in_specs=[SMEM_SPEC] + [VMEM_SPEC] * 3 + [ANY_SPEC] * len(earlier),
        out_specs=[VMEM_SPEC] * 3,
        compiler_params=pltpu.CompilerParams(vmem_limit_bytes=24 * MIB),
        cost_estimate=SMALL,
        name="pieces",
    )(table, px, py, bottom, *earlier)


def small_kernel(body, name, out_shape, inputs, earlier=()):
    count = len(inputs)

    def kernel(*refs):
        body(*refs[:count], *refs[count + len(earlier) :])

    return pl.pallas_call(
        kernel,
        out_shape=out_shape,
        in_specs=[VMEM_SPEC] * count + [ANY_SPEC] * len(earlier),
        out_specs=jax.tree.map(lambda _: VMEM_SPEC, out_shape),
        compiler_params=pltpu.CompilerParams(vmem_limit_bytes=16 * MIB),
        cost_estimate=SMALL,
        name=name,
    )(*inputs, *earlier)


def pair_body(mine, flip, out):
    out[0] = mine[...]
    out[1] = flip[...]


def new_pair_body(mine, flip, ghost, other, out):
    out[0] = mine[...] + TIME_STEP * ghost[...]
    out[1] = flip[...] + TIME_STEP * other[...]


def cores_body(keep, taken, give_near, give_far, keep_half):
    keep_half[...] = keep[0:4] + taken[0:4]
    give_near[...] = keep[4:6] + taken[4:6]
    give_far[...] = keep[6:8] + taken[6:8]


def whole_cores_body(keep, taken, give_half, keep_half):
    keep_half[...] = keep[0:4] + taken[0:4]
    give_half[...] = keep[4:8] + taken[4:8]


def halves_body(keep, *refs):
    outs = refs[-4:]
    got = [ref.at[i] for ref in refs[:-4] for i in range(ref.shape[0])]
    for i in range(4):
        outs[i][...] = keep[i] + got[i][...]


def ghost_body(own, a, b, c, out):
    out[...] = own[...] + (a[...] + b[...] + c[...])


def from_below(table, px, py, tops, picked, sems):
    def fetch(k):
        source, tile = table[k], table[4]
        x_step = ((source >> 3) ^ (tile >> 3)) & 1
        return pltpu.make_async_copy(tops.at[(source & 7) * 2 + x_step], picked.at[k], sems.at[k])

    for k in range(4):
        fetch(k).start()
    total = jnp.zeros((W, W), F32)
    for k in range(4):
        fetch(k).wait()
        left = product(split(px[k]), split(picked[k]), ((1,), (0,)))
        total = total + product(split(left), split(py[k]), ((1,), (1,)))
    return jnp.where(table[5] == 1, total, 0.0)


def ends_copies(field, speed, ends, sems):
    return [
        pltpu.make_async_copy(field.at[0], ends.at[0], sems.at[4]),
        pltpu.make_async_copy(speed.at[0], ends.at[1], sems.at[5]),
    ]


def below_value(table, px, py, field, speed, tops, picked, ends, sems):
    copies = ends_copies(field, speed, ends, sems)
    for copy in copies:
        copy.start()
    total = from_below(table, px, py, tops, picked, sems)
    for copy in copies:
        copy.wait()
    return ends[0] + TIME_STEP * (total + ends[1] * total)


def below_kernel(table, px, py, field, speed, tops, *refs):
    out, *scratch = refs[-4:]
    out[...] = below_value(table, px, py, field, speed, tops, *scratch)


BELOW_SCRATCH = [
    pltpu.VMEM((4, W, W), F32),
    pltpu.VMEM((2, W, W), F32),
    pltpu.SemaphoreType.DMA((7,)),
]


def below_update(table, px, py, field, speed, tops, *earlier):
    return pl.pallas_call(
        below_kernel,
        out_shape=planes(),
        in_specs=[SMEM_SPEC] + [VMEM_SPEC] * 2 + [ANY_SPEC] * (3 + len(earlier)),
        out_specs=VMEM_SPEC,
        scratch_shapes=BELOW_SCRATCH,
        compiler_params=pltpu.CompilerParams(vmem_limit_bytes=50 * MIB),
        cost_estimate=SMALL,
        name="below",
    )(table, px, py, field, speed, tops, *earlier)


def fix_bottom_kernel(table, px, py, speed, tops, field, out, picked, ends, sems):
    ends[0] = below_value(table, px, py, field, speed, tops, picked, ends, sems)
    copy = pltpu.make_async_copy(ends.at[0], out.at[0], sems.at[6])
    copy.start()
    copy.wait()


def fix_bottom(table, px, py, speed, tops, field):
    return pl.pallas_call(
        fix_bottom_kernel,
        out_shape=planes(NZ),
        in_specs=[SMEM_SPEC] + [VMEM_SPEC] * 2 + [ANY_SPEC] * 2 + [pl.BlockSpec(memory_space=pltpu.HBM)],
        out_specs=pl.BlockSpec(memory_space=pltpu.HBM),
        scratch_shapes=BELOW_SCRATCH,
        input_output_aliases={5: 0},
        compiler_params=pltpu.CompilerParams(vmem_limit_bytes=50 * MIB),
        cost_estimate=SMALL,
        name="fix_bottom",
    )(table, px, py, speed, tops, field)


def fix_top_kernel(table, ghost, field, out, plane, sems):
    fetch = pltpu.make_async_copy(field.at[NZ - 1], plane, sems.at[0])
    fetch.start()
    fetch.wait()
    plane[...] = plane[...] + TIME_STEP * jnp.where(table[6] == 1, AMBIENT, ghost[...])
    store = pltpu.make_async_copy(plane, out.at[NZ - 1], sems.at[1])
    store.start()
    store.wait()


def fix_top(table, ghost, field):
    return pl.pallas_call(
        fix_top_kernel,
        out_shape=planes(NZ),
        in_specs=[SMEM_SPEC, VMEM_SPEC, pl.BlockSpec(memory_space=pltpu.HBM)],
        out_specs=pl.BlockSpec(memory_space=pltpu.HBM),
        scratch_shapes=[pltpu.VMEM((W, W), F32), pltpu.SemaphoreType.DMA((2,))],
        input_output_aliases={2: 0},
        compiler_params=pltpu.CompilerParams(vmem_limit_bytes=8 * MIB),
        cost_estimate=SMALL,
        name="fix_top",
    )(table, ghost, field)


def rims_kernel(field, bottom, top, *refs):
    row_low, row_high, col_low, col_high = refs[-4:]
    lane = lax.broadcasted_iota(jnp.int32, (W, 128), 1)
    low = jnp.zeros((W, 128), F32)
    high = jnp.zeros((W, 128), F32)
    for z in range(NZ):
        ref = bottom if z == 0 else top if z == NZ - 1 else field.at[z]
        row_low[z : z + 1, :] = ref[0:1, :]
        row_high[z : z + 1, :] = ref[W - 1 : W, :]
        low = jnp.where(lane == z, ref[:, 0:1], low)
        high = jnp.where(lane == z, ref[:, W - 1 : W], high)
    col_low[...] = low.T[:NZ]
    col_high[...] = high.T[:NZ]


def rims_of(field, bottom, top, *earlier):
    rim = jax.ShapeDtypeStruct((NZ, W), F32)
    return pl.pallas_call(
        rims_kernel,
        out_shape=(rim,) * 4,
        in_specs=[VMEM_SPEC] * 3 + [ANY_SPEC] * len(earlier),
        out_specs=[VMEM_SPEC] * 4,
        compiler_params=pltpu.CompilerParams(vmem_limit_bytes=16 * MIB),
        cost_estimate=SMALL,
        name="rims",
    )(field, bottom, top, *earlier)


def stencil_kernel(inverse, inside, field, bottom, top, speed, inlets, x_low, x_high, y_low, y_high, out, mark, low, high, fast, sems):
    def fetch(z):
        return pltpu.make_async_copy(speed.at[z], fast.at[z], sems.at[z])

    for z in range(NZ):
        fetch(z).start()
    mark[...] = jnp.zeros_like(mark)
    pad = jnp.zeros((128 - NZ, W), F32)
    low[...] = jnp.concatenate([jnp.where(inside[2] == 1, y_low[...], 0.0), pad], axis=0).T
    high[...] = jnp.concatenate([jnp.where(inside[3] == 1, y_high[...], 0.0), pad], axis=0).T
    scale = inverse[0]

    def update(z, here, under, over):
        fetch(z).wait()
        pick = lax.broadcasted_iota(jnp.int32, (W, 128), 1) == z
        col_low = jnp.sum(jnp.where(pick, low[...], 0.0), axis=1, keepdims=True)
        col_high = jnp.sum(jnp.where(pick, high[...], 0.0), axis=1, keepdims=True)
        row = lax.broadcasted_iota(jnp.int32, (W, W), 0)
        lane = lax.broadcasted_iota(jnp.int32, (W, W), 1)
        row_low = jnp.where(inside[0] == 1, x_low[pl.ds(z, 1), :], 0.0)
        row_high = jnp.where(inside[1] == 1, x_high[pl.ds(z, 1), :], 0.0)
        beside = jnp.where(row == 0, row_low, pltpu.roll(here, 1, 0))
        beside = beside + jnp.where(row == W - 1, row_high, pltpu.roll(here, W - 1, 0))
        beside = beside + jnp.where(lane == 0, col_low, pltpu.roll(here, 1, 1))
        beside = beside + jnp.where(lane == W - 1, col_high, pltpu.roll(here, W - 1, 1))
        lapl = (beside - 4.0 * here) * scale
        change = lapl + over + under - 2.0 * here - fast[z] * (here - under)
        return here + TIME_STEP * change

    zero = jnp.zeros((W, W), F32)
    first = bottom[...]
    inject = INJECT_RATE * inlets[...].astype(F32)
    out[0] = update(0, first, zero, field[1]) + TIME_STEP * (inject * (1.0 - first))
    out[1] = update(1, field[1], first, field[2])

    def middle(z, carry):
        out[z] = update(z, field[z], field[z - 1], field[z + 1])
        return carry

    lax.fori_loop(2, NZ - 2, middle, 0)
    out[NZ - 2] = update(NZ - 2, field[NZ - 2], field[NZ - 3], top[...])
    out[NZ - 1] = update(NZ - 1, top[...], field[NZ - 2], zero)


def stencil(inverse, inside, field, bottom, top, speed, inlets, halos):
    return pl.pallas_call(
        stencil_kernel,
        out_shape=(planes(NZ), MARK),
        in_specs=[SMEM_SPEC] * 2 + [VMEM_SPEC] * 3 + [ANY_SPEC] + [VMEM_SPEC] * 5,
        out_specs=[VMEM_SPEC] * 2,
        scratch_shapes=[pltpu.VMEM((W, 128), F32)] * 2
        + [pltpu.VMEM((NZ, W, W), F32), pltpu.SemaphoreType.DMA((NZ,))],
        compiler_params=pltpu.CompilerParams(vmem_limit_bytes=24 * MIB),
        cost_estimate=SMALL,
        name="stencil",
    )(inverse, inside, field, bottom, top, speed, inlets, *halos)


def exchange_rims(rims):
    row_low, row_high, col_low, col_high = rims
    up = [(t, (t + TCOL) % TILES) for t in range(TILES)]
    right = [(t, t - t % TCOL + (t + 1) % TCOL) for t in range(TILES)]
    x_low = lax.ppermute(row_high, "tile", up)
    x_high = lax.ppermute(row_low, "tile", [(d, s) for s, d in up])
    y_low = lax.ppermute(col_high, "tile", right)
    y_high = lax.ppermute(col_low, "tile", [(d, s) for s, d in right])
    return x_low, x_high, y_low, y_high


def climb(plane):
    return send_lift(plane, 1, False), send_lift(plane, 1, True)


def gather_pair(pair):
    return lax.all_gather(pair, "tile", axis_index_groups=BY_HALF, axis=0, tiled=True)


def reduce_cores(give, keep, body, *counts, earlier=()):
    taken = lax.ppermute(give, "tile", OTHER_CORE)
    shapes = tuple(planes(count) for count in (*counts, 4))
    return small_kernel(body, "cores_sum", shapes, (keep, taken), earlier)


def reduce_halves(give):
    return lax.ppermute(give, "tile", OTHER_HALF)


def reduce_ring(keep, got, *earlier):
    own, *others = small_kernel(halves_body, "halves_sum", (planes(),) * 4, (keep, *got), earlier)
    return own, *(send_y(part, step) for part, step in zip(others, (1, 2, -1)))


def ghost_sum(parts, *earlier):
    return small_kernel(ghost_body, "ghost_sum", planes(), parts, earlier)


def on_device(oxygen, velocity, spacing, inlets, proj_x, proj_y, sources):
    field = oxygen.reshape(NZ, W, W)
    speed = velocity.reshape(NZ, W, W)
    inlets = inlets.reshape(W, W)
    px = proj_x.reshape(4, W, W)
    py = proj_y.reshape(4, W, W)
    inverse = 1.0 / (spacing * spacing)
    tile = lax.axis_index("tile").astype(jnp.int32)
    lift = lax.axis_index("lift")
    has_below = (lift > 0).astype(jnp.int32)
    is_top = lift == LIFTS - 1
    table = jnp.concatenate([sources.reshape(4) & (TILES - 1), tile[None], has_below[None], is_top[None].astype(jnp.int32)])
    inside = jnp.stack([tile >= TCOL, tile < TILES - TCOL, tile % TCOL > 0, tile % TCOL < TCOL - 1]).astype(jnp.int32)
    bottom, top = field[0], field[NZ - 1]

    mine, flip = climb(top)
    rims = rims_of(field, bottom, top)
    halos = exchange_rims(rims)
    pair = small_kernel(pair_body, "pair", planes(2), (mine, flip), (rims[0],))
    tops = gather_pair(pair)
    give, keep, mark = pieces_of(table, px, py, bottom, pair)
    give, keep = reduce_cores(give, keep, whole_cores_body, 4, earlier=halos)
    got = reduce_halves(give)
    field, mark = stencil(inverse, inside, field, bottom, top, speed, inlets, halos)
    high = field[NZ - 1]
    mine, flip = climb(high)
    parts = reduce_ring(keep, [got], mark)
    bottom = below_update(table, px, py, field, speed, tops, parts[0])
    give, keep, mark = pieces_of(table, px, py, bottom, mine, flip)
    give_near, give_far, keep = reduce_cores(give, keep, cores_body, 2, 2)
    ghost = ghost_sum(parts, give_near, mine, flip)
    got_near = reduce_halves(give_near)
    other_ghost = reduce_halves(ghost)
    ghost_above = jnp.where(is_top, AMBIENT, send_lift(ghost, -1, False))
    pair = small_kernel(new_pair_body, "new_pair", planes(2), (mine, flip, ghost, other_ghost), (got_near,))
    tops = gather_pair(pair)
    top = high + TIME_STEP * ghost_above
    got_far = reduce_halves(give_far)
    halos = exchange_rims(rims_of(field, bottom, top))
    field, mark = stencil(inverse, inside, field, bottom, top, speed, inlets, halos)
    parts = reduce_ring(keep, [got_near, got_far], *halos)
    ghost = send_lift(ghost_sum(parts, mark), -1, False)
    field = fix_bottom(table, px, py, speed, tops, field)
    field = fix_top(table, ghost, field)
    return field.reshape(1, NZ, 1, W, W)


def solution(mesh):
    return jax.shard_map(
        on_device,
        mesh=mesh,
        in_specs=(
            P("lift", None, "tile", None, None),
            P("lift", None, "tile", None, None),
            P("lift"),
            P("lift", "tile", None, None),
            P("lift", "tile", None, None, None),
            P("lift", "tile", None, None, None),
            P("lift", "tile", None),
        ),
        out_specs=P("lift", None, "tile", None, None),
        check_vma=False,
    )
```

```python
import jax
import jax.numpy as jnp
from jax import lax
from jax.experimental import pallas as pl
from jax.experimental.pallas import tpu as pltpu
from jax.sharding import PartitionSpec as P

TCOL = 4
LIFTS = 8
TILES = 16
NZ = 16
W = 256
H = W // 2
TIME_STEP = 0.1
INJECT_RATE = 2.0
AMBIENT = 1.0
F32 = jnp.float32
BF16 = jnp.bfloat16
MIB = 1 << 20


def tile_of(x_half, y, core):
    return x_half * 8 + (y % 4) * 2 + core


def coords(tile):
    return tile // 8, (tile // 2) % 4, tile % 2


def along_y(steps):
    return [(t, tile_of(coords(t)[0], coords(t)[1] + steps, coords(t)[2])) for t in range(TILES)]


OTHER_CORE = [(t, t ^ 1) for t in range(TILES)]
OTHER_HALF = [(t, t ^ 8) for t in range(TILES)]
BY_HALF = [list(range(8)), list(range(8, 16))]


def to_lift(steps, flip):
    return [
        (lift * TILES + t, (lift + steps) % LIFTS * TILES + (t ^ (8 if flip else 0)))
        for lift in range(LIFTS)
        for t in range(TILES)
    ]


def send_y(value, steps):
    return lax.ppermute(value, "tile", along_y(steps))


def send_lift(value, steps, flip):
    return lax.ppermute(value, ("lift", "tile"), to_lift(steps, flip))


def split(value):
    high = value.astype(BF16)
    return high, (value - high.astype(F32)).astype(BF16)


def product(a, b, dims):
    def one(u, v):
        return lax.dot_general(u, v, (dims, ((), ())), preferred_element_type=F32)

    return one(a[0], b[0]) + (one(a[0], b[1]) + one(a[1], b[0]))


SMEM_SPEC = pl.BlockSpec(memory_space=pltpu.SMEM)
VMEM_SPEC = pl.BlockSpec(memory_space=pltpu.VMEM)


def planes(*count):
    return jax.ShapeDtypeStruct((*count, W, W), F32)


MARK = jax.ShapeDtypeStruct((8, 128), F32)


SMALL = pl.CostEstimate(flops=1024, bytes_accessed=1024, transcendentals=0)


def pieces_kernel(table, px, py, bottom, *refs):
    give, keep, mark = refs[-3:]
    mark[...] = jnp.zeros_like(mark)
    give[...] = jnp.zeros_like(give)
    keep[...] = jnp.zeros_like(keep)
    plane = split(bottom[...])
    for k in range(4):
        left = product(split(px[k]), plane, ((0,), (0,)))
        piece = product(split(left), split(py[k]), ((1,), (0,)))
        source, tile = table[k], table[4]
        x_step = ((source >> 3) ^ (tile >> 3)) & 1
        y_step = ((source >> 1) - (tile >> 1)) & 3
        core_step = (source ^ tile) & 1
        slot = x_step * 4 + y_step

        @pl.when(core_step == 0)
        def _():
            keep[slot] = keep[slot] + piece

        @pl.when(core_step == 1)
        def _():
            give[slot] = give[slot] + piece


ANY_SPEC = pl.BlockSpec(memory_space=pl.ANY)


def pieces_of(table, px, py, bottom, *earlier):
    return pl.pallas_call(
        pieces_kernel,
        out_shape=(planes(8), planes(8), MARK),
        in_specs=[SMEM_SPEC] + [VMEM_SPEC] * 3 + [ANY_SPEC] * len(earlier),
        out_specs=[VMEM_SPEC] * 3,
        compiler_params=pltpu.CompilerParams(vmem_limit_bytes=24 * MIB),
        cost_estimate=SMALL,
        name="pieces",
    )(table, px, py, bottom, *earlier)


def small_kernel(body, name, out_shape, inputs, earlier=()):
    count = len(inputs)

    def kernel(*refs):
        body(*refs[:count], *refs[count + len(earlier) :])

    return pl.pallas_call(
        kernel,
        out_shape=out_shape,
        in_specs=[VMEM_SPEC] * count + [ANY_SPEC] * len(earlier),
        out_specs=jax.tree.map(lambda _: VMEM_SPEC, out_shape),
        compiler_params=pltpu.CompilerParams(vmem_limit_bytes=16 * MIB),
        cost_estimate=SMALL,
        name=name,
    )(*inputs, *earlier)


def pair_body(mine, flip, out):
    out[0] = mine[...]
    out[1] = flip[...]


def new_pair_body(mine, flip, ghost, other, out):
    out[0] = mine[...] + TIME_STEP * ghost[...]
    out[1] = flip[...] + TIME_STEP * other[...]


def cores_body(keep, taken, give_near, give_far, keep_half):
    keep_half[...] = keep[0:4] + taken[0:4]
    give_near[...] = keep[4:6] + taken[4:6]
    give_far[...] = keep[6:8] + taken[6:8]


def whole_cores_body(keep, taken, give_half, keep_half):
    keep_half[...] = keep[0:4] + taken[0:4]
    give_half[...] = keep[4:8] + taken[4:8]


def halves_body(keep, *refs):
    outs = refs[-4:]
    got = [ref.at[i] for ref in refs[:-4] for i in range(ref.shape[0])]
    for i in range(4):
        outs[i][...] = keep[i] + got[i][...]


def ghost_body(own, a, b, c, out):
    out[...] = own[...] + (a[...] + b[...] + c[...])


def from_below(table, px, py, tops, picked, sems):
    def fetch(k):
        source, tile = table[k], table[4]
        x_step = ((source >> 3) ^ (tile >> 3)) & 1
        return pltpu.make_async_copy(tops.at[(source & 7) * 2 + x_step], picked.at[k], sems.at[k])

    for k in range(4):
        fetch(k).start()
    total = jnp.zeros((W, W), F32)
    for k in range(4):
        fetch(k).wait()
        left = product(split(px[k]), split(picked[k]), ((1,), (0,)))
        total = total + product(split(left), split(py[k]), ((1,), (1,)))
    return jnp.where(table[5] == 1, total, 0.0)


def ends_copies(field, speed, ends, sems):
    return [
        pltpu.make_async_copy(field.at[0], ends.at[0], sems.at[4]),
        pltpu.make_async_copy(speed.at[0], ends.at[1], sems.at[5]),
    ]


def below_value(table, px, py, field, speed, tops, picked, ends, sems):
    copies = ends_copies(field, speed, ends, sems)
    for copy in copies:
        copy.start()
    total = from_below(table, px, py, tops, picked, sems)
    for copy in copies:
        copy.wait()
    return ends[0] + TIME_STEP * (total + ends[1] * total)


def below_kernel(table, px, py, field, speed, tops, *refs):
    out, *scratch = refs[-4:]
    out[...] = below_value(table, px, py, field, speed, tops, *scratch)


BELOW_SCRATCH = [
    pltpu.VMEM((4, W, W), F32),
    pltpu.VMEM((2, W, W), F32),
    pltpu.SemaphoreType.DMA((7,)),
]


def below_update(table, px, py, field, speed, tops, *earlier):
    return pl.pallas_call(
        below_kernel,
        out_shape=planes(),
        in_specs=[SMEM_SPEC] + [VMEM_SPEC] * 2 + [ANY_SPEC] * (3 + len(earlier)),
        out_specs=VMEM_SPEC,
        scratch_shapes=BELOW_SCRATCH,
        compiler_params=pltpu.CompilerParams(vmem_limit_bytes=50 * MIB),
        cost_estimate=SMALL,
        name="below",
    )(table, px, py, field, speed, tops, *earlier)


def fix_bottom_kernel(table, px, py, speed, tops, field, out, picked, ends, sems):
    ends[0] = below_value(table, px, py, field, speed, tops, picked, ends, sems)
    copy = pltpu.make_async_copy(ends.at[0], out.at[0], sems.at[6])
    copy.start()
    copy.wait()


def fix_bottom(table, px, py, speed, tops, field):
    return pl.pallas_call(
        fix_bottom_kernel,
        out_shape=planes(NZ),
        in_specs=[SMEM_SPEC] + [VMEM_SPEC] * 2 + [ANY_SPEC] * 2 + [pl.BlockSpec(memory_space=pltpu.HBM)],
        out_specs=pl.BlockSpec(memory_space=pltpu.HBM),
        scratch_shapes=BELOW_SCRATCH,
        input_output_aliases={5: 0},
        compiler_params=pltpu.CompilerParams(vmem_limit_bytes=50 * MIB),
        cost_estimate=SMALL,
        name="fix_bottom",
    )(table, px, py, speed, tops, field)


def fix_top_kernel(table, ghost, field, out, plane, sems):
    fetch = pltpu.make_async_copy(field.at[NZ - 1], plane, sems.at[0])
    fetch.start()
    fetch.wait()
    plane[...] = plane[...] + TIME_STEP * jnp.where(table[6] == 1, AMBIENT, ghost[...])
    store = pltpu.make_async_copy(plane, out.at[NZ - 1], sems.at[1])
    store.start()
    store.wait()


def fix_top(table, ghost, field):
    return pl.pallas_call(
        fix_top_kernel,
        out_shape=planes(NZ),
        in_specs=[SMEM_SPEC, VMEM_SPEC, pl.BlockSpec(memory_space=pltpu.HBM)],
        out_specs=pl.BlockSpec(memory_space=pltpu.HBM),
        scratch_shapes=[pltpu.VMEM((W, W), F32), pltpu.SemaphoreType.DMA((2,))],
        input_output_aliases={2: 0},
        compiler_params=pltpu.CompilerParams(vmem_limit_bytes=8 * MIB),
        cost_estimate=SMALL,
        name="fix_top",
    )(table, ghost, field)


def rims_kernel(field, bottom, top, *refs):
    row_low, row_high, col_low, col_high = refs[-4:]
    lane = lax.broadcasted_iota(jnp.int32, (W, 128), 1)
    low = jnp.zeros((W, 128), F32)
    high = jnp.zeros((W, 128), F32)
    for z in range(NZ):
        ref = bottom if z == 0 else top if z == NZ - 1 else field.at[z]
        row_low[z : z + 1, :] = ref[0:1, :]
        row_high[z : z + 1, :] = ref[W - 1 : W, :]
        low = jnp.where(lane == z, ref[:, 0:1], low)
        high = jnp.where(lane == z, ref[:, W - 1 : W], high)
    col_low[...] = low.T[:NZ]
    col_high[...] = high.T[:NZ]


def rims_of(field, bottom, top, *earlier):
    rim = jax.ShapeDtypeStruct((NZ, W), F32)
    return pl.pallas_call(
        rims_kernel,
        out_shape=(rim,) * 4,
        in_specs=[VMEM_SPEC] * 3 + [ANY_SPEC] * len(earlier),
        out_specs=[VMEM_SPEC] * 4,
        compiler_params=pltpu.CompilerParams(vmem_limit_bytes=16 * MIB),
        cost_estimate=SMALL,
        name="rims",
    )(field, bottom, top, *earlier)


def stencil_kernel(inverse, inside, field, bottom, top, speed, inlets, x_low, x_high, y_low, y_high, out, mark, low, high, fast, sems):
    def fetch(z):
        return pltpu.make_async_copy(speed.at[z], fast.at[z], sems.at[z])

    for z in range(NZ):
        fetch(z).start()
    mark[...] = jnp.zeros_like(mark)
    pad = jnp.zeros((128 - NZ, W), F32)
    low[...] = jnp.concatenate([jnp.where(inside[2] == 1, y_low[...], 0.0), pad], axis=0).T
    high[...] = jnp.concatenate([jnp.where(inside[3] == 1, y_high[...], 0.0), pad], axis=0).T
    scale = inverse[0]

    def update(z, here, under, over):
        fetch(z).wait()
        pick = lax.broadcasted_iota(jnp.int32, (W, 128), 1) == z
        col_low = jnp.sum(jnp.where(pick, low[...], 0.0), axis=1, keepdims=True)
        col_high = jnp.sum(jnp.where(pick, high[...], 0.0), axis=1, keepdims=True)
        row = lax.broadcasted_iota(jnp.int32, (W, W), 0)
        lane = lax.broadcasted_iota(jnp.int32, (W, W), 1)
        row_low = jnp.where(inside[0] == 1, x_low[pl.ds(z, 1), :], 0.0)
        row_high = jnp.where(inside[1] == 1, x_high[pl.ds(z, 1), :], 0.0)
        beside = jnp.where(row == 0, row_low, pltpu.roll(here, 1, 0))
        beside = beside + jnp.where(row == W - 1, row_high, pltpu.roll(here, W - 1, 0))
        beside = beside + jnp.where(lane == 0, col_low, pltpu.roll(here, 1, 1))
        beside = beside + jnp.where(lane == W - 1, col_high, pltpu.roll(here, W - 1, 1))
        lapl = (beside - 4.0 * here) * scale
        change = lapl + over + under - 2.0 * here - fast[z] * (here - under)
        return here + TIME_STEP * change

    zero = jnp.zeros((W, W), F32)
    first = bottom[...]
    inject = INJECT_RATE * inlets[...].astype(F32)
    out[0] = update(0, first, zero, field[1]) + TIME_STEP * (inject * (1.0 - first))
    out[1] = update(1, field[1], first, field[2])

    def middle(z, carry):
        out[z] = update(z, field[z], field[z - 1], field[z + 1])
        return carry

    lax.fori_loop(2, NZ - 2, middle, 0)
    out[NZ - 2] = update(NZ - 2, field[NZ - 2], field[NZ - 3], top[...])
    out[NZ - 1] = update(NZ - 1, top[...], field[NZ - 2], zero)


def stencil(inverse, inside, field, bottom, top, speed, inlets, halos):
    return pl.pallas_call(
        stencil_kernel,
        out_shape=(planes(NZ), MARK),
        in_specs=[SMEM_SPEC] * 2 + [VMEM_SPEC] * 3 + [ANY_SPEC] + [VMEM_SPEC] * 5,
        out_specs=[VMEM_SPEC] * 2,
        scratch_shapes=[pltpu.VMEM((W, 128), F32)] * 2
        + [pltpu.VMEM((NZ, W, W), F32), pltpu.SemaphoreType.DMA((NZ,))],
        compiler_params=pltpu.CompilerParams(vmem_limit_bytes=24 * MIB),
        cost_estimate=SMALL,
        name="stencil",
    )(inverse, inside, field, bottom, top, speed, inlets, *halos)


def exchange_rims(rims):
    row_low, row_high, col_low, col_high = rims
    up = [(t, (t + TCOL) % TILES) for t in range(TILES)]
    right = [(t, t - t % TCOL + (t + 1) % TCOL) for t in range(TILES)]
    x_low = lax.ppermute(row_high, "tile", up)
    x_high = lax.ppermute(row_low, "tile", [(d, s) for s, d in up])
    y_low = lax.ppermute(col_high, "tile", right)
    y_high = lax.ppermute(col_low, "tile", [(d, s) for s, d in right])
    return x_low, x_high, y_low, y_high


def climb(plane):
    return send_lift(plane, 1, False), send_lift(plane, 1, True)


def gather_pair(pair):
    return lax.all_gather(pair, "tile", axis_index_groups=BY_HALF, axis=0, tiled=True)


def reduce_cores(give, keep, body, *counts, earlier=()):
    taken = lax.ppermute(give, "tile", OTHER_CORE)
    shapes = tuple(planes(count) for count in (*counts, 4))
    return small_kernel(body, "cores_sum", shapes, (keep, taken), earlier)


def reduce_halves(give):
    return lax.ppermute(give, "tile", OTHER_HALF)


def reduce_ring(keep, got, *earlier):
    own, *others = small_kernel(halves_body, "halves_sum", (planes(),) * 4, (keep, *got), earlier)
    return own, *(send_y(part, step) for part, step in zip(others, (1, 2, -1)))


def ghost_sum(parts, *earlier):
    return small_kernel(ghost_body, "ghost_sum", planes(), parts, earlier)


def on_device(oxygen, velocity, spacing, inlets, proj_x, proj_y, sources):
    field = oxygen.reshape(NZ, W, W)
    speed = velocity.reshape(NZ, W, W)
    inlets = inlets.reshape(W, W)
    px = proj_x.reshape(4, W, W)
    py = proj_y.reshape(4, W, W)
    inverse = 1.0 / (spacing * spacing)
    tile = lax.axis_index("tile").astype(jnp.int32)
    lift = lax.axis_index("lift")
    has_below = (lift > 0).astype(jnp.int32)
    is_top = lift == LIFTS - 1
    table = jnp.concatenate([sources.reshape(4) & (TILES - 1), tile[None], has_below[None], is_top[None].astype(jnp.int32)])
    inside = jnp.stack([tile >= TCOL, tile < TILES - TCOL, tile % TCOL > 0, tile % TCOL < TCOL - 1]).astype(jnp.int32)
    bottom, top = field[0], field[NZ - 1]

    mine, flip = climb(top)
    halos = exchange_rims(rims_of(field, bottom, top))
    pair = small_kernel(pair_body, "pair", planes(2), (mine, flip), halos)
    tops = gather_pair(pair)
    give, keep, mark = pieces_of(table, px, py, bottom, pair)
    give, keep = reduce_cores(give, keep, whole_cores_body, 4)
    got = reduce_halves(give)
    field, mark = stencil(inverse, inside, field, bottom, top, speed, inlets, halos)
    high = field[NZ - 1]
    mine, flip = climb(high)
    parts = reduce_ring(keep, [got], mark)
    bottom = below_update(table, px, py, field, speed, tops, parts[0])
    give, keep, mark = pieces_of(table, px, py, bottom, mine, flip, parts[1], parts[3])
    give_near, give_far, keep = reduce_cores(give, keep, cores_body, 2, 2)
    ghost = ghost_sum(parts, give_near, mine, flip)
    got_near = reduce_halves(give_near)
    other_ghost = reduce_halves(ghost)
    ghost_above = send_lift(ghost, -1, False)
    earlier = (got_near, ghost_above)
    pair = small_kernel(new_pair_body, "new_pair", planes(2), (mine, flip, ghost, other_ghost), earlier)
    tops = gather_pair(pair)
    top = high + TIME_STEP * jnp.where(is_top, AMBIENT, ghost_above)
    got_far = reduce_halves(give_far)
    halos = exchange_rims(rims_of(field, bottom, top))
    field, mark = stencil(inverse, inside, field, bottom, top, speed, inlets, halos)
    parts = reduce_ring(keep, [got_near, got_far], *halos)
    ghost = send_lift(ghost_sum(parts, mark), -1, False)
    field = fix_bottom(table, px, py, speed, tops, field)
    field = fix_top(table, ghost, field)
    return field.reshape(1, NZ, 1, W, W)


def solution(mesh):
    return jax.shard_map(
        on_device,
        mesh=mesh,
        in_specs=(
            P("lift", None, "tile", None, None),
            P("lift", None, "tile", None, None),
            P("lift"),
            P("lift", "tile", None, None),
            P("lift", "tile", None, None, None),
            P("lift", "tile", None, None, None),
            P("lift", "tile", None),
        ),
        out_specs=P("lift", None, "tile", None, None),
        check_vma=False,
    )
```

```python
import jax
import jax.numpy as jnp
from jax import lax
from jax.experimental import pallas as pl
from jax.experimental.pallas import tpu as pltpu
from jax.sharding import PartitionSpec as P

TCOL = 4
LIFTS = 8
TILES = 16
NZ = 16
W = 256
H = W // 2
TIME_STEP = 0.1
INJECT_RATE = 2.0
AMBIENT = 1.0
F32 = jnp.float32
BF16 = jnp.bfloat16
MIB = 1 << 20


def tile_of(x_half, y, core):
    return x_half * 8 + (y % 4) * 2 + core


def coords(tile):
    return tile // 8, (tile // 2) % 4, tile % 2


def along_y(steps):
    return [(t, tile_of(coords(t)[0], coords(t)[1] + steps, coords(t)[2])) for t in range(TILES)]


OTHER_CORE = [(t, t ^ 1) for t in range(TILES)]
OTHER_HALF = [(t, t ^ 8) for t in range(TILES)]
BY_HALF = [list(range(8)), list(range(8, 16))]


def to_lift(steps, flip):
    return [
        (lift * TILES + t, (lift + steps) % LIFTS * TILES + (t ^ (8 if flip else 0)))
        for lift in range(LIFTS)
        for t in range(TILES)
    ]


def send_y(value, steps):
    return lax.ppermute(value, "tile", along_y(steps))


def send_lift(value, steps, flip):
    return lax.ppermute(value, ("lift", "tile"), to_lift(steps, flip))


def split(value):
    high = value.astype(BF16)
    return high, (value - high.astype(F32)).astype(BF16)


def product(a, b, dims):
    def one(u, v):
        return lax.dot_general(u, v, (dims, ((), ())), preferred_element_type=F32)

    return one(a[0], b[0]) + (one(a[0], b[1]) + one(a[1], b[0]))


SMEM_SPEC = pl.BlockSpec(memory_space=pltpu.SMEM)
VMEM_SPEC = pl.BlockSpec(memory_space=pltpu.VMEM)


def planes(*count):
    return jax.ShapeDtypeStruct((*count, W, W), F32)


MARK = jax.ShapeDtypeStruct((8, 128), F32)


SMALL = pl.CostEstimate(flops=1024, bytes_accessed=1024, transcendentals=0)


def pieces_kernel(table, px, py, bottom, *refs):
    give, keep, mark = refs[-3:]
    mark[...] = jnp.zeros_like(mark)
    give[...] = jnp.zeros_like(give)
    keep[...] = jnp.zeros_like(keep)
    plane = split(bottom[...])
    for k in range(4):
        left = product(split(px[k]), plane, ((0,), (0,)))
        piece = product(split(left), split(py[k]), ((1,), (0,)))
        source, tile = table[k], table[4]
        x_step = ((source >> 3) ^ (tile >> 3)) & 1
        y_step = ((source >> 1) - (tile >> 1)) & 3
        core_step = (source ^ tile) & 1
        slot = x_step * 4 + y_step

        @pl.when(core_step == 0)
        def _():
            keep[slot] = keep[slot] + piece

        @pl.when(core_step == 1)
        def _():
            give[slot] = give[slot] + piece


ANY_SPEC = pl.BlockSpec(memory_space=pl.ANY)


def pieces_of(table, px, py, bottom, *earlier):
    return pl.pallas_call(
        pieces_kernel,
        out_shape=(planes(8), planes(8), MARK),
        in_specs=[SMEM_SPEC] + [VMEM_SPEC] * 3 + [ANY_SPEC] * len(earlier),
        out_specs=[VMEM_SPEC] * 3,
        compiler_params=pltpu.CompilerParams(vmem_limit_bytes=24 * MIB),
        cost_estimate=SMALL,
        name="pieces",
    )(table, px, py, bottom, *earlier)


def small_kernel(body, name, out_shape, inputs, earlier=()):
    count = len(inputs)

    def kernel(*refs):
        body(*refs[:count], *refs[count + len(earlier) :])

    return pl.pallas_call(
        kernel,
        out_shape=out_shape,
        in_specs=[VMEM_SPEC] * count + [ANY_SPEC] * len(earlier),
        out_specs=jax.tree.map(lambda _: VMEM_SPEC, out_shape),
        compiler_params=pltpu.CompilerParams(vmem_limit_bytes=16 * MIB),
        cost_estimate=SMALL,
        name=name,
    )(*inputs, *earlier)


def pair_body(mine, flip, out):
    out[0] = mine[...]
    out[1] = flip[...]


def new_pair_body(mine, flip, ghost, other, out):
    out[0] = mine[...] + TIME_STEP * ghost[...]
    out[1] = flip[...] + TIME_STEP * other[...]


def cores_body(keep, taken, give_near, give_far, keep_half):
    keep_half[...] = keep[0:4] + taken[0:4]
    give_near[...] = keep[4:5] + taken[4:5]
    give_far[...] = keep[5:8] + taken[5:8]


def whole_cores_body(keep, taken, give_half, keep_half):
    keep_half[...] = keep[0:4] + taken[0:4]
    give_half[...] = keep[4:8] + taken[4:8]


def halves_body(keep, *refs):
    outs = refs[-4:]
    got = [ref.at[i] for ref in refs[:-4] for i in range(ref.shape[0])]
    for i in range(4):
        outs[i][...] = keep[i] + got[i][...]


def ghost_body(own, a, b, c, out):
    out[...] = own[...] + (a[...] + b[...] + c[...])


def from_below(table, px, py, tops, picked, sems):
    def fetch(k):
        source, tile = table[k], table[4]
        x_step = ((source >> 3) ^ (tile >> 3)) & 1
        return pltpu.make_async_copy(tops.at[(source & 7) * 2 + x_step], picked.at[k], sems.at[k])

    for k in range(4):
        fetch(k).start()
    total = jnp.zeros((W, W), F32)
    for k in range(4):
        fetch(k).wait()
        left = product(split(px[k]), split(picked[k]), ((1,), (0,)))
        total = total + product(split(left), split(py[k]), ((1,), (1,)))
    return jnp.where(table[5] == 1, total, 0.0)


def ends_copies(field, speed, ends, sems):
    return [
        pltpu.make_async_copy(field.at[0], ends.at[0], sems.at[4]),
        pltpu.make_async_copy(speed.at[0], ends.at[1], sems.at[5]),
    ]


def below_value(table, px, py, field, speed, tops, picked, ends, sems):
    copies = ends_copies(field, speed, ends, sems)
    for copy in copies:
        copy.start()
    total = from_below(table, px, py, tops, picked, sems)
    for copy in copies:
        copy.wait()
    return ends[0] + TIME_STEP * (total + ends[1] * total)


def below_kernel(table, px, py, field, speed, tops, *refs):
    out, *scratch = refs[-4:]
    out[...] = below_value(table, px, py, field, speed, tops, *scratch)


BELOW_SCRATCH = [
    pltpu.VMEM((4, W, W), F32),
    pltpu.VMEM((2, W, W), F32),
    pltpu.SemaphoreType.DMA((7,)),
]


def below_update(table, px, py, field, speed, tops, *earlier):
    return pl.pallas_call(
        below_kernel,
        out_shape=planes(),
        in_specs=[SMEM_SPEC] + [VMEM_SPEC] * 2 + [ANY_SPEC] * (3 + len(earlier)),
        out_specs=VMEM_SPEC,
        scratch_shapes=BELOW_SCRATCH,
        compiler_params=pltpu.CompilerParams(vmem_limit_bytes=50 * MIB),
        cost_estimate=SMALL,
        name="below",
    )(table, px, py, field, speed, tops, *earlier)


def fix_bottom_kernel(table, px, py, speed, tops, field, out, picked, ends, sems):
    ends[0] = below_value(table, px, py, field, speed, tops, picked, ends, sems)
    copy = pltpu.make_async_copy(ends.at[0], out.at[0], sems.at[6])
    copy.start()
    copy.wait()


def fix_bottom(table, px, py, speed, tops, field):
    return pl.pallas_call(
        fix_bottom_kernel,
        out_shape=planes(NZ),
        in_specs=[SMEM_SPEC] + [VMEM_SPEC] * 2 + [ANY_SPEC] * 2 + [pl.BlockSpec(memory_space=pltpu.HBM)],
        out_specs=pl.BlockSpec(memory_space=pltpu.HBM),
        scratch_shapes=BELOW_SCRATCH,
        input_output_aliases={5: 0},
        compiler_params=pltpu.CompilerParams(vmem_limit_bytes=50 * MIB),
        cost_estimate=SMALL,
        name="fix_bottom",
    )(table, px, py, speed, tops, field)


def fix_top_kernel(table, ghost, field, out, plane, sems):
    fetch = pltpu.make_async_copy(field.at[NZ - 1], plane, sems.at[0])
    fetch.start()
    fetch.wait()
    plane[...] = plane[...] + TIME_STEP * jnp.where(table[6] == 1, AMBIENT, ghost[...])
    store = pltpu.make_async_copy(plane, out.at[NZ - 1], sems.at[1])
    store.start()
    store.wait()


def fix_top(table, ghost, field):
    return pl.pallas_call(
        fix_top_kernel,
        out_shape=planes(NZ),
        in_specs=[SMEM_SPEC, VMEM_SPEC, pl.BlockSpec(memory_space=pltpu.HBM)],
        out_specs=pl.BlockSpec(memory_space=pltpu.HBM),
        scratch_shapes=[pltpu.VMEM((W, W), F32), pltpu.SemaphoreType.DMA((2,))],
        input_output_aliases={2: 0},
        compiler_params=pltpu.CompilerParams(vmem_limit_bytes=8 * MIB),
        cost_estimate=SMALL,
        name="fix_top",
    )(table, ghost, field)


def rims_kernel(field, bottom, top, *refs):
    row_low, row_high, col_low, col_high = refs[-4:]
    lane = lax.broadcasted_iota(jnp.int32, (W, 128), 1)
    low = jnp.zeros((W, 128), F32)
    high = jnp.zeros((W, 128), F32)
    for z in range(NZ):
        ref = bottom if z == 0 else top if z == NZ - 1 else field.at[z]
        row_low[z : z + 1, :] = ref[0:1, :]
        row_high[z : z + 1, :] = ref[W - 1 : W, :]
        low = jnp.where(lane == z, ref[:, 0:1], low)
        high = jnp.where(lane == z, ref[:, W - 1 : W], high)
    col_low[...] = low.T[:NZ]
    col_high[...] = high.T[:NZ]


def rims_of(field, bottom, top, *earlier):
    rim = jax.ShapeDtypeStruct((NZ, W), F32)
    return pl.pallas_call(
        rims_kernel,
        out_shape=(rim,) * 4,
        in_specs=[VMEM_SPEC] * 3 + [ANY_SPEC] * len(earlier),
        out_specs=[VMEM_SPEC] * 4,
        compiler_params=pltpu.CompilerParams(vmem_limit_bytes=16 * MIB),
        cost_estimate=SMALL,
        name="rims",
    )(field, bottom, top, *earlier)


def stencil_kernel(inverse, inside, field, bottom, top, speed, inlets, x_low, x_high, y_low, y_high, out, mark, low, high, fast, sems):
    def fetch(z):
        return pltpu.make_async_copy(speed.at[z], fast.at[z], sems.at[z])

    for z in range(NZ):
        fetch(z).start()
    mark[...] = jnp.zeros_like(mark)
    pad = jnp.zeros((128 - NZ, W), F32)
    low[...] = jnp.concatenate([jnp.where(inside[2] == 1, y_low[...], 0.0), pad], axis=0).T
    high[...] = jnp.concatenate([jnp.where(inside[3] == 1, y_high[...], 0.0), pad], axis=0).T
    scale = inverse[0]

    def update(z, here, under, over):
        fetch(z).wait()
        pick = lax.broadcasted_iota(jnp.int32, (W, 128), 1) == z
        col_low = jnp.sum(jnp.where(pick, low[...], 0.0), axis=1, keepdims=True)
        col_high = jnp.sum(jnp.where(pick, high[...], 0.0), axis=1, keepdims=True)
        row = lax.broadcasted_iota(jnp.int32, (W, W), 0)
        lane = lax.broadcasted_iota(jnp.int32, (W, W), 1)
        row_low = jnp.where(inside[0] == 1, x_low[pl.ds(z, 1), :], 0.0)
        row_high = jnp.where(inside[1] == 1, x_high[pl.ds(z, 1), :], 0.0)
        beside = jnp.where(row == 0, row_low, pltpu.roll(here, 1, 0))
        beside = beside + jnp.where(row == W - 1, row_high, pltpu.roll(here, W - 1, 0))
        beside = beside + jnp.where(lane == 0, col_low, pltpu.roll(here, 1, 1))
        beside = beside + jnp.where(lane == W - 1, col_high, pltpu.roll(here, W - 1, 1))
        lapl = (beside - 4.0 * here) * scale
        change = lapl + over + under - 2.0 * here - fast[z] * (here - under)
        return here + TIME_STEP * change

    zero = jnp.zeros((W, W), F32)
    first = bottom[...]
    inject = INJECT_RATE * inlets[...].astype(F32)
    out[0] = update(0, first, zero, field[1]) + TIME_STEP * (inject * (1.0 - first))
    out[1] = update(1, field[1], first, field[2])

    def middle(z, carry):
        out[z] = update(z, field[z], field[z - 1], field[z + 1])
        return carry

    lax.fori_loop(2, NZ - 2, middle, 0)
    out[NZ - 2] = update(NZ - 2, field[NZ - 2], field[NZ - 3], top[...])
    out[NZ - 1] = update(NZ - 1, top[...], field[NZ - 2], zero)


def stencil(inverse, inside, field, bottom, top, speed, inlets, halos):
    return pl.pallas_call(
        stencil_kernel,
        out_shape=(planes(NZ), MARK),
        in_specs=[SMEM_SPEC] * 2 + [VMEM_SPEC] * 3 + [ANY_SPEC] + [VMEM_SPEC] * 5,
        out_specs=[VMEM_SPEC] * 2,
        scratch_shapes=[pltpu.VMEM((W, 128), F32)] * 2
        + [pltpu.VMEM((NZ, W, W), F32), pltpu.SemaphoreType.DMA((NZ,))],
        compiler_params=pltpu.CompilerParams(vmem_limit_bytes=24 * MIB),
        cost_estimate=SMALL,
        name="stencil",
    )(inverse, inside, field, bottom, top, speed, inlets, *halos)


def exchange_rims(rims):
    row_low, row_high, col_low, col_high = rims
    up = [(t, (t + TCOL) % TILES) for t in range(TILES)]
    right = [(t, t - t % TCOL + (t + 1) % TCOL) for t in range(TILES)]
    x_low = lax.ppermute(row_high, "tile", up)
    x_high = lax.ppermute(row_low, "tile", [(d, s) for s, d in up])
    y_low = lax.ppermute(col_high, "tile", right)
    y_high = lax.ppermute(col_low, "tile", [(d, s) for s, d in right])
    return x_low, x_high, y_low, y_high


def climb(plane):
    return send_lift(plane, 1, False), send_lift(plane, 1, True)


def gather_pair(pair):
    return lax.all_gather(pair, "tile", axis_index_groups=BY_HALF, axis=0, tiled=True)


def reduce_cores(give, keep, body, *counts, earlier=()):
    taken = lax.ppermute(give, "tile", OTHER_CORE)
    shapes = tuple(planes(count) for count in (*counts, 4))
    return small_kernel(body, "cores_sum", shapes, (keep, taken), earlier)


def reduce_halves(give):
    return lax.ppermute(give, "tile", OTHER_HALF)


def reduce_ring(keep, got, *earlier):
    own, *others = small_kernel(halves_body, "halves_sum", (planes(),) * 4, (keep, *got), earlier)
    return own, *(send_y(part, step) for part, step in zip(others, (1, 2, -1)))


def ghost_sum(parts, *earlier):
    return small_kernel(ghost_body, "ghost_sum", planes(), parts, earlier)


def on_device(oxygen, velocity, spacing, inlets, proj_x, proj_y, sources):
    field = oxygen.reshape(NZ, W, W)
    speed = velocity.reshape(NZ, W, W)
    inlets = inlets.reshape(W, W)
    px = proj_x.reshape(4, W, W)
    py = proj_y.reshape(4, W, W)
    inverse = 1.0 / (spacing * spacing)
    tile = lax.axis_index("tile").astype(jnp.int32)
    lift = lax.axis_index("lift")
    has_below = (lift > 0).astype(jnp.int32)
    is_top = lift == LIFTS - 1
    table = jnp.concatenate([sources.reshape(4) & (TILES - 1), tile[None], has_below[None], is_top[None].astype(jnp.int32)])
    inside = jnp.stack([tile >= TCOL, tile < TILES - TCOL, tile % TCOL > 0, tile % TCOL < TCOL - 1]).astype(jnp.int32)
    bottom, top = field[0], field[NZ - 1]

    mine, flip = climb(top)
    give, keep, mark = pieces_of(table, px, py, bottom)
    halos = exchange_rims(rims_of(field, bottom, top, mark))
    give, keep = reduce_cores(give, keep, whole_cores_body, 4, earlier=halos)
    tops = gather_pair(small_kernel(pair_body, "pair", planes(2), (mine, flip), (give,)))
    got = reduce_halves(give)
    field, mark = stencil(inverse, inside, field, bottom, top, speed, inlets, halos)
    high = field[NZ - 1]
    mine, flip = climb(high)
    parts = reduce_ring(keep, [got], mark)
    bottom = below_update(table, px, py, field, speed, tops, parts[0])
    give, keep, mark = pieces_of(table, px, py, bottom, mine, flip, parts[1], parts[3])
    give_near, give_far, keep = reduce_cores(give, keep, cores_body, 1, 3)
    ghost = ghost_sum(parts, give_near, mine, flip)
    got_near = reduce_halves(give_near)
    other_ghost = reduce_halves(ghost)
    ghost_above = send_lift(ghost, -1, False)
    earlier = (got_near, ghost_above)
    pair = small_kernel(new_pair_body, "new_pair", planes(2), (mine, flip, ghost, other_ghost), earlier)
    tops = gather_pair(pair)
    top = high + TIME_STEP * jnp.where(is_top, AMBIENT, ghost_above)
    got_far = reduce_halves(give_far)
    halos = exchange_rims(rims_of(field, bottom, top))
    field, mark = stencil(inverse, inside, field, bottom, top, speed, inlets, halos)
    parts = reduce_ring(keep, [got_near, got_far], *halos)
    ghost = send_lift(ghost_sum(parts, mark), -1, False)
    field = fix_bottom(table, px, py, speed, tops, field)
    field = fix_top(table, ghost, field)
    return field.reshape(1, NZ, 1, W, W)


def solution(mesh):
    return jax.shard_map(
        on_device,
        mesh=mesh,
        in_specs=(
            P("lift", None, "tile", None, None),
            P("lift", None, "tile", None, None),
            P("lift"),
            P("lift", "tile", None, None),
            P("lift", "tile", None, None, None),
            P("lift", "tile", None, None, None),
            P("lift", "tile", None),
        ),
        out_specs=P("lift", None, "tile", None, None),
        check_vma=False,
    )
```

```python
import jax
import jax.numpy as jnp
from jax import lax
from jax.experimental import pallas as pl
from jax.experimental.pallas import tpu as pltpu
from jax.sharding import PartitionSpec as P

TCOL = 4
LIFTS = 8
TILES = 16
NZ = 16
W = 256
H = W // 2
TIME_STEP = 0.1
INJECT_RATE = 2.0
AMBIENT = 1.0
F32 = jnp.float32
BF16 = jnp.bfloat16
MIB = 1 << 20


def tile_of(x_half, y, core):
    return x_half * 8 + (y % 4) * 2 + core


def coords(tile):
    return tile // 8, (tile // 2) % 4, tile % 2


def along_y(steps):
    return [(t, tile_of(coords(t)[0], coords(t)[1] + steps, coords(t)[2])) for t in range(TILES)]


OTHER_CORE = [(t, t ^ 1) for t in range(TILES)]
OTHER_HALF = [(t, t ^ 8) for t in range(TILES)]


def to_lift(steps, flip):
    return [
        (lift * TILES + t, (lift + steps) % LIFTS * TILES + (t ^ (8 if flip else 0)))
        for lift in range(LIFTS)
        for t in range(TILES)
    ]


def send_y(value, steps):
    return lax.ppermute(value, "tile", along_y(steps))


def send_lift(value, steps, flip):
    return lax.ppermute(value, ("lift", "tile"), to_lift(steps, flip))


def split(value):
    high = value.astype(BF16)
    return high, (value - high.astype(F32)).astype(BF16)


def product(a, b, dims):
    def one(u, v):
        return lax.dot_general(u, v, (dims, ((), ())), preferred_element_type=F32)

    return one(a[0], b[0]) + (one(a[0], b[1]) + one(a[1], b[0]))


SMEM_SPEC = pl.BlockSpec(memory_space=pltpu.SMEM)
VMEM_SPEC = pl.BlockSpec(memory_space=pltpu.VMEM)


def planes(*count):
    return jax.ShapeDtypeStruct((*count, W, W), F32)


MARK = jax.ShapeDtypeStruct((8, 128), F32)


SMALL = pl.CostEstimate(flops=1024, bytes_accessed=1024, transcendentals=0)


def pieces_kernel(table, px, py, bottom, *refs):
    give, keep, mark = refs[-3:]
    mark[...] = jnp.zeros_like(mark)
    give[...] = jnp.zeros_like(give)
    keep[...] = jnp.zeros_like(keep)
    plane = split(bottom[...])
    for k in range(4):
        left = product(split(px[k]), plane, ((0,), (0,)))
        piece = product(split(left), split(py[k]), ((1,), (0,)))
        source, tile = table[k], table[4]
        x_step = ((source >> 3) ^ (tile >> 3)) & 1
        y_step = ((source >> 1) - (tile >> 1)) & 3
        core_step = (source ^ tile) & 1
        slot = x_step * 4 + y_step

        @pl.when(core_step == 0)
        def _():
            keep[slot] = keep[slot] + piece

        @pl.when(core_step == 1)
        def _():
            give[slot] = give[slot] + piece


ANY_SPEC = pl.BlockSpec(memory_space=pl.ANY)


def pieces_of(table, px, py, bottom, *earlier):
    return pl.pallas_call(
        pieces_kernel,
        out_shape=(planes(8), planes(8), MARK),
        in_specs=[SMEM_SPEC] + [VMEM_SPEC] * 3 + [ANY_SPEC] * len(earlier),
        out_specs=[VMEM_SPEC] * 3,
        compiler_params=pltpu.CompilerParams(vmem_limit_bytes=24 * MIB),
        cost_estimate=SMALL,
        name="pieces",
    )(table, px, py, bottom, *earlier)


def small_kernel(body, name, out_shape, inputs, earlier=()):
    count = len(inputs)

    def kernel(*refs):
        body(*refs[:count], *refs[count + len(earlier) :])

    return pl.pallas_call(
        kernel,
        out_shape=out_shape,
        in_specs=[VMEM_SPEC] * count + [ANY_SPEC] * len(earlier),
        out_specs=jax.tree.map(lambda _: VMEM_SPEC, out_shape),
        compiler_params=pltpu.CompilerParams(vmem_limit_bytes=16 * MIB),
        cost_estimate=SMALL,
        name=name,
    )(*inputs, *earlier)


def pair_body(mine, flip, out):
    out[0] = mine[...]
    out[1] = flip[...]


def new_pair_body(mine, flip, ghost, other, out):
    out[0] = mine[...] + TIME_STEP * ghost[...]
    out[1] = flip[...] + TIME_STEP * other[...]


def cores_body(keep, taken, give_near, give_far, keep_half):
    keep_half[...] = keep[0:4] + taken[0:4]
    give_near[...] = keep[4:5] + taken[4:5]
    give_far[...] = keep[5:8] + taken[5:8]


def whole_cores_body(keep, taken, give_half, keep_half):
    keep_half[...] = keep[0:4] + taken[0:4]
    give_half[...] = keep[4:8] + taken[4:8]


def halves_body(keep, *refs):
    outs = refs[-4:]
    got = [ref.at[i] for ref in refs[:-4] for i in range(ref.shape[0])]
    for i in range(4):
        outs[i][...] = keep[i] + got[i][...]


def ghost_body(own, a, b, c, out):
    out[...] = own[...] + (a[...] + b[...] + c[...])


def from_below(table, px, py, tops, picked, sems):
    def place(k):
        source, tile = table[k], table[4]
        x_step = ((source >> 3) ^ (tile >> 3)) & 1
        y_step = ((source >> 1) - (tile >> 1)) & 3
        return (source ^ tile) & 1, y_step, x_step

    def fetch(plane, k):
        return pltpu.make_async_copy(plane, picked.at[k], sems.at[k])

    for k in range(4):
        core_step, y_step, x_step = place(k)
        for core in range(2):
            pair, right, left, *far = tops[5 * core : 5 * core + 5]
            for step, near in ((0, pair), (1, right), (3, left)):

                @pl.when((core_step == core) & (y_step == step))
                def _():
                    fetch(near.at[x_step], k).start()

            for half in range(2):

                @pl.when((core_step == core) & (y_step == 2) & (x_step == half))
                def _():
                    fetch(far[half], k).start()

    total = jnp.zeros((W, W), F32)
    for k in range(4):
        fetch(tops[3], k).wait()
        left = product(split(px[k]), split(picked[k]), ((1,), (0,)))
        total = total + product(split(left), split(py[k]), ((1,), (1,)))
    return jnp.where(table[5] == 1, total, 0.0)


def ends_copies(field, speed, ends, sems):
    return [
        pltpu.make_async_copy(field.at[0], ends.at[0], sems.at[4]),
        pltpu.make_async_copy(speed.at[0], ends.at[1], sems.at[5]),
    ]


def below_value(table, px, py, field, speed, tops, picked, ends, sems):
    copies = ends_copies(field, speed, ends, sems)
    for copy in copies:
        copy.start()
    total = from_below(table, px, py, tops, picked, sems)
    for copy in copies:
        copy.wait()
    return ends[0] + TIME_STEP * (total + ends[1] * total)


def below_kernel(table, px, py, field, speed, *refs):
    tops, (out, *scratch) = refs[:10], refs[-4:]
    out[...] = below_value(table, px, py, field, speed, tops, *scratch)


BELOW_SCRATCH = [
    pltpu.VMEM((4, W, W), F32),
    pltpu.VMEM((2, W, W), F32),
    pltpu.SemaphoreType.DMA((7,)),
]


def below_update(table, px, py, field, speed, tops, *earlier):
    return pl.pallas_call(
        below_kernel,
        out_shape=planes(),
        in_specs=[SMEM_SPEC] + [VMEM_SPEC] * 2 + [ANY_SPEC] * (12 + len(earlier)),
        out_specs=VMEM_SPEC,
        scratch_shapes=BELOW_SCRATCH,
        compiler_params=pltpu.CompilerParams(vmem_limit_bytes=50 * MIB),
        cost_estimate=SMALL,
        name="below",
    )(table, px, py, field, speed, *tops, *earlier)


def fix_bottom_kernel(table, px, py, speed, *refs):
    tops, (field, out, picked, ends, sems) = refs[:10], refs[10:]
    ends[0] = below_value(table, px, py, field, speed, tops, picked, ends, sems)
    copy = pltpu.make_async_copy(ends.at[0], out.at[0], sems.at[6])
    copy.start()
    copy.wait()


def fix_bottom(table, px, py, speed, tops, field):
    return pl.pallas_call(
        fix_bottom_kernel,
        out_shape=planes(NZ),
        in_specs=[SMEM_SPEC] + [VMEM_SPEC] * 2 + [ANY_SPEC] * 11 + [pl.BlockSpec(memory_space=pltpu.HBM)],
        out_specs=pl.BlockSpec(memory_space=pltpu.HBM),
        scratch_shapes=BELOW_SCRATCH,
        input_output_aliases={14: 0},
        compiler_params=pltpu.CompilerParams(vmem_limit_bytes=50 * MIB),
        cost_estimate=SMALL,
        name="fix_bottom",
    )(table, px, py, speed, *tops, field)


def fix_top_kernel(table, ghost, field, out, plane, sems):
    fetch = pltpu.make_async_copy(field.at[NZ - 1], plane, sems.at[0])
    fetch.start()
    fetch.wait()
    plane[...] = plane[...] + TIME_STEP * jnp.where(table[6] == 1, AMBIENT, ghost[...])
    store = pltpu.make_async_copy(plane, out.at[NZ - 1], sems.at[1])
    store.start()
    store.wait()


def fix_top(table, ghost, field):
    return pl.pallas_call(
        fix_top_kernel,
        out_shape=planes(NZ),
        in_specs=[SMEM_SPEC, VMEM_SPEC, pl.BlockSpec(memory_space=pltpu.HBM)],
        out_specs=pl.BlockSpec(memory_space=pltpu.HBM),
        scratch_shapes=[pltpu.VMEM((W, W), F32), pltpu.SemaphoreType.DMA((2,))],
        input_output_aliases={2: 0},
        compiler_params=pltpu.CompilerParams(vmem_limit_bytes=8 * MIB),
        cost_estimate=SMALL,
        name="fix_top",
    )(table, ghost, field)


def rims_kernel(field, bottom, top, *refs):
    row_low, row_high, col_low, col_high = refs[-4:]
    lane = lax.broadcasted_iota(jnp.int32, (W, 128), 1)
    low = jnp.zeros((W, 128), F32)
    high = jnp.zeros((W, 128), F32)
    for z in range(NZ):
        ref = bottom if z == 0 else top if z == NZ - 1 else field.at[z]
        row_low[z : z + 1, :] = ref[0:1, :]
        row_high[z : z + 1, :] = ref[W - 1 : W, :]
        low = jnp.where(lane == z, ref[:, 0:1], low)
        high = jnp.where(lane == z, ref[:, W - 1 : W], high)
    col_low[...] = low.T[:NZ]
    col_high[...] = high.T[:NZ]


def rims_of(field, bottom, top, *earlier):
    rim = jax.ShapeDtypeStruct((NZ, W), F32)
    return pl.pallas_call(
        rims_kernel,
        out_shape=(rim,) * 4,
        in_specs=[VMEM_SPEC] * 3 + [ANY_SPEC] * len(earlier),
        out_specs=[VMEM_SPEC] * 4,
        compiler_params=pltpu.CompilerParams(vmem_limit_bytes=16 * MIB),
        cost_estimate=SMALL,
        name="rims",
    )(field, bottom, top, *earlier)


def stencil_kernel(inverse, inside, field, bottom, top, speed, inlets, x_low, x_high, y_low, y_high, *refs):
    out, mark, low, high, fast, sems = refs[-6:]

    def fetch(z):
        return pltpu.make_async_copy(speed.at[z], fast.at[z], sems.at[z])

    for z in range(NZ):
        fetch(z).start()
    mark[...] = jnp.zeros_like(mark)
    pad = jnp.zeros((128 - NZ, W), F32)
    low[...] = jnp.concatenate([jnp.where(inside[2] == 1, y_low[...], 0.0), pad], axis=0).T
    high[...] = jnp.concatenate([jnp.where(inside[3] == 1, y_high[...], 0.0), pad], axis=0).T
    scale = inverse[0]

    def update(z, here, under, over):
        fetch(z).wait()
        pick = lax.broadcasted_iota(jnp.int32, (W, 128), 1) == z
        col_low = jnp.sum(jnp.where(pick, low[...], 0.0), axis=1, keepdims=True)
        col_high = jnp.sum(jnp.where(pick, high[...], 0.0), axis=1, keepdims=True)
        row = lax.broadcasted_iota(jnp.int32, (W, W), 0)
        lane = lax.broadcasted_iota(jnp.int32, (W, W), 1)
        row_low = jnp.where(inside[0] == 1, x_low[pl.ds(z, 1), :], 0.0)
        row_high = jnp.where(inside[1] == 1, x_high[pl.ds(z, 1), :], 0.0)
        beside = jnp.where(row == 0, row_low, pltpu.roll(here, 1, 0))
        beside = beside + jnp.where(row == W - 1, row_high, pltpu.roll(here, W - 1, 0))
        beside = beside + jnp.where(lane == 0, col_low, pltpu.roll(here, 1, 1))
        beside = beside + jnp.where(lane == W - 1, col_high, pltpu.roll(here, W - 1, 1))
        lapl = (beside - 4.0 * here) * scale
        change = lapl + over + under - 2.0 * here - fast[z] * (here - under)
        return here + TIME_STEP * change

    zero = jnp.zeros((W, W), F32)
    first = bottom[...]
    inject = INJECT_RATE * inlets[...].astype(F32)
    out[0] = update(0, first, zero, field[1]) + TIME_STEP * (inject * (1.0 - first))
    out[1] = update(1, field[1], first, field[2])

    def middle(z, carry):
        out[z] = update(z, field[z], field[z - 1], field[z + 1])
        return carry

    lax.fori_loop(2, NZ - 2, middle, 0)
    out[NZ - 2] = update(NZ - 2, field[NZ - 2], field[NZ - 3], top[...])
    out[NZ - 1] = update(NZ - 1, top[...], field[NZ - 2], zero)


def stencil(inverse, inside, field, bottom, top, speed, inlets, halos, *earlier):
    return pl.pallas_call(
        stencil_kernel,
        out_shape=(planes(NZ), MARK),
        in_specs=[SMEM_SPEC] * 2 + [VMEM_SPEC] * 3 + [ANY_SPEC] + [VMEM_SPEC] * 5 + [ANY_SPEC] * len(earlier),
        out_specs=[VMEM_SPEC] * 2,
        scratch_shapes=[pltpu.VMEM((W, 128), F32)] * 2
        + [pltpu.VMEM((NZ, W, W), F32), pltpu.SemaphoreType.DMA((NZ,))],
        compiler_params=pltpu.CompilerParams(vmem_limit_bytes=24 * MIB),
        cost_estimate=SMALL,
        name="stencil",
    )(inverse, inside, field, bottom, top, speed, inlets, *halos, *earlier)


def exchange_rims(rims):
    row_low, row_high, col_low, col_high = rims
    up = [(t, (t + TCOL) % TILES) for t in range(TILES)]
    right = [(t, t - t % TCOL + (t + 1) % TCOL) for t in range(TILES)]
    x_low = lax.ppermute(row_high, "tile", up)
    x_high = lax.ppermute(row_low, "tile", [(d, s) for s, d in up])
    y_low = lax.ppermute(col_high, "tile", right)
    y_high = lax.ppermute(col_low, "tile", [(d, s) for s, d in right])
    return x_low, x_high, y_low, y_high


def climb(plane):
    return send_lift(plane, 1, False), send_lift(plane, 1, True)


def other_core(value):
    return lax.ppermute(value, "tile", OTHER_CORE)


def gather_near(pair):
    return send_y(pair, -1), send_y(pair, 1)


def far_body(right, left, mine, flip):
    mine[...] = left[0]
    flip[...] = right[1]


def gather_far(near, *earlier):
    mine, flip = small_kernel(far_body, "far_planes", (planes(), planes()), near, earlier)
    return send_y(mine, 1), send_y(flip, -1)


def reduce_cores(give, keep, body, *counts, earlier=()):
    taken = lax.ppermute(give, "tile", OTHER_CORE)
    shapes = tuple(planes(count) for count in (*counts, 4))
    return small_kernel(body, "cores_sum", shapes, (keep, taken), earlier)


def reduce_halves(give):
    return lax.ppermute(give, "tile", OTHER_HALF)


def reduce_ring(keep, got, *earlier):
    own, *others = small_kernel(halves_body, "halves_sum", (planes(),) * 4, (keep, *got), earlier)
    return own, *(send_y(part, step) for part, step in zip(others, (1, 2, -1)))


def ghost_sum(parts, *earlier):
    return small_kernel(ghost_body, "ghost_sum", planes(), parts, earlier)


def on_device(oxygen, velocity, spacing, inlets, proj_x, proj_y, sources):
    field = oxygen.reshape(NZ, W, W)
    speed = velocity.reshape(NZ, W, W)
    inlets = inlets.reshape(W, W)
    px = proj_x.reshape(4, W, W)
    py = proj_y.reshape(4, W, W)
    inverse = 1.0 / (spacing * spacing)
    tile = lax.axis_index("tile").astype(jnp.int32)
    lift = lax.axis_index("lift")
    has_below = (lift > 0).astype(jnp.int32)
    is_top = lift == LIFTS - 1
    table = jnp.concatenate([sources.reshape(4) & (TILES - 1), tile[None], has_below[None], is_top[None].astype(jnp.int32)])
    inside = jnp.stack([tile >= TCOL, tile < TILES - TCOL, tile % TCOL > 0, tile % TCOL < TCOL - 1]).astype(jnp.int32)
    bottom, top = field[0], field[NZ - 1]

    mine, flip = climb(top)
    give, keep, mark = pieces_of(table, px, py, bottom)
    halos = exchange_rims(rims_of(field, bottom, top, mark))
    give, keep = reduce_cores(give, keep, whole_cores_body, 4, earlier=halos)
    pair = small_kernel(pair_body, "pair", planes(2), (mine, flip), (give,))
    near = gather_near(pair)
    got = reduce_halves(give)
    field, mark = stencil(inverse, inside, field, bottom, top, speed, inlets, halos)
    far = gather_far(near, mark)
    tops = [pair, *near, *far]
    tops = tops + [other_core(value) for value in tops]
    high = field[NZ - 1]
    mine, flip = climb(high)
    parts = reduce_ring(keep, [got], mark)
    bottom = below_update(table, px, py, field, speed, tops, parts[0])
    give, keep, mark = pieces_of(table, px, py, bottom, mine, flip, parts[1], parts[3])
    give_near, give_far, keep = reduce_cores(give, keep, cores_body, 1, 3)
    ghost = ghost_sum(parts, give_near, mine, flip)
    got_near = reduce_halves(give_near)
    other_ghost = reduce_halves(ghost)
    ghost_above = send_lift(ghost, -1, False)
    earlier = (got_near, ghost_above)
    pair = small_kernel(new_pair_body, "new_pair", planes(2), (mine, flip, ghost, other_ghost), earlier)
    near = gather_near(pair)
    far = gather_far(near)
    tops = [pair, *near, *far]
    tops = tops + [other_core(value) for value in tops]
    top = high + TIME_STEP * jnp.where(is_top, AMBIENT, ghost_above)
    got_far = reduce_halves(give_far)
    halos = exchange_rims(rims_of(field, bottom, top))
    field, mark = stencil(inverse, inside, field, bottom, top, speed, inlets, halos, *far)
    parts = reduce_ring(keep, [got_near, got_far], *halos, *near)
    ghost = send_lift(ghost_sum(parts, mark), -1, False)
    field = fix_bottom(table, px, py, speed, tops, field)
    field = fix_top(table, ghost, field)
    return field.reshape(1, NZ, 1, W, W)


def solution(mesh):
    return jax.shard_map(
        on_device,
        mesh=mesh,
        in_specs=(
            P("lift", None, "tile", None, None),
            P("lift", None, "tile", None, None),
            P("lift"),
            P("lift", "tile", None, None),
            P("lift", "tile", None, None, None),
            P("lift", "tile", None, None, None),
            P("lift", "tile", None),
        ),
        out_specs=P("lift", None, "tile", None, None),
        check_vma=False,
    )
```

```python
import jax
import jax.numpy as jnp
from jax import lax
from jax.experimental import pallas as pl
from jax.experimental.pallas import tpu as pltpu
from jax.sharding import PartitionSpec as P

TCOL = 4
LIFTS = 8
TILES = 16
NZ = 16
W = 256
H = W // 2
TIME_STEP = 0.1
INJECT_RATE = 2.0
AMBIENT = 1.0
F32 = jnp.float32
BF16 = jnp.bfloat16
MIB = 1 << 20


def tile_of(x_half, y, core):
    return x_half * 8 + (y % 4) * 2 + core


def coords(tile):
    return tile // 8, (tile // 2) % 4, tile % 2


def along_y(steps):
    return [(t, tile_of(coords(t)[0], coords(t)[1] + steps, coords(t)[2])) for t in range(TILES)]


OTHER_CORE = [(t, t ^ 1) for t in range(TILES)]
OTHER_HALF = [(t, t ^ 8) for t in range(TILES)]


def to_lift(steps, flip):
    return [
        (lift * TILES + t, (lift + steps) % LIFTS * TILES + (t ^ (8 if flip else 0)))
        for lift in range(LIFTS)
        for t in range(TILES)
    ]


def send_y(value, steps):
    return lax.ppermute(value, "tile", along_y(steps))


def send_lift(value, steps, flip):
    return lax.ppermute(value, ("lift", "tile"), to_lift(steps, flip))


def split(value):
    high = value.astype(BF16)
    return high, (value - high.astype(F32)).astype(BF16)


def product(a, b, dims):
    def one(u, v):
        return lax.dot_general(u, v, (dims, ((), ())), preferred_element_type=F32)

    return one(a[0], b[0]) + (one(a[0], b[1]) + one(a[1], b[0]))


SMEM_SPEC = pl.BlockSpec(memory_space=pltpu.SMEM)
VMEM_SPEC = pl.BlockSpec(memory_space=pltpu.VMEM)


def planes(*count):
    return jax.ShapeDtypeStruct((*count, W, W), F32)


MARK = jax.ShapeDtypeStruct((8, 128), F32)


SMALL = pl.CostEstimate(flops=1024, bytes_accessed=1024, transcendentals=0)


def pieces_kernel(table, px, py, bottom, *refs):
    give, keep, mark = refs[-3:]
    mark[...] = jnp.zeros_like(mark)
    give[...] = jnp.zeros_like(give)
    keep[...] = jnp.zeros_like(keep)
    plane = split(bottom[...])
    for k in range(4):
        left = product(split(px[k]), plane, ((0,), (0,)))
        piece = product(split(left), split(py[k]), ((1,), (0,)))
        source, tile = table[k], table[4]
        x_step = ((source >> 3) ^ (tile >> 3)) & 1
        y_step = ((source >> 1) - (tile >> 1)) & 3
        core_step = (source ^ tile) & 1
        slot = x_step * 4 + y_step

        @pl.when(core_step == 0)
        def _():
            keep[slot] = keep[slot] + piece

        @pl.when(core_step == 1)
        def _():
            give[slot] = give[slot] + piece


ANY_SPEC = pl.BlockSpec(memory_space=pl.ANY)


def pieces_of(table, px, py, bottom, *earlier):
    return pl.pallas_call(
        pieces_kernel,
        out_shape=(planes(8), planes(8), MARK),
        in_specs=[SMEM_SPEC] + [VMEM_SPEC] * 3 + [ANY_SPEC] * len(earlier),
        out_specs=[VMEM_SPEC] * 3,
        compiler_params=pltpu.CompilerParams(vmem_limit_bytes=24 * MIB),
        cost_estimate=SMALL,
        name="pieces",
    )(table, px, py, bottom, *earlier)


def small_kernel(body, name, out_shape, inputs, earlier=()):
    count = len(inputs)

    def kernel(*refs):
        body(*refs[:count], *refs[count + len(earlier) :])

    return pl.pallas_call(
        kernel,
        out_shape=out_shape,
        in_specs=[VMEM_SPEC] * count + [ANY_SPEC] * len(earlier),
        out_specs=jax.tree.map(lambda _: VMEM_SPEC, out_shape),
        compiler_params=pltpu.CompilerParams(vmem_limit_bytes=16 * MIB),
        cost_estimate=SMALL,
        name=name,
    )(*inputs, *earlier)


def pair_body(mine, flip, out):
    out[0] = mine[...]
    out[1] = flip[...]


def new_pair_body(mine, flip, ghost, other, out):
    out[0] = mine[...] + TIME_STEP * ghost[...]
    out[1] = flip[...] + TIME_STEP * other[...]


def cores_body(keep, taken, give_near, give_far, keep_half):
    keep_half[...] = keep[0:4] + taken[0:4]
    give_near[...] = keep[4:5] + taken[4:5]
    give_far[...] = keep[5:8] + taken[5:8]


def whole_cores_body(keep, taken, give_half, keep_half):
    keep_half[...] = keep[0:4] + taken[0:4]
    give_half[...] = keep[4:8] + taken[4:8]


def halves_body(keep, *refs):
    outs = refs[-4:]
    got = [ref.at[i] for ref in refs[:-4] for i in range(ref.shape[0])]
    for i in range(4):
        outs[i][...] = keep[i] + got[i][...]


def ghost_body(own, a, b, c, out):
    out[...] = own[...] + (a[...] + b[...] + c[...])


def from_below(table, px, py, tops, picked, sems):
    def place(k):
        source, tile = table[k], table[4]
        x_step = ((source >> 3) ^ (tile >> 3)) & 1
        y_step = ((source >> 1) - (tile >> 1)) & 3
        return (source ^ tile) & 1, y_step, x_step

    def fetch(plane, k):
        return pltpu.make_async_copy(plane, picked.at[k], sems.at[k])

    for k in range(4):
        core_step, y_step, x_step = place(k)
        for core in range(2):
            pair, right, left, *far = tops[5 * core : 5 * core + 5]
            for step, near in ((0, pair), (1, right), (3, left)):

                @pl.when((core_step == core) & (y_step == step))
                def _():
                    fetch(near.at[x_step], k).start()

            for half in range(2):

                @pl.when((core_step == core) & (y_step == 2) & (x_step == half))
                def _():
                    fetch(far[half], k).start()

    total = jnp.zeros((W, W), F32)
    for k in range(4):
        fetch(tops[3], k).wait()
        left = product(split(px[k]), split(picked[k]), ((1,), (0,)))
        total = total + product(split(left), split(py[k]), ((1,), (1,)))
    return jnp.where(table[5] == 1, total, 0.0)


def ends_copies(field, speed, ends, sems):
    return [
        pltpu.make_async_copy(field.at[0], ends.at[0], sems.at[4]),
        pltpu.make_async_copy(speed.at[0], ends.at[1], sems.at[5]),
    ]


def below_value(table, px, py, field, speed, tops, picked, ends, sems):
    copies = ends_copies(field, speed, ends, sems)
    for copy in copies:
        copy.start()
    total = from_below(table, px, py, tops, picked, sems)
    for copy in copies:
        copy.wait()
    return ends[0] + TIME_STEP * (total + ends[1] * total)


def below_kernel(table, px, py, field, speed, *refs):
    tops, (out, *scratch) = refs[:10], refs[-4:]
    out[...] = below_value(table, px, py, field, speed, tops, *scratch)


BELOW_SCRATCH = [
    pltpu.VMEM((4, W, W), F32),
    pltpu.VMEM((2, W, W), F32),
    pltpu.SemaphoreType.DMA((7,)),
]


def below_update(table, px, py, field, speed, tops, *earlier):
    return pl.pallas_call(
        below_kernel,
        out_shape=planes(),
        in_specs=[SMEM_SPEC] + [VMEM_SPEC] * 2 + [ANY_SPEC] * (12 + len(earlier)),
        out_specs=VMEM_SPEC,
        scratch_shapes=BELOW_SCRATCH,
        compiler_params=pltpu.CompilerParams(vmem_limit_bytes=50 * MIB),
        cost_estimate=SMALL,
        name="below",
    )(table, px, py, field, speed, *tops, *earlier)


def fix_bottom_kernel(table, px, py, speed, *refs):
    tops, (field, out, picked, ends, sems) = refs[:10], refs[10:]
    ends[0] = below_value(table, px, py, field, speed, tops, picked, ends, sems)
    copy = pltpu.make_async_copy(ends.at[0], out.at[0], sems.at[6])
    copy.start()
    copy.wait()


def fix_bottom(table, px, py, speed, tops, field):
    return pl.pallas_call(
        fix_bottom_kernel,
        out_shape=planes(NZ),
        in_specs=[SMEM_SPEC] + [VMEM_SPEC] * 2 + [ANY_SPEC] * 11 + [pl.BlockSpec(memory_space=pltpu.HBM)],
        out_specs=pl.BlockSpec(memory_space=pltpu.HBM),
        scratch_shapes=BELOW_SCRATCH,
        input_output_aliases={14: 0},
        compiler_params=pltpu.CompilerParams(vmem_limit_bytes=50 * MIB),
        cost_estimate=SMALL,
        name="fix_bottom",
    )(table, px, py, speed, *tops, field)


def fix_top_kernel(table, ghost, field, out, plane, sems):
    fetch = pltpu.make_async_copy(field.at[NZ - 1], plane, sems.at[0])
    fetch.start()
    fetch.wait()
    plane[...] = plane[...] + TIME_STEP * jnp.where(table[6] == 1, AMBIENT, ghost[...])
    store = pltpu.make_async_copy(plane, out.at[NZ - 1], sems.at[1])
    store.start()
    store.wait()


def fix_top(table, ghost, field):
    return pl.pallas_call(
        fix_top_kernel,
        out_shape=planes(NZ),
        in_specs=[SMEM_SPEC, VMEM_SPEC, pl.BlockSpec(memory_space=pltpu.HBM)],
        out_specs=pl.BlockSpec(memory_space=pltpu.HBM),
        scratch_shapes=[pltpu.VMEM((W, W), F32), pltpu.SemaphoreType.DMA((2,))],
        input_output_aliases={2: 0},
        compiler_params=pltpu.CompilerParams(vmem_limit_bytes=8 * MIB),
        cost_estimate=SMALL,
        name="fix_top",
    )(table, ghost, field)


def rims_kernel(field, bottom, top, *refs):
    row_low, row_high, col_low, col_high = refs[-4:]
    lane = lax.broadcasted_iota(jnp.int32, (W, 128), 1)
    low = jnp.zeros((W, 128), F32)
    high = jnp.zeros((W, 128), F32)
    for z in range(NZ):
        ref = bottom if z == 0 else top if z == NZ - 1 else field.at[z]
        row_low[z : z + 1, :] = ref[0:1, :]
        row_high[z : z + 1, :] = ref[W - 1 : W, :]
        low = jnp.where(lane == z, ref[:, 0:1], low)
        high = jnp.where(lane == z, ref[:, W - 1 : W], high)
    col_low[...] = low.T[:NZ]
    col_high[...] = high.T[:NZ]


def rims_of(field, bottom, top, *earlier):
    rim = jax.ShapeDtypeStruct((NZ, W), F32)
    return pl.pallas_call(
        rims_kernel,
        out_shape=(rim,) * 4,
        in_specs=[VMEM_SPEC] * 3 + [ANY_SPEC] * len(earlier),
        out_specs=[VMEM_SPEC] * 4,
        compiler_params=pltpu.CompilerParams(vmem_limit_bytes=16 * MIB),
        cost_estimate=SMALL,
        name="rims",
    )(field, bottom, top, *earlier)


def stencil_kernel(inverse, inside, field, bottom, top, speed, inlets, x_low, x_high, y_low, y_high, *refs):
    out, mark, low, high, fast, sems = refs[-6:]

    def fetch(z):
        return pltpu.make_async_copy(speed.at[z], fast.at[z], sems.at[z])

    for z in range(NZ):
        fetch(z).start()
    mark[...] = jnp.zeros_like(mark)
    pad = jnp.zeros((128 - NZ, W), F32)
    low[...] = jnp.concatenate([jnp.where(inside[2] == 1, y_low[...], 0.0), pad], axis=0).T
    high[...] = jnp.concatenate([jnp.where(inside[3] == 1, y_high[...], 0.0), pad], axis=0).T
    scale = inverse[0]

    def update(z, here, under, over):
        fetch(z).wait()
        pick = lax.broadcasted_iota(jnp.int32, (W, 128), 1) == z
        col_low = jnp.sum(jnp.where(pick, low[...], 0.0), axis=1, keepdims=True)
        col_high = jnp.sum(jnp.where(pick, high[...], 0.0), axis=1, keepdims=True)
        row = lax.broadcasted_iota(jnp.int32, (W, W), 0)
        lane = lax.broadcasted_iota(jnp.int32, (W, W), 1)
        row_low = jnp.where(inside[0] == 1, x_low[pl.ds(z, 1), :], 0.0)
        row_high = jnp.where(inside[1] == 1, x_high[pl.ds(z, 1), :], 0.0)
        beside = jnp.where(row == 0, row_low, pltpu.roll(here, 1, 0))
        beside = beside + jnp.where(row == W - 1, row_high, pltpu.roll(here, W - 1, 0))
        beside = beside + jnp.where(lane == 0, col_low, pltpu.roll(here, 1, 1))
        beside = beside + jnp.where(lane == W - 1, col_high, pltpu.roll(here, W - 1, 1))
        lapl = (beside - 4.0 * here) * scale
        change = lapl + over + under - 2.0 * here - fast[z] * (here - under)
        return here + TIME_STEP * change

    zero = jnp.zeros((W, W), F32)
    first = bottom[...]
    inject = INJECT_RATE * inlets[...].astype(F32)
    out[0] = update(0, first, zero, field[1]) + TIME_STEP * (inject * (1.0 - first))
    out[1] = update(1, field[1], first, field[2])

    def middle(z, carry):
        out[z] = update(z, field[z], field[z - 1], field[z + 1])
        return carry

    lax.fori_loop(2, NZ - 2, middle, 0)
    out[NZ - 2] = update(NZ - 2, field[NZ - 2], field[NZ - 3], top[...])
    out[NZ - 1] = update(NZ - 1, top[...], field[NZ - 2], zero)


def stencil(inverse, inside, field, bottom, top, speed, inlets, halos, *earlier):
    return pl.pallas_call(
        stencil_kernel,
        out_shape=(planes(NZ), MARK),
        in_specs=[SMEM_SPEC] * 2 + [VMEM_SPEC] * 3 + [ANY_SPEC] + [VMEM_SPEC] * 5 + [ANY_SPEC] * len(earlier),
        out_specs=[VMEM_SPEC] * 2,
        scratch_shapes=[pltpu.VMEM((W, 128), F32)] * 2
        + [pltpu.VMEM((NZ, W, W), F32), pltpu.SemaphoreType.DMA((NZ,))],
        compiler_params=pltpu.CompilerParams(vmem_limit_bytes=24 * MIB),
        cost_estimate=SMALL,
        name="stencil",
    )(inverse, inside, field, bottom, top, speed, inlets, *halos, *earlier)


def exchange_rims(rims):
    row_low, row_high, col_low, col_high = rims
    up = [(t, (t + TCOL) % TILES) for t in range(TILES)]
    right = [(t, t - t % TCOL + (t + 1) % TCOL) for t in range(TILES)]
    x_low = lax.ppermute(row_high, "tile", up)
    x_high = lax.ppermute(row_low, "tile", [(d, s) for s, d in up])
    y_low = lax.ppermute(col_high, "tile", right)
    y_high = lax.ppermute(col_low, "tile", [(d, s) for s, d in right])
    return x_low, x_high, y_low, y_high


def climb(plane):
    return send_lift(plane, 1, False), send_lift(plane, 1, True)


def other_core(value):
    return lax.ppermute(value, "tile", OTHER_CORE)


def gather_near(pair):
    return send_y(pair, -1), send_y(pair, 1)


def far_body(right, left, mine, flip):
    mine[...] = left[0]
    flip[...] = right[1]


def gather_far(near, *earlier):
    mine, flip = small_kernel(far_body, "far_planes", (planes(), planes()), near, earlier)
    return send_y(mine, 1), send_y(flip, -1)


def reduce_cores(give, keep, body, *counts, earlier=()):
    taken = lax.ppermute(give, "tile", OTHER_CORE)
    shapes = tuple(planes(count) for count in (*counts, 4))
    return small_kernel(body, "cores_sum", shapes, (keep, taken), earlier)


def reduce_halves(give):
    return lax.ppermute(give, "tile", OTHER_HALF)


def reduce_ring(keep, got, *earlier):
    own, *others = small_kernel(halves_body, "halves_sum", (planes(),) * 4, (keep, *got), earlier)
    return own, *(send_y(part, step) for part, step in zip(others, (1, 2, -1)))


def ghost_sum(parts, *earlier):
    return small_kernel(ghost_body, "ghost_sum", planes(), parts, earlier)


def on_device(oxygen, velocity, spacing, inlets, proj_x, proj_y, sources):
    field = oxygen.reshape(NZ, W, W)
    speed = velocity.reshape(NZ, W, W)
    inlets = inlets.reshape(W, W)
    px = proj_x.reshape(4, W, W)
    py = proj_y.reshape(4, W, W)
    inverse = 1.0 / (spacing * spacing)
    tile = lax.axis_index("tile").astype(jnp.int32)
    lift = lax.axis_index("lift")
    has_below = (lift > 0).astype(jnp.int32)
    is_top = lift == LIFTS - 1
    table = jnp.concatenate([sources.reshape(4) & (TILES - 1), tile[None], has_below[None], is_top[None].astype(jnp.int32)])
    inside = jnp.stack([tile >= TCOL, tile < TILES - TCOL, tile % TCOL > 0, tile % TCOL < TCOL - 1]).astype(jnp.int32)
    bottom, top = field[0], field[NZ - 1]

    mine, flip = climb(top)
    give, keep, mark = pieces_of(table, px, py, bottom)
    halos = exchange_rims(rims_of(field, bottom, top, mark))
    give, keep = reduce_cores(give, keep, whole_cores_body, 4, earlier=(mine, flip, *halos))
    pair = small_kernel(pair_body, "pair", planes(2), (mine, flip), (give,))
    near = gather_near(pair)
    got = reduce_halves(give)
    field, mark = stencil(inverse, inside, field, bottom, top, speed, inlets, halos)
    far = gather_far(near, mark)
    tops = [pair, *near, *far]
    tops = tops + [other_core(value) for value in tops]
    high = field[NZ - 1]
    mine, flip = climb(high)
    parts = reduce_ring(keep, [got], mark)
    bottom = below_update(table, px, py, field, speed, tops, parts[0])
    give, keep, mark = pieces_of(table, px, py, bottom, mine, flip, parts[1], parts[3])
    give_near, give_far, keep = reduce_cores(give, keep, cores_body, 1, 3)
    ghost = ghost_sum(parts, give_near, mine, flip)
    got_near = reduce_halves(give_near)
    other_ghost = reduce_halves(ghost)
    ghost_above = send_lift(ghost, -1, False)
    earlier = (got_near, ghost_above)
    pair = small_kernel(new_pair_body, "new_pair", planes(2), (mine, flip, ghost, other_ghost), earlier)
    near = gather_near(pair)
    top = high + TIME_STEP * jnp.where(is_top, AMBIENT, ghost_above)
    got_far = reduce_halves(give_far)
    halos = exchange_rims(rims_of(field, bottom, top))
    field, mark = stencil(inverse, inside, field, bottom, top, speed, inlets, halos)
    parts = reduce_ring(keep, [got_near, got_far], *halos, *near)
    far = gather_far(near, mark)
    tops = [pair, *near, *far]
    tops = tops + [other_core(value) for value in tops]
    ghost = send_lift(ghost_sum(parts, mark), -1, False)
    field = fix_bottom(table, px, py, speed, tops, field)
    field = fix_top(table, ghost, field)
    return field.reshape(1, NZ, 1, W, W)


def solution(mesh):
    return jax.shard_map(
        on_device,
        mesh=mesh,
        in_specs=(
            P("lift", None, "tile", None, None),
            P("lift", None, "tile", None, None),
            P("lift"),
            P("lift", "tile", None, None),
            P("lift", "tile", None, None, None),
            P("lift", "tile", None, None, None),
            P("lift", "tile", None),
        ),
        out_specs=P("lift", None, "tile", None, None),
        check_vma=False,
    )
```

```python
import jax
import jax.numpy as jnp
from jax import lax
from jax.experimental import pallas as pl
from jax.experimental.pallas import tpu as pltpu
from jax.sharding import PartitionSpec as P

TCOL = 4
LIFTS = 8
TILES = 16
NZ = 16
W = 256
H = W // 2
TIME_STEP = 0.1
INJECT_RATE = 2.0
AMBIENT = 1.0
F32 = jnp.float32
BF16 = jnp.bfloat16
MIB = 1 << 20


def tile_of(x_half, y, core):
    return x_half * 8 + (y % 4) * 2 + core


def coords(tile):
    return tile // 8, (tile // 2) % 4, tile % 2


def along_y(steps):
    return [(t, tile_of(coords(t)[0], coords(t)[1] + steps, coords(t)[2])) for t in range(TILES)]


OTHER_CORE = [(t, t ^ 1) for t in range(TILES)]
OTHER_HALF = [(t, t ^ 8) for t in range(TILES)]


def to_lift(steps, flip):
    return [
        (lift * TILES + t, (lift + steps) % LIFTS * TILES + (t ^ (8 if flip else 0)))
        for lift in range(LIFTS)
        for t in range(TILES)
    ]


def send_y(value, steps):
    return lax.ppermute(value, "tile", along_y(steps))


def send_lift(value, steps, flip):
    return lax.ppermute(value, ("lift", "tile"), to_lift(steps, flip))


def split(value):
    high = value.astype(BF16)
    return high, (value - high.astype(F32)).astype(BF16)


def product(a, b, dims):
    def one(u, v):
        return lax.dot_general(u, v, (dims, ((), ())), preferred_element_type=F32)

    return one(a[0], b[0]) + (one(a[0], b[1]) + one(a[1], b[0]))


SMEM_SPEC = pl.BlockSpec(memory_space=pltpu.SMEM)
VMEM_SPEC = pl.BlockSpec(memory_space=pltpu.VMEM)


def planes(*count):
    return jax.ShapeDtypeStruct((*count, W, W), F32)


MARK = jax.ShapeDtypeStruct((8, 128), F32)


SMALL = pl.CostEstimate(flops=1024, bytes_accessed=1024, transcendentals=0)


def pieces_kernel(table, px, py, bottom, *refs):
    give, keep, mark = refs[-3:]
    mark[...] = jnp.zeros_like(mark)
    give[...] = jnp.zeros_like(give)
    keep[...] = jnp.zeros_like(keep)
    plane = split(bottom[...])
    for k in range(4):
        left = product(split(px[k]), plane, ((0,), (0,)))
        piece = product(split(left), split(py[k]), ((1,), (0,)))
        source, tile = table[k], table[4]
        x_step = ((source >> 3) ^ (tile >> 3)) & 1
        y_step = ((source >> 1) - (tile >> 1)) & 3
        core_step = (source ^ tile) & 1
        slot = x_step * 4 + y_step

        @pl.when(core_step == 0)
        def _():
            keep[slot] = keep[slot] + piece

        @pl.when(core_step == 1)
        def _():
            give[slot] = give[slot] + piece


ANY_SPEC = pl.BlockSpec(memory_space=pl.ANY)


def pieces_of(table, px, py, bottom, *earlier):
    return pl.pallas_call(
        pieces_kernel,
        out_shape=(planes(8), planes(8), MARK),
        in_specs=[SMEM_SPEC] + [VMEM_SPEC] * 3 + [ANY_SPEC] * len(earlier),
        out_specs=[VMEM_SPEC] * 3,
        compiler_params=pltpu.CompilerParams(vmem_limit_bytes=24 * MIB),
        cost_estimate=SMALL,
        name="pieces",
    )(table, px, py, bottom, *earlier)


def small_kernel(body, name, out_shape, inputs, earlier=()):
    count = len(inputs)

    def kernel(*refs):
        body(*refs[:count], *refs[count + len(earlier) :])

    return pl.pallas_call(
        kernel,
        out_shape=out_shape,
        in_specs=[VMEM_SPEC] * count + [ANY_SPEC] * len(earlier),
        out_specs=jax.tree.map(lambda _: VMEM_SPEC, out_shape),
        compiler_params=pltpu.CompilerParams(vmem_limit_bytes=16 * MIB),
        cost_estimate=SMALL,
        name=name,
    )(*inputs, *earlier)


def pair_body(mine, flip, out):
    out[0] = mine[...]
    out[1] = flip[...]


def new_pair_body(mine, flip, ghost, other, out):
    out[0] = mine[...] + TIME_STEP * ghost[...]
    out[1] = flip[...] + TIME_STEP * other[...]


def cores_body(keep, taken, give_near, give_far, keep_half):
    keep_half[...] = keep[0:4] + taken[0:4]
    give_near[...] = keep[4:5] + taken[4:5]
    give_far[...] = keep[5:8] + taken[5:8]


def whole_cores_body(keep, taken, give_half, keep_half):
    keep_half[...] = keep[0:4] + taken[0:4]
    give_half[...] = keep[4:8] + taken[4:8]


def halves_body(keep, *refs):
    outs = refs[-4:]
    got = [ref.at[i] for ref in refs[:-4] for i in range(ref.shape[0])]
    for i in range(4):
        outs[i][...] = keep[i] + got[i][...]


def ghost_body(own, a, b, c, out):
    out[...] = own[...] + (a[...] + b[...] + c[...])


def from_below(table, px, py, tops, picked, sems):
    def place(k):
        source, tile = table[k], table[4]
        x_step = ((source >> 3) ^ (tile >> 3)) & 1
        y_step = ((source >> 1) - (tile >> 1)) & 3
        return (source ^ tile) & 1, y_step, x_step

    def fetch(plane, k):
        return pltpu.make_async_copy(plane, picked.at[k], sems.at[k])

    for k in range(4):
        core_step, y_step, x_step = place(k)
        for core in range(2):
            pair, right, left, *far = tops[5 * core : 5 * core + 5]
            for step, near in ((0, pair), (1, right), (3, left)):

                @pl.when((core_step == core) & (y_step == step))
                def _():
                    fetch(near.at[x_step], k).start()

            for half in range(2):

                @pl.when((core_step == core) & (y_step == 2) & (x_step == half))
                def _():
                    fetch(far[half], k).start()

    total = jnp.zeros((W, W), F32)
    for k in range(4):
        fetch(tops[3], k).wait()
        left = product(split(px[k]), split(picked[k]), ((1,), (0,)))
        total = total + product(split(left), split(py[k]), ((1,), (1,)))
    return jnp.where(table[5] == 1, total, 0.0)


def ends_copies(field, speed, ends, sems):
    return [
        pltpu.make_async_copy(field.at[0], ends.at[0], sems.at[4]),
        pltpu.make_async_copy(speed.at[0], ends.at[1], sems.at[5]),
    ]


def below_value(table, px, py, field, speed, tops, picked, ends, sems):
    copies = ends_copies(field, speed, ends, sems)
    for copy in copies:
        copy.start()
    total = from_below(table, px, py, tops, picked, sems)
    for copy in copies:
        copy.wait()
    return ends[0] + TIME_STEP * (total + ends[1] * total)


def below_kernel(table, px, py, field, speed, *refs):
    tops, (out, *scratch) = refs[:10], refs[-4:]
    out[...] = below_value(table, px, py, field, speed, tops, *scratch)


BELOW_SCRATCH = [
    pltpu.VMEM((4, W, W), F32),
    pltpu.VMEM((2, W, W), F32),
    pltpu.SemaphoreType.DMA((7,)),
]


def below_update(table, px, py, field, speed, tops, *earlier):
    return pl.pallas_call(
        below_kernel,
        out_shape=planes(),
        in_specs=[SMEM_SPEC] + [VMEM_SPEC] * 2 + [ANY_SPEC] * (12 + len(earlier)),
        out_specs=VMEM_SPEC,
        scratch_shapes=BELOW_SCRATCH,
        compiler_params=pltpu.CompilerParams(vmem_limit_bytes=50 * MIB),
        cost_estimate=SMALL,
        name="below",
    )(table, px, py, field, speed, *tops, *earlier)


def fix_bottom_kernel(table, px, py, speed, *refs):
    tops, (field, out, picked, ends, sems) = refs[:10], refs[10:]
    ends[0] = below_value(table, px, py, field, speed, tops, picked, ends, sems)
    copy = pltpu.make_async_copy(ends.at[0], out.at[0], sems.at[6])
    copy.start()
    copy.wait()


def fix_bottom(table, px, py, speed, tops, field):
    return pl.pallas_call(
        fix_bottom_kernel,
        out_shape=planes(NZ),
        in_specs=[SMEM_SPEC] + [VMEM_SPEC] * 2 + [ANY_SPEC] * 11 + [pl.BlockSpec(memory_space=pltpu.HBM)],
        out_specs=pl.BlockSpec(memory_space=pltpu.HBM),
        scratch_shapes=BELOW_SCRATCH,
        input_output_aliases={14: 0},
        compiler_params=pltpu.CompilerParams(vmem_limit_bytes=50 * MIB),
        cost_estimate=SMALL,
        name="fix_bottom",
    )(table, px, py, speed, *tops, field)


def fix_top_kernel(table, ghost, field, out, plane, sems):
    fetch = pltpu.make_async_copy(field.at[NZ - 1], plane, sems.at[0])
    fetch.start()
    fetch.wait()
    plane[...] = plane[...] + TIME_STEP * jnp.where(table[6] == 1, AMBIENT, ghost[...])
    store = pltpu.make_async_copy(plane, out.at[NZ - 1], sems.at[1])
    store.start()
    store.wait()


def fix_top(table, ghost, field):
    return pl.pallas_call(
        fix_top_kernel,
        out_shape=planes(NZ),
        in_specs=[SMEM_SPEC, VMEM_SPEC, pl.BlockSpec(memory_space=pltpu.HBM)],
        out_specs=pl.BlockSpec(memory_space=pltpu.HBM),
        scratch_shapes=[pltpu.VMEM((W, W), F32), pltpu.SemaphoreType.DMA((2,))],
        input_output_aliases={2: 0},
        compiler_params=pltpu.CompilerParams(vmem_limit_bytes=8 * MIB),
        cost_estimate=SMALL,
        name="fix_top",
    )(table, ghost, field)


def rims_kernel(field, bottom, top, *refs):
    row_low, row_high, col_low, col_high = refs[-4:]
    lane = lax.broadcasted_iota(jnp.int32, (W, 128), 1)
    low = jnp.zeros((W, 128), F32)
    high = jnp.zeros((W, 128), F32)
    for z in range(NZ):
        ref = bottom if z == 0 else top if z == NZ - 1 else field.at[z]
        row_low[z : z + 1, :] = ref[0:1, :]
        row_high[z : z + 1, :] = ref[W - 1 : W, :]
        low = jnp.where(lane == z, ref[:, 0:1], low)
        high = jnp.where(lane == z, ref[:, W - 1 : W], high)
    col_low[...] = low.T[:NZ]
    col_high[...] = high.T[:NZ]


def rims_of(field, bottom, top, *earlier):
    rim = jax.ShapeDtypeStruct((NZ, W), F32)
    return pl.pallas_call(
        rims_kernel,
        out_shape=(rim,) * 4,
        in_specs=[VMEM_SPEC] * 3 + [ANY_SPEC] * len(earlier),
        out_specs=[VMEM_SPEC] * 4,
        compiler_params=pltpu.CompilerParams(vmem_limit_bytes=16 * MIB),
        cost_estimate=SMALL,
        name="rims",
    )(field, bottom, top, *earlier)


def stencil_kernel(inverse, inside, field, bottom, top, speed, inlets, x_low, x_high, y_low, y_high, *refs):
    out, mark, low, high, fast, sems = refs[-6:]

    def fetch(z):
        return pltpu.make_async_copy(speed.at[z], fast.at[z], sems.at[z])

    for z in range(NZ):
        fetch(z).start()
    mark[...] = jnp.zeros_like(mark)
    pad = jnp.zeros((128 - NZ, W), F32)
    low[...] = jnp.concatenate([jnp.where(inside[2] == 1, y_low[...], 0.0), pad], axis=0).T
    high[...] = jnp.concatenate([jnp.where(inside[3] == 1, y_high[...], 0.0), pad], axis=0).T
    scale = inverse[0]

    def update(z, here, under, over):
        fetch(z).wait()
        pick = lax.broadcasted_iota(jnp.int32, (W, 128), 1) == z
        col_low = jnp.sum(jnp.where(pick, low[...], 0.0), axis=1, keepdims=True)
        col_high = jnp.sum(jnp.where(pick, high[...], 0.0), axis=1, keepdims=True)
        row = lax.broadcasted_iota(jnp.int32, (W, W), 0)
        lane = lax.broadcasted_iota(jnp.int32, (W, W), 1)
        row_low = jnp.where(inside[0] == 1, x_low[pl.ds(z, 1), :], 0.0)
        row_high = jnp.where(inside[1] == 1, x_high[pl.ds(z, 1), :], 0.0)
        beside = jnp.where(row == 0, row_low, pltpu.roll(here, 1, 0))
        beside = beside + jnp.where(row == W - 1, row_high, pltpu.roll(here, W - 1, 0))
        beside = beside + jnp.where(lane == 0, col_low, pltpu.roll(here, 1, 1))
        beside = beside + jnp.where(lane == W - 1, col_high, pltpu.roll(here, W - 1, 1))
        lapl = (beside - 4.0 * here) * scale
        change = lapl + over + under - 2.0 * here - fast[z] * (here - under)
        return here + TIME_STEP * change

    zero = jnp.zeros((W, W), F32)
    first = bottom[...]
    inject = INJECT_RATE * inlets[...].astype(F32)
    out[0] = update(0, first, zero, field[1]) + TIME_STEP * (inject * (1.0 - first))
    out[1] = update(1, field[1], first, field[2])

    def middle(z, carry):
        out[z] = update(z, field[z], field[z - 1], field[z + 1])
        return carry

    lax.fori_loop(2, NZ - 2, middle, 0)
    out[NZ - 2] = update(NZ - 2, field[NZ - 2], field[NZ - 3], top[...])
    out[NZ - 1] = update(NZ - 1, top[...], field[NZ - 2], zero)


def stencil(inverse, inside, field, bottom, top, speed, inlets, halos, *earlier):
    return pl.pallas_call(
        stencil_kernel,
        out_shape=(planes(NZ), MARK),
        in_specs=[SMEM_SPEC] * 2 + [VMEM_SPEC] * 3 + [ANY_SPEC] + [VMEM_SPEC] * 5 + [ANY_SPEC] * len(earlier),
        out_specs=[VMEM_SPEC] * 2,
        scratch_shapes=[pltpu.VMEM((W, 128), F32)] * 2
        + [pltpu.VMEM((NZ, W, W), F32), pltpu.SemaphoreType.DMA((NZ,))],
        compiler_params=pltpu.CompilerParams(vmem_limit_bytes=24 * MIB),
        cost_estimate=SMALL,
        name="stencil",
    )(inverse, inside, field, bottom, top, speed, inlets, *halos, *earlier)


def exchange_rims(rims):
    row_low, row_high, col_low, col_high = rims
    up = [(t, (t + TCOL) % TILES) for t in range(TILES)]
    right = [(t, t - t % TCOL + (t + 1) % TCOL) for t in range(TILES)]
    x_low = lax.ppermute(row_high, "tile", up)
    x_high = lax.ppermute(row_low, "tile", [(d, s) for s, d in up])
    y_low = lax.ppermute(col_high, "tile", right)
    y_high = lax.ppermute(col_low, "tile", [(d, s) for s, d in right])
    return x_low, x_high, y_low, y_high


def climb(plane):
    return send_lift(plane, 1, False), send_lift(plane, 1, True)


def other_core(value):
    return lax.ppermute(value, "tile", OTHER_CORE)


def gather_near(pair):
    return send_y(pair, -1), send_y(pair, 1)


def far_body(right, left, mine, flip):
    mine[...] = left[0]
    flip[...] = right[1]


def gather_far(near, *earlier):
    mine, flip = small_kernel(far_body, "far_planes", (planes(), planes()), near, earlier)
    return send_y(mine, 1), send_y(flip, -1)


def reduce_cores(give, keep, body, *counts, earlier=()):
    taken = lax.ppermute(give, "tile", OTHER_CORE)
    shapes = tuple(planes(count) for count in (*counts, 4))
    return small_kernel(body, "cores_sum", shapes, (keep, taken), earlier)


def reduce_halves(give):
    return lax.ppermute(give, "tile", OTHER_HALF)


def reduce_ring(keep, got, *earlier):
    own, *others = small_kernel(halves_body, "halves_sum", (planes(),) * 4, (keep, *got), earlier)
    return own, *(send_y(part, step) for part, step in zip(others, (1, 2, -1)))


def ghost_sum(parts, *earlier):
    return small_kernel(ghost_body, "ghost_sum", planes(), parts, earlier)


def on_device(oxygen, velocity, spacing, inlets, proj_x, proj_y, sources):
    field = oxygen.reshape(NZ, W, W)
    speed = velocity.reshape(NZ, W, W)
    inlets = inlets.reshape(W, W)
    px = proj_x.reshape(4, W, W)
    py = proj_y.reshape(4, W, W)
    inverse = 1.0 / (spacing * spacing)
    tile = lax.axis_index("tile").astype(jnp.int32)
    lift = lax.axis_index("lift")
    has_below = (lift > 0).astype(jnp.int32)
    is_top = lift == LIFTS - 1
    table = jnp.concatenate([sources.reshape(4) & (TILES - 1), tile[None], has_below[None], is_top[None].astype(jnp.int32)])
    inside = jnp.stack([tile >= TCOL, tile < TILES - TCOL, tile % TCOL > 0, tile % TCOL < TCOL - 1]).astype(jnp.int32)
    bottom, top = field[0], field[NZ - 1]

    mine, flip = climb(top)
    give, keep, mark = pieces_of(table, px, py, bottom)
    halos = exchange_rims(rims_of(field, bottom, top, mark))
    give, keep = reduce_cores(give, keep, whole_cores_body, 4, earlier=(mine, flip, *halos))
    pair = small_kernel(pair_body, "pair", planes(2), (mine, flip), (give,))
    near = gather_near(pair)
    got = reduce_halves(give)
    field, mark = stencil(inverse, inside, field, bottom, top, speed, inlets, halos)
    far = gather_far(near, mark)
    tops = [pair, *near, *far]
    tops = tops + [other_core(value) for value in tops]
    high = field[NZ - 1]
    mine, flip = climb(high)
    parts = reduce_ring(keep, [got], mark)
    bottom = below_update(table, px, py, field, speed, tops, parts[0])
    give, keep, mark = pieces_of(table, px, py, bottom, mine, flip, parts[1], parts[3])
    give_near, give_far, keep = reduce_cores(give, keep, cores_body, 1, 3)
    ghost = ghost_sum(parts, give_near, mine, flip)
    got_near = reduce_halves(give_near)
    other_ghost = reduce_halves(ghost)
    ghost_above = send_lift(ghost, -1, False)
    earlier = (got_near,)
    pair = small_kernel(new_pair_body, "new_pair", planes(2), (mine, flip, ghost, other_ghost), earlier)
    near = gather_near(pair)
    top = high + TIME_STEP * jnp.where(is_top, AMBIENT, ghost_above)
    got_far = reduce_halves(give_far)
    halos = exchange_rims(rims_of(field, bottom, top))
    field, mark = stencil(inverse, inside, field, bottom, top, speed, inlets, halos)
    parts = reduce_ring(keep, [got_near, got_far], *near)
    far = gather_far(near)
    tops = [pair, *near, *far]
    tops = tops + [other_core(value) for value in tops]
    ghost = send_lift(ghost_sum(parts, mark), -1, False)
    field = fix_bottom(table, px, py, speed, tops, field)
    field = fix_top(table, ghost, field)
    return field.reshape(1, NZ, 1, W, W)


def solution(mesh):
    return jax.shard_map(
        on_device,
        mesh=mesh,
        in_specs=(
            P("lift", None, "tile", None, None),
            P("lift", None, "tile", None, None),
            P("lift"),
            P("lift", "tile", None, None),
            P("lift", "tile", None, None, None),
            P("lift", "tile", None, None, None),
            P("lift", "tile", None),
        ),
        out_specs=P("lift", None, "tile", None, None),
        check_vma=False,
    )
```

```python
import jax
import jax.numpy as jnp
from jax import lax
from jax.experimental import pallas as pl
from jax.experimental.pallas import tpu as pltpu
from jax.sharding import PartitionSpec as P

TCOL = 4
LIFTS = 8
TILES = 16
NZ = 16
W = 256
H = W // 2
TIME_STEP = 0.1
INJECT_RATE = 2.0
AMBIENT = 1.0
F32 = jnp.float32
BF16 = jnp.bfloat16
MIB = 1 << 20


def tile_of(x_half, y, core):
    return x_half * 8 + (y % 4) * 2 + core


def coords(tile):
    return tile // 8, (tile // 2) % 4, tile % 2


def along_y(steps):
    return [(t, tile_of(coords(t)[0], coords(t)[1] + steps, coords(t)[2])) for t in range(TILES)]


OTHER_CORE = [(t, t ^ 1) for t in range(TILES)]
OTHER_HALF = [(t, t ^ 8) for t in range(TILES)]


def to_lift(steps, flip):
    return [
        (lift * TILES + t, (lift + steps) % LIFTS * TILES + (t ^ (8 if flip else 0)))
        for lift in range(LIFTS)
        for t in range(TILES)
    ]


def send_y(value, steps):
    return lax.ppermute(value, "tile", along_y(steps))


def send_lift(value, steps, flip):
    return lax.ppermute(value, ("lift", "tile"), to_lift(steps, flip))


def split(value):
    high = value.astype(BF16)
    return high, (value - high.astype(F32)).astype(BF16)


def product(a, b, dims):
    def one(u, v):
        return lax.dot_general(u, v, (dims, ((), ())), preferred_element_type=F32)

    return one(a[0], b[0]) + (one(a[0], b[1]) + one(a[1], b[0]))


SMEM_SPEC = pl.BlockSpec(memory_space=pltpu.SMEM)
VMEM_SPEC = pl.BlockSpec(memory_space=pltpu.VMEM)


def planes(*count):
    return jax.ShapeDtypeStruct((*count, W, W), F32)


MARK = jax.ShapeDtypeStruct((8, 128), F32)


SMALL = pl.CostEstimate(flops=1024, bytes_accessed=1024, transcendentals=0)


def pieces_kernel(table, px, py, bottom, *refs):
    give, keep, mark = refs[-3:]
    mark[...] = jnp.zeros_like(mark)
    give[...] = jnp.zeros_like(give)
    keep[...] = jnp.zeros_like(keep)
    plane = split(bottom[...])
    for k in range(4):
        left = product(split(px[k]), plane, ((0,), (0,)))
        piece = product(split(left), split(py[k]), ((1,), (0,)))
        source, tile = table[k], table[4]
        x_step = ((source >> 3) ^ (tile >> 3)) & 1
        y_step = ((source >> 1) - (tile >> 1)) & 3
        core_step = (source ^ tile) & 1
        slot = x_step * 4 + y_step

        @pl.when(core_step == 0)
        def _():
            keep[slot] = keep[slot] + piece

        @pl.when(core_step == 1)
        def _():
            give[slot] = give[slot] + piece


ANY_SPEC = pl.BlockSpec(memory_space=pl.ANY)


def pieces_of(table, px, py, bottom, *earlier):
    return pl.pallas_call(
        pieces_kernel,
        out_shape=(planes(8), planes(8), MARK),
        in_specs=[SMEM_SPEC] + [VMEM_SPEC] * 3 + [ANY_SPEC] * len(earlier),
        out_specs=[VMEM_SPEC] * 3,
        compiler_params=pltpu.CompilerParams(vmem_limit_bytes=24 * MIB),
        cost_estimate=SMALL,
        name="pieces",
    )(table, px, py, bottom, *earlier)


def small_kernel(body, name, out_shape, inputs, earlier=()):
    count = len(inputs)

    def kernel(*refs):
        body(*refs[:count], *refs[count + len(earlier) :])

    return pl.pallas_call(
        kernel,
        out_shape=out_shape,
        in_specs=[VMEM_SPEC] * count + [ANY_SPEC] * len(earlier),
        out_specs=jax.tree.map(lambda _: VMEM_SPEC, out_shape),
        compiler_params=pltpu.CompilerParams(vmem_limit_bytes=16 * MIB),
        cost_estimate=SMALL,
        name=name,
    )(*inputs, *earlier)


def pair_body(mine, flip, out):
    out[0] = mine[...]
    out[1] = flip[...]


def new_pair_body(mine, flip, ghost, other, out):
    out[0] = mine[...] + TIME_STEP * ghost[...]
    out[1] = flip[...] + TIME_STEP * other[...]


def cores_body(keep, taken, give_near, give_far, keep_half):
    keep_half[...] = keep[0:4] + taken[0:4]
    give_near[...] = keep[4:5] + taken[4:5]
    give_far[...] = keep[5:8] + taken[5:8]


def whole_cores_body(keep, taken, give_half, keep_half):
    keep_half[...] = keep[0:4] + taken[0:4]
    give_half[...] = keep[4:8] + taken[4:8]


def halves_body(keep, *refs):
    outs = refs[-4:]
    got = [ref.at[i] for ref in refs[:-4] for i in range(ref.shape[0])]
    for i in range(4):
        outs[i][...] = keep[i] + got[i][...]


def ghost_body(own, a, b, c, out):
    out[...] = own[...] + (a[...] + b[...] + c[...])


def from_below(table, px, py, tops, picked, sems):
    def place(k):
        source, tile = table[k], table[4]
        x_step = ((source >> 3) ^ (tile >> 3)) & 1
        y_step = ((source >> 1) - (tile >> 1)) & 3
        return (source ^ tile) & 1, y_step, x_step

    def fetch(plane, k):
        return pltpu.make_async_copy(plane, picked.at[k], sems.at[k])

    for k in range(4):
        core_step, y_step, x_step = place(k)
        for core in range(2):
            pair, right, left, *far = tops[5 * core : 5 * core + 5]
            for step, near in ((0, pair), (1, right), (3, left)):

                @pl.when((core_step == core) & (y_step == step))
                def _():
                    fetch(near.at[x_step], k).start()

            for half in range(2):

                @pl.when((core_step == core) & (y_step == 2) & (x_step == half))
                def _():
                    fetch(far[half], k).start()

    total = jnp.zeros((W, W), F32)
    for k in range(4):
        fetch(tops[3], k).wait()
        left = product(split(px[k]), split(picked[k]), ((1,), (0,)))
        total = total + product(split(left), split(py[k]), ((1,), (1,)))
    return jnp.where(table[5] == 1, total, 0.0)


def ends_copies(field, speed, ends, sems):
    return [
        pltpu.make_async_copy(field.at[0], ends.at[0], sems.at[4]),
        pltpu.make_async_copy(speed.at[0], ends.at[1], sems.at[5]),
    ]


def below_value(table, px, py, field, speed, tops, picked, ends, sems):
    copies = ends_copies(field, speed, ends, sems)
    for copy in copies:
        copy.start()
    total = from_below(table, px, py, tops, picked, sems)
    for copy in copies:
        copy.wait()
    return ends[0] + TIME_STEP * (total + ends[1] * total)


def below_kernel(table, px, py, field, speed, *refs):
    tops, (out, *scratch) = refs[:10], refs[-4:]
    out[...] = below_value(table, px, py, field, speed, tops, *scratch)


BELOW_SCRATCH = [
    pltpu.VMEM((4, W, W), F32),
    pltpu.VMEM((2, W, W), F32),
    pltpu.SemaphoreType.DMA((7,)),
]


def below_update(table, px, py, field, speed, tops, *earlier):
    return pl.pallas_call(
        below_kernel,
        out_shape=planes(),
        in_specs=[SMEM_SPEC] + [VMEM_SPEC] * 2 + [ANY_SPEC] * (12 + len(earlier)),
        out_specs=VMEM_SPEC,
        scratch_shapes=BELOW_SCRATCH,
        compiler_params=pltpu.CompilerParams(vmem_limit_bytes=50 * MIB),
        cost_estimate=SMALL,
        name="below",
    )(table, px, py, field, speed, *tops, *earlier)


def fix_bottom_kernel(table, px, py, speed, *refs):
    tops, (field, out, picked, ends, sems) = refs[:10], refs[10:]
    ends[0] = below_value(table, px, py, field, speed, tops, picked, ends, sems)
    copy = pltpu.make_async_copy(ends.at[0], out.at[0], sems.at[6])
    copy.start()
    copy.wait()


def fix_bottom(table, px, py, speed, tops, field):
    return pl.pallas_call(
        fix_bottom_kernel,
        out_shape=planes(NZ),
        in_specs=[SMEM_SPEC] + [VMEM_SPEC] * 2 + [ANY_SPEC] * 11 + [pl.BlockSpec(memory_space=pltpu.HBM)],
        out_specs=pl.BlockSpec(memory_space=pltpu.HBM),
        scratch_shapes=BELOW_SCRATCH,
        input_output_aliases={14: 0},
        compiler_params=pltpu.CompilerParams(vmem_limit_bytes=50 * MIB),
        cost_estimate=SMALL,
        name="fix_bottom",
    )(table, px, py, speed, *tops, field)


def fix_top_kernel(table, ghost, field, out, plane, sems):
    fetch = pltpu.make_async_copy(field.at[NZ - 1], plane, sems.at[0])
    fetch.start()
    fetch.wait()
    plane[...] = plane[...] + TIME_STEP * jnp.where(table[6] == 1, AMBIENT, ghost[...])
    store = pltpu.make_async_copy(plane, out.at[NZ - 1], sems.at[1])
    store.start()
    store.wait()


def fix_top(table, ghost, field):
    return pl.pallas_call(
        fix_top_kernel,
        out_shape=planes(NZ),
        in_specs=[SMEM_SPEC, VMEM_SPEC, pl.BlockSpec(memory_space=pltpu.HBM)],
        out_specs=pl.BlockSpec(memory_space=pltpu.HBM),
        scratch_shapes=[pltpu.VMEM((W, W), F32), pltpu.SemaphoreType.DMA((2,))],
        input_output_aliases={2: 0},
        compiler_params=pltpu.CompilerParams(vmem_limit_bytes=8 * MIB),
        cost_estimate=SMALL,
        name="fix_top",
    )(table, ghost, field)


def rims_kernel(field, bottom, top, *refs):
    row_low, row_high, col_low, col_high = refs[-4:]
    lane = lax.broadcasted_iota(jnp.int32, (W, 128), 1)
    low = jnp.zeros((W, 128), F32)
    high = jnp.zeros((W, 128), F32)
    for z in range(NZ):
        ref = bottom if z == 0 else top if z == NZ - 1 else field.at[z]
        row_low[z : z + 1, :] = ref[0:1, :]
        row_high[z : z + 1, :] = ref[W - 1 : W, :]
        low = jnp.where(lane == z, ref[:, 0:1], low)
        high = jnp.where(lane == z, ref[:, W - 1 : W], high)
    col_low[...] = low.T[:NZ]
    col_high[...] = high.T[:NZ]


def rims_of(field, bottom, top, *earlier):
    rim = jax.ShapeDtypeStruct((NZ, W), F32)
    return pl.pallas_call(
        rims_kernel,
        out_shape=(rim,) * 4,
        in_specs=[VMEM_SPEC] * 3 + [ANY_SPEC] * len(earlier),
        out_specs=[VMEM_SPEC] * 4,
        compiler_params=pltpu.CompilerParams(vmem_limit_bytes=16 * MIB),
        cost_estimate=SMALL,
        name="rims",
    )(field, bottom, top, *earlier)


def stencil_kernel(inverse, inside, field, bottom, top, speed, inlets, x_low, x_high, y_low, y_high, *refs):
    out, mark, low, high, fast, sems = refs[-6:]

    def fetch(z):
        return pltpu.make_async_copy(speed.at[z], fast.at[z], sems.at[z])

    for z in range(NZ):
        fetch(z).start()
    mark[...] = jnp.zeros_like(mark)
    pad = jnp.zeros((128 - NZ, W), F32)
    low[...] = jnp.concatenate([jnp.where(inside[2] == 1, y_low[...], 0.0), pad], axis=0).T
    high[...] = jnp.concatenate([jnp.where(inside[3] == 1, y_high[...], 0.0), pad], axis=0).T
    scale = inverse[0]

    def update(z, here, under, over):
        fetch(z).wait()
        pick = lax.broadcasted_iota(jnp.int32, (W, 128), 1) == z
        col_low = jnp.sum(jnp.where(pick, low[...], 0.0), axis=1, keepdims=True)
        col_high = jnp.sum(jnp.where(pick, high[...], 0.0), axis=1, keepdims=True)
        row = lax.broadcasted_iota(jnp.int32, (W, W), 0)
        lane = lax.broadcasted_iota(jnp.int32, (W, W), 1)
        row_low = jnp.where(inside[0] == 1, x_low[pl.ds(z, 1), :], 0.0)
        row_high = jnp.where(inside[1] == 1, x_high[pl.ds(z, 1), :], 0.0)
        beside = jnp.where(row == 0, row_low, pltpu.roll(here, 1, 0))
        beside = beside + jnp.where(row == W - 1, row_high, pltpu.roll(here, W - 1, 0))
        beside = beside + jnp.where(lane == 0, col_low, pltpu.roll(here, 1, 1))
        beside = beside + jnp.where(lane == W - 1, col_high, pltpu.roll(here, W - 1, 1))
        lapl = (beside - 4.0 * here) * scale
        change = lapl + over + under - 2.0 * here - fast[z] * (here - under)
        return here + TIME_STEP * change

    zero = jnp.zeros((W, W), F32)
    first = bottom[...]
    inject = INJECT_RATE * inlets[...].astype(F32)
    out[0] = update(0, first, zero, field[1]) + TIME_STEP * (inject * (1.0 - first))
    out[1] = update(1, field[1], first, field[2])

    def middle(z, carry):
        out[z] = update(z, field[z], field[z - 1], field[z + 1])
        return carry

    lax.fori_loop(2, NZ - 2, middle, 0)
    out[NZ - 2] = update(NZ - 2, field[NZ - 2], field[NZ - 3], top[...])
    out[NZ - 1] = update(NZ - 1, top[...], field[NZ - 2], zero)


def stencil(inverse, inside, field, bottom, top, speed, inlets, halos, *earlier):
    return pl.pallas_call(
        stencil_kernel,
        out_shape=(planes(NZ), MARK),
        in_specs=[SMEM_SPEC] * 2 + [VMEM_SPEC] * 3 + [ANY_SPEC] + [VMEM_SPEC] * 5 + [ANY_SPEC] * len(earlier),
        out_specs=[VMEM_SPEC] * 2,
        scratch_shapes=[pltpu.VMEM((W, 128), F32)] * 2
        + [pltpu.VMEM((NZ, W, W), F32), pltpu.SemaphoreType.DMA((NZ,))],
        compiler_params=pltpu.CompilerParams(vmem_limit_bytes=24 * MIB),
        cost_estimate=SMALL,
        name="stencil",
    )(inverse, inside, field, bottom, top, speed, inlets, *halos, *earlier)


def exchange_rims(rims):
    row_low, row_high, col_low, col_high = rims
    up = [(t, (t + TCOL) % TILES) for t in range(TILES)]
    right = [(t, t - t % TCOL + (t + 1) % TCOL) for t in range(TILES)]
    x_low = lax.ppermute(row_high, "tile", up)
    x_high = lax.ppermute(row_low, "tile", [(d, s) for s, d in up])
    y_low = lax.ppermute(col_high, "tile", right)
    y_high = lax.ppermute(col_low, "tile", [(d, s) for s, d in right])
    return x_low, x_high, y_low, y_high


def climb(plane):
    return send_lift(plane, 1, False), send_lift(plane, 1, True)


def other_core(value):
    return lax.ppermute(value, "tile", OTHER_CORE)


def gather_near(pair):
    return send_y(pair, -1), send_y(pair, 1)


def far_body(right, left, mine, flip):
    mine[...] = left[0]
    flip[...] = right[1]


def gather_far(near, *earlier):
    mine, flip = small_kernel(far_body, "far_planes", (planes(), planes()), near, earlier)
    return send_y(mine, 1), send_y(flip, -1)


def reduce_cores(give, keep, body, *counts, earlier=()):
    taken = lax.ppermute(give, "tile", OTHER_CORE)
    shapes = tuple(planes(count) for count in (*counts, 4))
    return small_kernel(body, "cores_sum", shapes, (keep, taken), earlier)


def reduce_halves(give):
    return lax.ppermute(give, "tile", OTHER_HALF)


def reduce_ring(keep, got, *earlier):
    own, *others = small_kernel(halves_body, "halves_sum", (planes(),) * 4, (keep, *got), earlier)
    return own, *(send_y(part, step) for part, step in zip(others, (1, 2, -1)))


def ghost_sum(parts, *earlier):
    return small_kernel(ghost_body, "ghost_sum", planes(), parts, earlier)


def on_device(oxygen, velocity, spacing, inlets, proj_x, proj_y, sources):
    field = oxygen.reshape(NZ, W, W)
    speed = velocity.reshape(NZ, W, W)
    inlets = inlets.reshape(W, W)
    px = proj_x.reshape(4, W, W)
    py = proj_y.reshape(4, W, W)
    inverse = 1.0 / (spacing * spacing)
    tile = lax.axis_index("tile").astype(jnp.int32)
    lift = lax.axis_index("lift")
    has_below = (lift > 0).astype(jnp.int32)
    is_top = lift == LIFTS - 1
    table = jnp.concatenate([sources.reshape(4) & (TILES - 1), tile[None], has_below[None], is_top[None].astype(jnp.int32)])
    inside = jnp.stack([tile >= TCOL, tile < TILES - TCOL, tile % TCOL > 0, tile % TCOL < TCOL - 1]).astype(jnp.int32)
    bottom, top = field[0], field[NZ - 1]

    mine, flip = climb(top)
    give, keep, mark = pieces_of(table, px, py, bottom)
    halos = exchange_rims(rims_of(field, bottom, top, mark))
    give, keep = reduce_cores(give, keep, whole_cores_body, 4, earlier=(mine, flip, *halos[:2]))
    pair = small_kernel(pair_body, "pair", planes(2), (mine, flip), (give, *halos[2:]))
    near = gather_near(pair)
    got = reduce_halves(give)
    field, mark = stencil(inverse, inside, field, bottom, top, speed, inlets, halos)
    far = gather_far(near, mark)
    tops = [pair, *near, *far]
    tops = tops + [other_core(value) for value in tops]
    high = field[NZ - 1]
    mine, flip = climb(high)
    parts = reduce_ring(keep, [got], mark)
    bottom = below_update(table, px, py, field, speed, tops, parts[0])
    give, keep, mark = pieces_of(table, px, py, bottom, mine, flip, parts[1], parts[3])
    give_near, give_far, keep = reduce_cores(give, keep, cores_body, 1, 3)
    ghost = ghost_sum(parts, give_near, mine, flip)
    got_near = reduce_halves(give_near)
    other_ghost = reduce_halves(ghost)
    ghost_above = send_lift(ghost, -1, False)
    earlier = (got_near, ghost_above)
    pair = small_kernel(new_pair_body, "new_pair", planes(2), (mine, flip, ghost, other_ghost), earlier)
    near = gather_near(pair)
    top = high + TIME_STEP * jnp.where(is_top, AMBIENT, ghost_above)
    got_far = reduce_halves(give_far)
    halos = exchange_rims(rims_of(field, bottom, top))
    field, mark = stencil(inverse, inside, field, bottom, top, speed, inlets, halos)
    parts = reduce_ring(keep, [got_near, got_far], *halos, *near)
    far = gather_far(near, mark)
    tops = [pair, *near, *far]
    tops = tops + [other_core(value) for value in tops]
    ghost = send_lift(ghost_sum(parts, mark), -1, False)
    field = fix_bottom(table, px, py, speed, tops, field)
    field = fix_top(table, ghost, field)
    return field.reshape(1, NZ, 1, W, W)


def solution(mesh):
    return jax.shard_map(
        on_device,
        mesh=mesh,
        in_specs=(
            P("lift", None, "tile", None, None),
            P("lift", None, "tile", None, None),
            P("lift"),
            P("lift", "tile", None, None),
            P("lift", "tile", None, None, None),
            P("lift", "tile", None, None, None),
            P("lift", "tile", None),
        ),
        out_specs=P("lift", None, "tile", None, None),
        check_vma=False,
    )
```

```python
import jax
import jax.numpy as jnp
from jax import lax
from jax.experimental import pallas as pl
from jax.experimental.pallas import tpu as pltpu
from jax.sharding import PartitionSpec as P

TCOL = 4
LIFTS = 8
TILES = 16
NZ = 16
W = 256
H = W // 2
TIME_STEP = 0.1
INJECT_RATE = 2.0
AMBIENT = 1.0
F32 = jnp.float32
BF16 = jnp.bfloat16
MIB = 1 << 20


def tile_of(x_half, y, core):
    return x_half * 8 + (y % 4) * 2 + core


def coords(tile):
    return tile // 8, (tile // 2) % 4, tile % 2


def along_y(steps):
    return [(t, tile_of(coords(t)[0], coords(t)[1] + steps, coords(t)[2])) for t in range(TILES)]


OTHER_CORE = [(t, t ^ 1) for t in range(TILES)]
OTHER_HALF = [(t, t ^ 8) for t in range(TILES)]


def to_lift(steps, flip):
    return [
        (lift * TILES + t, (lift + steps) % LIFTS * TILES + (t ^ (8 if flip else 0)))
        for lift in range(LIFTS)
        for t in range(TILES)
    ]


def send_y(value, steps):
    return lax.ppermute(value, "tile", along_y(steps))


def send_lift(value, steps, flip):
    return lax.ppermute(value, ("lift", "tile"), to_lift(steps, flip))


def split(value):
    high = value.astype(BF16)
    return high, (value - high.astype(F32)).astype(BF16)


def product(a, b, dims):
    def one(u, v):
        return lax.dot_general(u, v, (dims, ((), ())), preferred_element_type=F32)

    return one(a[0], b[0]) + (one(a[0], b[1]) + one(a[1], b[0]))


SMEM_SPEC = pl.BlockSpec(memory_space=pltpu.SMEM)
VMEM_SPEC = pl.BlockSpec(memory_space=pltpu.VMEM)


def planes(*count):
    return jax.ShapeDtypeStruct((*count, W, W), F32)


MARK = jax.ShapeDtypeStruct((8, 128), F32)


SMALL = pl.CostEstimate(flops=1024, bytes_accessed=1024, transcendentals=0)


def pieces_kernel(table, px, py, bottom, *refs):
    give, keep, mark = refs[-3:]
    mark[...] = jnp.zeros_like(mark)
    give[...] = jnp.zeros_like(give)
    keep[...] = jnp.zeros_like(keep)
    plane = split(bottom[...])
    for k in range(4):
        left = product(split(px[k]), plane, ((0,), (0,)))
        piece = product(split(left), split(py[k]), ((1,), (0,)))
        source, tile = table[k], table[4]
        x_step = ((source >> 3) ^ (tile >> 3)) & 1
        y_step = ((source >> 1) - (tile >> 1)) & 3
        core_step = (source ^ tile) & 1
        slot = x_step * 4 + y_step

        @pl.when(core_step == 0)
        def _():
            keep[slot] = keep[slot] + piece

        @pl.when(core_step == 1)
        def _():
            give[slot] = give[slot] + piece


ANY_SPEC = pl.BlockSpec(memory_space=pl.ANY)


def pieces_of(table, px, py, bottom, *earlier):
    return pl.pallas_call(
        pieces_kernel,
        out_shape=(planes(8), planes(8), MARK),
        in_specs=[SMEM_SPEC] + [VMEM_SPEC] * 3 + [ANY_SPEC] * len(earlier),
        out_specs=[VMEM_SPEC] * 3,
        compiler_params=pltpu.CompilerParams(vmem_limit_bytes=24 * MIB),
        cost_estimate=SMALL,
        name="pieces",
    )(table, px, py, bottom, *earlier)


def small_kernel(body, name, out_shape, inputs, earlier=()):
    count = len(inputs)

    def kernel(*refs):
        body(*refs[:count], *refs[count + len(earlier) :])

    return pl.pallas_call(
        kernel,
        out_shape=out_shape,
        in_specs=[VMEM_SPEC] * count + [ANY_SPEC] * len(earlier),
        out_specs=jax.tree.map(lambda _: VMEM_SPEC, out_shape),
        compiler_params=pltpu.CompilerParams(vmem_limit_bytes=16 * MIB),
        cost_estimate=SMALL,
        name=name,
    )(*inputs, *earlier)


def pair_body(mine, flip, out):
    out[0] = mine[...]
    out[1] = flip[...]


def new_pair_body(mine, flip, ghost, other, out):
    out[0] = mine[...] + TIME_STEP * ghost[...]
    out[1] = flip[...] + TIME_STEP * other[...]


def cores_body(keep, taken, give_near, give_far, keep_half):
    keep_half[...] = keep[0:4] + taken[0:4]
    give_near[...] = keep[4:5] + taken[4:5]
    give_far[...] = keep[5:8] + taken[5:8]


def whole_cores_body(keep, taken, give_half, keep_half):
    keep_half[...] = keep[0:4] + taken[0:4]
    give_half[...] = keep[4:8] + taken[4:8]


def halves_body(keep, *refs):
    outs = refs[-4:]
    got = [ref.at[i] for ref in refs[:-4] for i in range(ref.shape[0])]
    for i in range(4):
        outs[i][...] = keep[i] + got[i][...]


def ghost_body(own, a, b, c, out):
    out[...] = own[...] + (a[...] + b[...] + c[...])


def from_below(table, px, py, tops, picked, sems):
    def place(k):
        source, tile = table[k], table[4]
        x_step = ((source >> 3) ^ (tile >> 3)) & 1
        y_step = ((source >> 1) - (tile >> 1)) & 3
        return (source ^ tile) & 1, y_step, x_step

    def fetch(plane, k):
        return pltpu.make_async_copy(plane, picked.at[k], sems.at[k])

    for k in range(4):
        core_step, y_step, x_step = place(k)
        for core in range(2):
            pair, right, left, *far = tops[5 * core : 5 * core + 5]
            for step, near in ((0, pair), (1, right), (3, left)):

                @pl.when((core_step == core) & (y_step == step))
                def _():
                    fetch(near.at[x_step], k).start()

            for half in range(2):

                @pl.when((core_step == core) & (y_step == 2) & (x_step == half))
                def _():
                    fetch(far[half], k).start()

    total = jnp.zeros((W, W), F32)
    for k in range(4):
        fetch(tops[3], k).wait()
        left = product(split(px[k]), split(picked[k]), ((1,), (0,)))
        total = total + product(split(left), split(py[k]), ((1,), (1,)))
    return jnp.where(table[5] == 1, total, 0.0)


def ends_copies(field, speed, ends, sems):
    return [
        pltpu.make_async_copy(field.at[0], ends.at[0], sems.at[4]),
        pltpu.make_async_copy(speed.at[0], ends.at[1], sems.at[5]),
    ]


def below_value(table, px, py, field, speed, tops, picked, ends, sems):
    copies = ends_copies(field, speed, ends, sems)
    for copy in copies:
        copy.start()
    total = from_below(table, px, py, tops, picked, sems)
    for copy in copies:
        copy.wait()
    return ends[0] + TIME_STEP * (total + ends[1] * total)


def below_kernel(table, px, py, field, speed, *refs):
    tops, (out, *scratch) = refs[:10], refs[-4:]
    out[...] = below_value(table, px, py, field, speed, tops, *scratch)


BELOW_SCRATCH = [
    pltpu.VMEM((4, W, W), F32),
    pltpu.VMEM((2, W, W), F32),
    pltpu.SemaphoreType.DMA((8,)),
]


def below_update(table, px, py, field, speed, tops, *earlier):
    return pl.pallas_call(
        below_kernel,
        out_shape=planes(),
        in_specs=[SMEM_SPEC] + [VMEM_SPEC] * 2 + [ANY_SPEC] * (12 + len(earlier)),
        out_specs=VMEM_SPEC,
        scratch_shapes=BELOW_SCRATCH,
        compiler_params=pltpu.CompilerParams(vmem_limit_bytes=50 * MIB),
        cost_estimate=SMALL,
        name="below",
    )(table, px, py, field, speed, *tops, *earlier)


def fix_bottom_kernel(table, px, py, speed, *refs):
    tops, (field, out, high, picked, ends, sems) = refs[:10], refs[10:]
    fetch = pltpu.make_async_copy(field.at[NZ - 1], high, sems.at[7])
    fetch.start()
    ends[0] = below_value(table, px, py, field, speed, tops, picked, ends, sems)
    copy = pltpu.make_async_copy(ends.at[0], out.at[0], sems.at[6])
    copy.start()
    fetch.wait()
    copy.wait()


def fix_bottom(table, px, py, speed, tops, field):
    return pl.pallas_call(
        fix_bottom_kernel,
        out_shape=(planes(NZ), planes()),
        in_specs=[SMEM_SPEC] + [VMEM_SPEC] * 2 + [ANY_SPEC] * 11 + [pl.BlockSpec(memory_space=pltpu.HBM)],
        out_specs=[pl.BlockSpec(memory_space=pltpu.HBM), VMEM_SPEC],
        scratch_shapes=BELOW_SCRATCH,
        input_output_aliases={14: 0},
        compiler_params=pltpu.CompilerParams(vmem_limit_bytes=50 * MIB),
        cost_estimate=SMALL,
        name="fix_bottom",
    )(table, px, py, speed, *tops, field)


def fix_top_kernel(table, ghost, high, field, out, plane, sems):
    plane[...] = high[...] + TIME_STEP * jnp.where(table[6] == 1, AMBIENT, ghost[...])
    store = pltpu.make_async_copy(plane, out.at[NZ - 1], sems.at[0])
    store.start()
    store.wait()


def fix_top(table, ghost, high, field):
    return pl.pallas_call(
        fix_top_kernel,
        out_shape=planes(NZ),
        in_specs=[SMEM_SPEC, VMEM_SPEC, VMEM_SPEC, pl.BlockSpec(memory_space=pltpu.HBM)],
        out_specs=pl.BlockSpec(memory_space=pltpu.HBM),
        scratch_shapes=[pltpu.VMEM((W, W), F32), pltpu.SemaphoreType.DMA((1,))],
        input_output_aliases={3: 0},
        compiler_params=pltpu.CompilerParams(vmem_limit_bytes=8 * MIB),
        cost_estimate=SMALL,
        name="fix_top",
    )(table, ghost, high, field)


def rims_kernel(field, bottom, top, *refs):
    row_low, row_high, col_low, col_high = refs[-4:]
    lane = lax.broadcasted_iota(jnp.int32, (W, 128), 1)
    low = jnp.zeros((W, 128), F32)
    high = jnp.zeros((W, 128), F32)
    for z in range(NZ):
        ref = bottom if z == 0 else top if z == NZ - 1 else field.at[z]
        row_low[z : z + 1, :] = ref[0:1, :]
        row_high[z : z + 1, :] = ref[W - 1 : W, :]
        low = jnp.where(lane == z, ref[:, 0:1], low)
        high = jnp.where(lane == z, ref[:, W - 1 : W], high)
    col_low[...] = low.T[:NZ]
    col_high[...] = high.T[:NZ]


def rims_of(field, bottom, top, *earlier):
    rim = jax.ShapeDtypeStruct((NZ, W), F32)
    return pl.pallas_call(
        rims_kernel,
        out_shape=(rim,) * 4,
        in_specs=[VMEM_SPEC] * 3 + [ANY_SPEC] * len(earlier),
        out_specs=[VMEM_SPEC] * 4,
        compiler_params=pltpu.CompilerParams(vmem_limit_bytes=16 * MIB),
        cost_estimate=SMALL,
        name="rims",
    )(field, bottom, top, *earlier)


def stencil_kernel(inverse, inside, field, bottom, top, speed, inlets, x_low, x_high, y_low, y_high, *refs):
    out, mark, low, high, fast, sems = refs[-6:]

    def fetch(z):
        return pltpu.make_async_copy(speed.at[z], fast.at[z], sems.at[z])

    for z in range(NZ):
        fetch(z).start()
    mark[...] = jnp.zeros_like(mark)
    pad = jnp.zeros((128 - NZ, W), F32)
    low[...] = jnp.concatenate([jnp.where(inside[2] == 1, y_low[...], 0.0), pad], axis=0).T
    high[...] = jnp.concatenate([jnp.where(inside[3] == 1, y_high[...], 0.0), pad], axis=0).T
    scale = inverse[0]

    def update(z, here, under, over):
        fetch(z).wait()
        pick = lax.broadcasted_iota(jnp.int32, (W, 128), 1) == z
        col_low = jnp.sum(jnp.where(pick, low[...], 0.0), axis=1, keepdims=True)
        col_high = jnp.sum(jnp.where(pick, high[...], 0.0), axis=1, keepdims=True)
        row = lax.broadcasted_iota(jnp.int32, (W, W), 0)
        lane = lax.broadcasted_iota(jnp.int32, (W, W), 1)
        row_low = jnp.where(inside[0] == 1, x_low[pl.ds(z, 1), :], 0.0)
        row_high = jnp.where(inside[1] == 1, x_high[pl.ds(z, 1), :], 0.0)
        beside = jnp.where(row == 0, row_low, pltpu.roll(here, 1, 0))
        beside = beside + jnp.where(row == W - 1, row_high, pltpu.roll(here, W - 1, 0))
        beside = beside + jnp.where(lane == 0, col_low, pltpu.roll(here, 1, 1))
        beside = beside + jnp.where(lane == W - 1, col_high, pltpu.roll(here, W - 1, 1))
        lapl = (beside - 4.0 * here) * scale
        change = lapl + over + under - 2.0 * here - fast[z] * (here - under)
        return here + TIME_STEP * change

    zero = jnp.zeros((W, W), F32)
    first = bottom[...]
    inject = INJECT_RATE * inlets[...].astype(F32)
    out[0] = update(0, first, zero, field[1]) + TIME_STEP * (inject * (1.0 - first))
    out[1] = update(1, field[1], first, field[2])

    def middle(z, carry):
        out[z] = update(z, field[z], field[z - 1], field[z + 1])
        return carry

    lax.fori_loop(2, NZ - 2, middle, 0)
    out[NZ - 2] = update(NZ - 2, field[NZ - 2], field[NZ - 3], top[...])
    out[NZ - 1] = update(NZ - 1, top[...], field[NZ - 2], zero)


def stencil(inverse, inside, field, bottom, top, speed, inlets, halos, *earlier):
    return pl.pallas_call(
        stencil_kernel,
        out_shape=(planes(NZ), MARK),
        in_specs=[SMEM_SPEC] * 2 + [VMEM_SPEC] * 3 + [ANY_SPEC] + [VMEM_SPEC] * 5 + [ANY_SPEC] * len(earlier),
        out_specs=[VMEM_SPEC] * 2,
        scratch_shapes=[pltpu.VMEM((W, 128), F32)] * 2
        + [pltpu.VMEM((NZ, W, W), F32), pltpu.SemaphoreType.DMA((NZ,))],
        compiler_params=pltpu.CompilerParams(vmem_limit_bytes=24 * MIB),
        cost_estimate=SMALL,
        name="stencil",
    )(inverse, inside, field, bottom, top, speed, inlets, *halos, *earlier)


def exchange_rims(rims):
    row_low, row_high, col_low, col_high = rims
    up = [(t, (t + TCOL) % TILES) for t in range(TILES)]
    right = [(t, t - t % TCOL + (t + 1) % TCOL) for t in range(TILES)]
    x_low = lax.ppermute(row_high, "tile", up)
    x_high = lax.ppermute(row_low, "tile", [(d, s) for s, d in up])
    y_low = lax.ppermute(col_high, "tile", right)
    y_high = lax.ppermute(col_low, "tile", [(d, s) for s, d in right])
    return x_low, x_high, y_low, y_high


def climb(plane):
    return send_lift(plane, 1, False), send_lift(plane, 1, True)


def other_core(value):
    return lax.ppermute(value, "tile", OTHER_CORE)


def gather_near(pair):
    return send_y(pair, -1), send_y(pair, 1)


def far_body(right, left, mine, flip):
    mine[...] = left[0]
    flip[...] = right[1]


def gather_far(near, *earlier):
    mine, flip = small_kernel(far_body, "far_planes", (planes(), planes()), near, earlier)
    return send_y(mine, 1), send_y(flip, -1)


def reduce_cores(give, keep, body, *counts, earlier=()):
    taken = lax.ppermute(give, "tile", OTHER_CORE)
    shapes = tuple(planes(count) for count in (*counts, 4))
    return small_kernel(body, "cores_sum", shapes, (keep, taken), earlier)


def reduce_halves(give):
    return lax.ppermute(give, "tile", OTHER_HALF)


def reduce_ring(keep, got, *earlier):
    own, *others = small_kernel(halves_body, "halves_sum", (planes(),) * 4, (keep, *got), earlier)
    return own, *(send_y(part, step) for part, step in zip(others, (1, 2, -1)))


def ghost_sum(parts, *earlier):
    return small_kernel(ghost_body, "ghost_sum", planes(), parts, earlier)


def on_device(oxygen, velocity, spacing, inlets, proj_x, proj_y, sources):
    field = oxygen.reshape(NZ, W, W)
    speed = velocity.reshape(NZ, W, W)
    inlets = inlets.reshape(W, W)
    px = proj_x.reshape(4, W, W)
    py = proj_y.reshape(4, W, W)
    inverse = 1.0 / (spacing * spacing)
    tile = lax.axis_index("tile").astype(jnp.int32)
    lift = lax.axis_index("lift")
    has_below = (lift > 0).astype(jnp.int32)
    is_top = lift == LIFTS - 1
    table = jnp.concatenate([sources.reshape(4) & (TILES - 1), tile[None], has_below[None], is_top[None].astype(jnp.int32)])
    inside = jnp.stack([tile >= TCOL, tile < TILES - TCOL, tile % TCOL > 0, tile % TCOL < TCOL - 1]).astype(jnp.int32)
    bottom, top = field[0], field[NZ - 1]

    mine, flip = climb(top)
    give, keep, mark = pieces_of(table, px, py, bottom)
    halos = exchange_rims(rims_of(field, bottom, top, mark))
    give, keep = reduce_cores(give, keep, whole_cores_body, 4, earlier=(mine, flip, *halos))
    pair = small_kernel(pair_body, "pair", planes(2), (mine, flip), (give,))
    near = gather_near(pair)
    got = reduce_halves(give)
    field, mark = stencil(inverse, inside, field, bottom, top, speed, inlets, halos)
    far = gather_far(near, mark)
    tops = [pair, *near, *far]
    tops = tops + [other_core(value) for value in tops]
    high = field[NZ - 1]
    mine, flip = climb(high)
    parts = reduce_ring(keep, [got], mark)
    bottom = below_update(table, px, py, field, speed, tops, parts[0])
    give, keep, mark = pieces_of(table, px, py, bottom, mine, flip, parts[1], parts[3])
    give_near, give_far, keep = reduce_cores(give, keep, cores_body, 1, 3)
    ghost = ghost_sum(parts, give_near, mine, flip)
    got_near = reduce_halves(give_near)
    other_ghost = reduce_halves(ghost)
    ghost_above = send_lift(ghost, -1, False)
    earlier = (got_near, ghost_above)
    pair = small_kernel(new_pair_body, "new_pair", planes(2), (mine, flip, ghost, other_ghost), earlier)
    near = gather_near(pair)
    top = high + TIME_STEP * jnp.where(is_top, AMBIENT, ghost_above)
    got_far = reduce_halves(give_far)
    halos = exchange_rims(rims_of(field, bottom, top))
    field, mark = stencil(inverse, inside, field, bottom, top, speed, inlets, halos)
    parts = reduce_ring(keep, [got_near, got_far], *halos, *near)
    far = gather_far(near, mark)
    tops = [pair, *near, *far]
    tops = tops + [other_core(value) for value in tops]
    ghost = send_lift(ghost_sum(parts, mark), -1, False)
    field, high = fix_bottom(table, px, py, speed, tops, field)
    field = fix_top(table, ghost, high, field)
    return field.reshape(1, NZ, 1, W, W)


def solution(mesh):
    return jax.shard_map(
        on_device,
        mesh=mesh,
        in_specs=(
            P("lift", None, "tile", None, None),
            P("lift", None, "tile", None, None),
            P("lift"),
            P("lift", "tile", None, None),
            P("lift", "tile", None, None, None),
            P("lift", "tile", None, None, None),
            P("lift", "tile", None),
        ),
        out_specs=P("lift", None, "tile", None, None),
        check_vma=False,
    )
```
